256 devices in a mesh: facet: 32 (over x, z), uv: 8 (over y, core).
Axes of the slice: x: 4, y: 4, z: 8, core: 2. Of those that a mesh axis runs over, the one named last changes fastest.
Arguments:
- sky_image: bfloat16 [256, 65536], P('uv', 'facet'), may hold values from -6 to 6
- subgrid_offsets: int32 [32], replicated, may hold values from 0 to 2047
- owner_order: int32 [32], replicated, may hold values from 0 to 31, each once
- visibility_count: int32 [32], P('facet'), may hold values from 1 to 512, 8192 in all
- visibility_cell: int32 [32, 512], P('facet'), may hold values from 0 to 255
- observed: bfloat16 [32, 2, 256, 512], P('facet', None, 'uv'), may hold values from -6 to 6
- visibility_weight: float32 [32, 256, 512], P('facet', 'uv'), may hold values from 0.3 to 3
- row_kernel: float32 [7], replicated, may hold values from 0.3 to 1
- column_kernel: float32 [7], replicated, may hold values from 0.3 to 1
Outputs:
- weighted_residual: float32 [32, 2, 256, 512], P('facet', None, 'uv')
- dirty_image: float32 [256, 65536], P('uv', 'facet')
The draws below stay inside these ranges and needn't reach their ends.
Inputs may be any that keep to these rules, and one draw needn't show every extreme that they name: `owner_order`: a permutation of the 32 subgrids over the slots. `visibility_count`: the counts sum to 8192, and some slot has exactly 512 live visibilities in every draw.
All inputs are finite; a program needn't handle non-finite values. No bound on the sum of `visibility_count` on one device may be relied on, other than what follows from the above.
Results may differ from the reference program's by a relative error of at most 0.022.
Values may be sent and summed in bfloat16 or wider, within the bound.
No kernel may reach another device: no remote copies, remote signals or barrier semaphores. Data moves between devices by JAX's collectives and lax.ppermute only.
A program may use at most 64 MiB of HBM per device.

```python
import math
import jax
import jax.numpy as jnp
import numpy as np
from jax import lax

FR = 2048
XC = 128
SG = 256
TAPS = 7
VMAX = 512
NSUB = 32
NROWS = 65536
COLS = 256
N_FACET = 32


def place_ends(values, stream_key, least, largest):
    longest = values.shape.index(max(values.shape))
    spots = []
    for shift in (0, 1):
        where = [jax.random.randint(jax.random.fold_in(stream_key, axis), (), 0, length) for axis, length in enumerate(values.shape)]
        where[longest] = (where[longest] + shift) % values.shape[longest]
        spots.append(tuple(where))
    return values.at[spots[0]].set(least).at[spots[1]].set(largest)


def steps_of(key, dims, cuts, low, high):
    factor_of = 1.0
    for axis_at, shards_of in cuts:
        heights = jax.random.uniform(jax.random.fold_in(jax.random.fold_in(key, 6), axis_at), (shards_of,), jnp.float32, low / len(cuts), high / len(cuts))
        factor_of = factor_of * jnp.repeat(jnp.exp(heights), dims[axis_at] // shards_of).reshape((-1,) + (1,) * (len(dims) - 1 - axis_at))
    return factor_of


def length_profile(number_of, total, limit, lean):
    weights = [(1 << 20) // math.isqrt(standing ** lean) + 1 for standing in range(2, number_of + 1)]
    spare, given = total - limit - (number_of - 1), [1] * (number_of - 1)
    while spare > 0:
        candidates = [i for i in range(number_of - 1) if given[i] < limit]
        pool, left = sum([weights[i] for i in candidates]), spare
        for i in candidates:
            addition = min(limit - given[i], max(1, left * weights[i] // pool), spare)
            given[i] = given[i] + addition
            spare = spare - addition
    return np.array([limit] + given)


def uneven_parts(own_key, count, total, reach, skew):
    if count == 2:
        one = jax.random.randint(own_key, (), max(1, total - reach), min(reach, total - 1) + 1)
        return jnp.stack([one, total - one])
    tallies = jnp.asarray(length_profile(count, total, reach, skew), jnp.int32)
    couples = (count - 1) // 2
    source_of, sink = tallies[1:1 + 2 * couples:2], tallies[2:2 + 2 * couples:2]
    slack = jnp.minimum(source_of - 1, reach - sink)
    moved = jax.random.randint(jax.random.fold_in(own_key, 1), (couples,), 0, 1 << 20) % (slack + 1)
    tallies = tallies.at[1:1 + 2 * couples:2].set(source_of - moved).at[2:2 + 2 * couples:2].set(sink + moved)
    return tallies[jax.random.permutation(jax.random.fold_in(own_key, 2), count)]


def bell_draw(own_key, dims, width, bound, cuts=(), kind=jnp.bfloat16):
    array = jax.random.normal(own_key, dims, jnp.float32) * width
    if len(cuts) > 0:
        array = steps_of(own_key, dims, cuts, -0.22, 0.18) * array
    return jnp.clip(array, min=-bound, max=bound).astype(kind)


def setup_inputs(seed: int = 0) -> dict:
    splits = jax.random.split(jax.random.key(seed), 10)
    return {
        "sky_image": bell_draw(splits[0], (COLS, NROWS), 1.0, 6.0, ((0, 8), (1, 32))),
        "subgrid_offsets": place_ends(jax.random.randint(splits[1], (NSUB,), 0, FR), jax.random.fold_in(splits[1], 1), 0, FR - 1).astype(jnp.int32),
        "owner_order": jax.random.permutation(splits[2], NSUB).astype(jnp.int32),
        "visibility_count": uneven_parts(splits[3], NSUB, NSUB * VMAX // 2, VMAX, 2).astype(jnp.int32),
        "visibility_cell": place_ends(jax.random.randint(splits[4], (NSUB, VMAX), 0, SG), jax.random.fold_in(splits[4], 1), 0, SG - 1).astype(jnp.int32),
        "observed": bell_draw(splits[5], (NSUB, 2, COLS, VMAX), 1.0, 6.0, ((0, 32), (2, 8))),
        "visibility_weight": jnp.clip(jnp.exp(math.log(3.0) - 2.3025851 * jax.random.uniform(splits[6], (NSUB, COLS, VMAX), jnp.float32) ** steps_of(splits[6], (NSUB, COLS, VMAX), ((0, 32), (1, 8)), -0.2, 0.2)), 0.3, 3.0),
        "row_kernel": jnp.clip(jax.random.uniform(splits[7], (TAPS,), jnp.float32, 0.3, 1.0), 0.3, 1.0),
        "column_kernel": jnp.clip(jax.random.uniform(splits[8], (TAPS,), jnp.float32, 0.3, 1.0), 0.3, 1.0),
    }


def taper_values(strip_rows):
    position = jnp.arange(strip_rows, dtype=jnp.float32)
    return jnp.sin((position + 0.5) * (math.pi / strip_rows)) / math.sqrt(strip_rows)

def shift_values(slot_offsets, strip_rows):
    position = jnp.arange(strip_rows, dtype=jnp.int32)
    shifted = jnp.bitwise_and(slot_offsets[:, None] * position[None, :], strip_rows - 1)
    angle_shift = shifted.astype(jnp.float32) * (2.0 * math.pi / strip_rows)
    return jnp.stack([jnp.cos(angle_shift), -jnp.sin(angle_shift)], axis=1)

def base_tables(coarse, strip_rows):
    position = jnp.arange(strip_rows, dtype=jnp.int32)
    base = jnp.bitwise_and(jnp.arange(coarse, dtype=jnp.int32)[:, None] * position[None, :], strip_rows - 1)
    angle_base = base.astype(jnp.float32) * (2.0 * math.pi / strip_rows)
    cosine = jnp.cos(angle_base)
    sine_part = jnp.sin(angle_base)
    upper = jnp.stack([cosine, sine_part])
    lower = jnp.stack([-sine_part, cosine])
    return jnp.stack([upper, lower]).astype(jnp.bfloat16)

def expand_tables(facet, coarse, strip_rows, facet_count):
    grid_width = 2 * coarse
    image_rows = strip_rows * facet_count
    fine_index = jnp.arange(grid_width, dtype=jnp.int32)[:, None]
    coarse_index = jnp.arange(coarse, dtype=jnp.int32)[None, :]
    centre = (facet * strip_rows + strip_rows // 2)[..., None, None]
    product = jnp.bitwise_and(jnp.bitwise_and(fine_index * coarse_index, grid_width - 1) * (image_rows // grid_width) + (fine_index - 2 * coarse_index) * centre, image_rows - 1)
    radians = product.astype(jnp.float32) * (2.0 * math.pi / image_rows)
    factor = 1.0 / math.sqrt(facet_count * coarse)
    cosine = jnp.cos(radians) * factor
    sine_part = jnp.sin(radians) * factor
    upper = jnp.stack([cosine, -sine_part], axis=-3)
    lower = jnp.stack([sine_part, cosine], axis=-3)
    return jnp.stack([upper, lower], axis=-4).astype(jnp.bfloat16)

def degrid_matrix(positions, kernel, grid_width):
    margin = (kernel.shape[0] - 1) // 2
    distance = jnp.arange(grid_width, dtype=jnp.int32)[None, :] - positions[:, None] + margin
    matrix = jnp.zeros(distance.shape, jnp.float32)
    for tap_index in range(kernel.shape[0]):
        matrix = matrix + jnp.where(distance == tap_index, kernel[tap_index], 0.0)
    return matrix.astype(jnp.bfloat16)

def convolve(padded, kernel, columns, flipped):
    tap_count = kernel.shape[0]
    result = jnp.zeros(padded.shape[:-2] + (columns, padded.shape[-1]), jnp.float32)
    for tap_index in range(tap_count):
        first_column = tap_count - 1 - tap_index if flipped else tap_index
        result = result + kernel[tap_index] * padded[..., first_column:first_column + columns, :]
    return result

def rounded(values):
    return lax.optimization_barrier(values.astype(jnp.bfloat16)).astype(jnp.float32)

def reference(sky_image, subgrid_offsets, owner_order, visibility_count, visibility_cell, observed, visibility_weight, row_kernel, column_kernel):
    strip_rows = FR
    columns = sky_image.shape[0]
    margin = (TAPS - 1) // 2
    window_taper = taper_values(strip_rows)
    windowed = (sky_image.astype(jnp.float32).reshape(columns, N_FACET, strip_rows) * window_taper[None, None, :]).astype(jnp.bfloat16)
    windowed_wide = windowed.astype(jnp.float32)
    expansion = expand_tables(jnp.arange(N_FACET, dtype=jnp.int32), XC, strip_rows, N_FACET).astype(jnp.float32)
    base_table = base_tables(XC, strip_rows).astype(jnp.float32)
    slot_offset = subgrid_offsets[owner_order]
    shift_table = shift_values(slot_offset, strip_rows)
    row_index = jnp.arange(VMAX, dtype=jnp.int32)

    def one_slot(dirty_sum, inputs):
        shift, live_count, positions, observed_slot, weights = inputs
        modulated = rounded(shift[:, None, None, :] * windowed_wide[None, :, :, :])
        contribution = rounded(jnp.einsum('pqkr,qcfr->fpck', base_table, modulated))
        subgrid = jnp.einsum('fpqjk,fqck->pcj', expansion, contribution)
        padded = jnp.pad(subgrid, ((0, 0), (margin, margin), (0, 0)))
        grid_values = rounded(convolve(padded, column_kernel, columns, False))
        degrid_table = degrid_matrix(positions, row_kernel, SG).astype(jnp.float32)
        model_rows = jnp.einsum('vj,pcj->pcv', degrid_table, grid_values)
        live_rows = (row_index < live_count).astype(jnp.float32)
        residual = live_rows[None, None, :] * weights[None, :, :] * (observed_slot.astype(jnp.float32) - model_rows)
        gridded = jnp.einsum('vj,pcv->pcj', degrid_table, rounded(residual))
        padded_back = jnp.pad(gridded, ((0, 0), (margin, margin), (0, 0)))
        back_grid = rounded(convolve(padded_back, column_kernel, columns, True))
        back_pieces = rounded(jnp.einsum('fqpjk,qcj->fpck', expansion, back_grid))
        back_rows = jnp.einsum('pqkr,fpck->qcfr', base_table, back_pieces)
        dirty_sum = dirty_sum + lax.optimization_barrier(jnp.sum(shift[:, None, None, :] * back_rows, axis=0))
        return (dirty_sum, residual)
    dirty_sum, residuals = lax.scan(one_slot, jnp.zeros((columns, N_FACET, strip_rows), jnp.float32), (shift_table, visibility_count, visibility_cell, observed, visibility_weight))
    dirty_image = (dirty_sum * window_taper[None, None, :]).reshape(columns, N_FACET * strip_rows)
    return (residuals, dirty_image)
```

```python
import functools
import math

import jax
import jax.numpy as jnp
import numpy as np
from jax import lax
from jax.experimental import pallas as pl
from jax.experimental.pallas import tpu as pltpu
from jax.sharding import PartitionSpec as P

FR = 2048
XC = 128
SG = 256
NF = 32
CB = 32
CE = 40
TAPS = 7
VM = 512
EXT = 3968
BF = jnp.bfloat16
F32 = jnp.float32


def facet_table():
    s = np.arange(EXT)[:, None] + 64
    k = np.arange(XC)[None, :]
    a = 2.0 * np.pi * ((s * k) % FR) / FR
    return np.concatenate([np.cos(a), -np.sin(a)], axis=1).astype(np.float32)


def subgrid_table():
    j = np.arange(SG)[None, :]
    k = np.arange(XC)[:, None]
    a = 2.0 * np.pi * ((j * k) % SG) / SG
    c, s = np.cos(a) / 64.0, np.sin(a) / 64.0
    return np.block([[c, s], [-s, c]]).astype(np.float32)


def facet_phase():
    f = np.arange(NF)[:, None]
    j = np.arange(SG)[None, :]
    a = 2.0 * np.pi * ((j * (2 * f + 1)) % 64) / 64
    return np.stack([np.cos(a), np.sin(a)]).astype(np.float32)


def window():
    r = np.arange(FR)
    return (np.sin((r + 0.5) * np.pi / FR) / math.sqrt(FR)).astype(np.float32)[None, :]


def turn(n):
    q = (n + 256) >> 9
    x = (n - (q << 9)).astype(F32) * (math.pi / 1024.0)
    y = x * x
    c = 1.0 + y * (-0.5 + y * (1.0 / 24 + y * (-1.0 / 720 + y * (1.0 / 40320))))
    s = x * (1.0 + y * (-1.0 / 6 + y * (1.0 / 120 + y * (-1.0 / 5040 + y * (1.0 / 362880)))))
    odd = (q & 1) == 1
    cos = jnp.where(odd, s, c)
    sin = jnp.where(odd, c, s)
    cos = jnp.where(((q + 1) & 2) == 2, -cos, cos)
    sin = jnp.where((q & 2) == 2, -sin, sin)
    return cos, sin


def shifts(offs_ref, order_ref, sh_ref):
    row = lax.broadcasted_iota(jnp.int32, (NF, 128), 0)
    off = jnp.zeros((NF, 128), jnp.int32)
    for i in range(NF):
        off = jnp.where(row == i, offs_ref[order_ref[i]], off)
    for b in range(FR // 128):
        r = lax.broadcasted_iota(jnp.int32, (NF, 128), 1) + 128 * b
        c, s = turn((off * r) & (FR - 1))
        sh_ref[0, :, 128 * b : 128 * (b + 1)] = c
        sh_ref[1, :, 128 * b : 128 * (b + 1)] = s


def halo_rows(after, before, axis):
    row = lax.broadcasted_iota(jnp.int32, after.shape, axis)
    return jnp.where(row < 3, after, jnp.where(row >= 5, before, jnp.zeros_like(after)))


def k1_body(
    offs_ref, order_ref, ck_ref, fm_ref, sky_ref, before_ref, after_ref, win_ref, tab_hbm,
    out_ref, tab_ref, ext_ref, conv_ref, sh_ref, lhs_ref, sem,
):
    start = pl.multiple_of(fm_ref[0] * 128, 128)
    copy = pltpu.make_async_copy(tab_hbm.at[pl.ds(start, FR), :], tab_ref, sem)
    copy.start()
    shifts(offs_ref, order_ref, sh_ref)
    win = win_ref[...]
    ext_ref[8:16, :] = before_ref[...].astype(F32) * win
    ext_ref[16:48, :] = sky_ref[...].astype(F32) * win
    ext_ref[48:56, :] = after_ref[...].astype(F32) * win
    own = jnp.zeros((CB, FR), F32)
    lo = jnp.zeros((8, FR), F32)
    hi = jnp.zeros((8, FR), F32)
    for t in range(TAPS):
        k = ck_ref[t]
        own = own + k * ext_ref[13 + t : 45 + t, :]
        lo = lo + k * ext_ref[5 + t : 13 + t, :]
        hi = hi + k * ext_ref[45 + t : 53 + t, :]
    conv_ref[0:CB, :] = own
    conv_ref[CB:CE, :] = halo_rows(hi, lo, 0)
    copy.wait()

    def chunk(g, _):
        for h in range(4):
            i = g * 8 + 2 * h
            for q in range(2):
                for b in range(4):
                    lanes = slice(512 * b, 512 * (b + 1))
                    w = conv_ref[:, lanes]
                    x = w * sh_ref[q, pl.ds(i, 1), lanes]
                    y = w * sh_ref[q, pl.ds(i + 1, 1), lanes]
                    lhs_ref[q * 320 + 80 * h : q * 320 + 80 * (h + 1), lanes] = jnp.concatenate(
                        [x, y], axis=0
                    ).astype(BF)
        u = jnp.dot(lhs_ref[...], tab_ref[...], preferred_element_type=F32)
        re = u[:320, :XC] + u[320:, XC:]
        im = u[:320, XC:] - u[320:, :XC]
        for s in range(8):
            out_ref[g * 8 + s, 0] = re[s * CE : (s + 1) * CE].astype(BF)
            out_ref[g * 8 + s, 1] = im[s * CE : (s + 1) * CE].astype(BF)
        return 0

    lax.fori_loop(0, 4, chunk, 0)


SMEM = pl.BlockSpec(memory_space=pltpu.SMEM)
VMEM = pl.BlockSpec(memory_space=pltpu.VMEM)
ANY = pl.BlockSpec(memory_space=pl.ANY)


def k1(offs, order, ck, fm, sky, before, after):
    return pl.pallas_call(
        k1_body,
        out_shape=jax.ShapeDtypeStruct((NF, 2, CE, XC), BF),
        in_specs=[SMEM, SMEM, SMEM, SMEM, VMEM, VMEM, VMEM, VMEM, ANY],
        out_specs=VMEM,
        scratch_shapes=[
            pltpu.VMEM((FR, 2 * XC), BF),
            pltpu.VMEM((64, FR), F32),
            pltpu.VMEM((CE, FR), F32),
            pltpu.VMEM((2, NF, FR), F32),
            pltpu.VMEM((640, FR), BF),
            pltpu.SemaphoreType.DMA,
        ],
        name="facet_to_slots",
    )(offs, order, ck, fm, sky, before, after, window(), jnp.asarray(facet_table(), BF))


def k2_body(
    count_ref, rk_ref, ck_ref, arr_ref, cell_ref, obs_ref, obs_b_ref, obs_a_ref,
    wt_ref, wt_b_ref, wt_a_ref, w_ref, wt_tab_ref, ph_ref,
    res_ref, out_ref, u_ref, dt_ref, ext_ref, y_ref,
):
    cell = cell_ref[...]
    d = lax.broadcasted_iota(jnp.int32, (SG, VM), 0) - cell + 3
    m = jnp.zeros((SG, VM), F32)
    for t in range(TAPS):
        m = jnp.where(d == t, rk_ref[t], m)
    dt_ref[...] = m.astype(BF)

    re = jnp.zeros((CE, SG), F32)
    im = jnp.zeros((CE, SG), F32)
    for g in range(8):
        lhs = jnp.concatenate(
            [
                jnp.concatenate([arr_ref[4 * g + h, 0], arr_ref[4 * g + h, 1]], axis=1)
                for h in range(4)
            ],
            axis=0,
        )
        u = jnp.dot(lhs, w_ref[...], preferred_element_type=F32)
        for h in range(4):
            ur = u[h * CE : (h + 1) * CE, :SG]
            ui = u[h * CE : (h + 1) * CE, SG:]
            pc = ph_ref[0, 4 * g + h : 4 * g + h + 1, :]
            ps = ph_ref[1, 4 * g + h : 4 * g + h + 1, :]
            re = re + (ur * pc - ui * ps)
            im = im + (ur * ps + ui * pc)
    grid = jnp.concatenate([re, im], axis=0).astype(BF)
    model = jnp.dot(grid, dt_ref[...], preferred_element_type=F32)

    live = (lax.broadcasted_iota(jnp.int32, (1, VM), 1) < count_ref[0]).astype(F32)
    wt = wt_ref[...] * live
    wt_h = halo_rows(wt_a_ref[...], wt_b_ref[...], 0) * live
    parts = []
    for p in range(2):
        own = wt * (obs_ref[p].astype(F32) - model[p * CE : p * CE + CB])
        res_ref[p] = own
        obs_h = halo_rows(obs_a_ref[p].astype(F32), obs_b_ref[p].astype(F32), 0)
        parts += [own, wt_h * (obs_h - model[p * CE + CB : (p + 1) * CE])]
    rr = jnp.concatenate(parts, axis=0).astype(BF)
    gridded = lax.dot_general(
        rr, dt_ref[...], (((1,), (1,)), ((), ())), preferred_element_type=F32
    )
    backs = []
    for p in range(2):
        halo = gridded[p * CE + CB : (p + 1) * CE]
        ext_ref[p, 0:8, :] = halo
        ext_ref[p, 8:40, :] = gridded[p * CE : p * CE + CB]
        ext_ref[p, 40:48, :] = halo
        b = jnp.zeros((CB, SG), F32)
        for t in range(TAPS):
            b = b + ck_ref[t] * ext_ref[p, 11 - t : 43 - t, :]
        backs.append(b)
    br, bi = backs
    for g in range(8):
        for h in range(4):
            pc = ph_ref[0, 4 * g + h : 4 * g + h + 1, :]
            ps = ph_ref[1, 4 * g + h : 4 * g + h + 1, :]
            y_ref[h * CB : (h + 1) * CB, :SG] = (br * pc + bi * ps).astype(BF)
            y_ref[h * CB : (h + 1) * CB, SG:] = (bi * pc - br * ps).astype(BF)
        z = jnp.dot(y_ref[...], wt_tab_ref[...], preferred_element_type=F32)
        for h in range(4):
            out_ref[4 * g + h, 0] = z[h * CB : (h + 1) * CB, :XC].astype(BF)
            out_ref[4 * g + h, 1] = z[h * CB : (h + 1) * CB, XC:].astype(BF)


def k2(count, rk, ck, arrived, cell, obs, obs_b, obs_a, wt, wt_b, wt_a):
    tab = subgrid_table()
    return pl.pallas_call(
        k2_body,
        out_shape=(
            jax.ShapeDtypeStruct((2, CB, VM), F32),
            jax.ShapeDtypeStruct((NF, 2, CB, XC), BF),
        ),
        in_specs=[SMEM, SMEM, SMEM] + [VMEM] * 11,
        out_specs=(VMEM, VMEM),
        scratch_shapes=[
            pltpu.VMEM((8, 128), F32),
            pltpu.VMEM((SG, VM), BF),
            pltpu.VMEM((2, 48, SG), F32),
            pltpu.VMEM((4 * CB, 2 * SG), BF),
        ],
        name="slot_round_trip",
    )(
        count, rk, ck, arrived, cell, obs, obs_b, obs_a, wt, wt_b, wt_a,
        jnp.asarray(tab, BF), jnp.asarray(tab.T, BF), facet_phase(),
    )


def k3_body(
    offs_ref, order_ref, fm_ref, bp_ref, win_ref, tab_hbm, out_ref, tab_ref, sh_ref, lhs_ref, sem
):
    start = pl.multiple_of(fm_ref[0] * 128, 128)
    copy = pltpu.make_async_copy(tab_hbm.at[:, pl.ds(start, FR)], tab_ref, sem)
    copy.start()
    shifts(offs_ref, order_ref, sh_ref)
    for i in range(NF):
        a = bp_ref[i, 0]
        b = bp_ref[i, 1]
        lhs_ref[i * CB : (i + 1) * CB, :] = jnp.concatenate([a, b], axis=1)
        lhs_ref[1024 + i * CB : 1024 + (i + 1) * CB, :] = jnp.concatenate([b, -a], axis=1)
    copy.wait()

    def tile(n, _):
        lanes = pl.ds(pl.multiple_of(n * 256, 256), 256)
        z = jnp.dot(lhs_ref[...], tab_ref[:, lanes], preferred_element_type=F32)
        acc = jnp.zeros((CB, 256), F32)
        for i in range(NF):
            c = sh_ref[0, i : i + 1, lanes]
            s = sh_ref[1, i : i + 1, lanes]
            acc = acc + (c * z[i * CB : (i + 1) * CB] - s * z[1024 + i * CB : 1024 + (i + 1) * CB])
        out_ref[:, lanes] = acc * win_ref[:, lanes]
        return 0

    lax.fori_loop(0, FR // 256, tile, 0)


def k3(offs, order, fm, bp):
    return pl.pallas_call(
        k3_body,
        out_shape=jax.ShapeDtypeStruct((CB, FR), F32),
        in_specs=[SMEM, SMEM, SMEM, VMEM, VMEM, ANY],
        out_specs=VMEM,
        scratch_shapes=[
            pltpu.VMEM((2 * XC, FR), BF),
            pltpu.VMEM((2, NF, FR), F32),
            pltpu.VMEM((2048, 2 * XC), BF),
            pltpu.SemaphoreType.DMA,
        ],
        name="slots_to_facet",
    )(offs, order, fm, bp, window(), jnp.asarray(facet_table().T, BF))


def neighbours(first, last):
    n = lax.axis_size("uv")
    up = [(i, i + 1) for i in range(n - 1)]
    down = [(i + 1, i) for i in range(n - 1)]
    return lax.ppermute(last, "uv", up), lax.ppermute(first, "uv", down)


def local(
    sky_image, subgrid_offsets, owner_order, visibility_count, visibility_cell, observed,
    visibility_weight, row_kernel, column_kernel,
):
    fm = (lax.axis_index("facet") % 16).astype(jnp.int32).reshape(1)
    obs = observed[0]
    wt = visibility_weight[0]
    sky_b, sky_a = neighbours(sky_image[:8], sky_image[24:])
    obs_b, obs_a = neighbours(obs[:, :8], obs[:, 24:])
    wt_b, wt_a = neighbours(wt[:8], wt[24:])
    out = k1(subgrid_offsets, owner_order, column_kernel, fm, sky_image, sky_b, sky_a)
    arrived = lax.all_to_all(out, "facet", split_axis=0, concat_axis=0, tiled=True)
    res, outgoing = k2(
        visibility_count, row_kernel, column_kernel, arrived, visibility_cell,
        obs, obs_b, obs_a, wt, wt_b, wt_a,
    )
    back = lax.all_to_all(outgoing, "facet", split_axis=0, concat_axis=0, tiled=True)
    dirty = k3(subgrid_offsets, owner_order, fm, back)
    return (res[None], dirty)


def solution(mesh):
    in_specs = (
        P("uv", "facet"),
        P(),
        P(),
        P("facet"),
        P("facet", None),
        P("facet", None, "uv", None),
        P("facet", "uv", None),
        P(),
        P(),
    )
    out_specs = (P("facet", None, "uv", None), P("uv", "facet"))
    return jax.shard_map(local, mesh=mesh, in_specs=in_specs, out_specs=out_specs, check_vma=False)
```

```python
import math

import jax
import jax.numpy as jnp
import numpy as np
from jax import lax
from jax.experimental import pallas as pl
from jax.experimental.pallas import tpu as pltpu
from jax.sharding import PartitionSpec as P

FR = 2048
XC = 128
SG = 256
NF = 32
CB = 32
CE = 40
TAPS = 7
VM = 512
BF = jnp.bfloat16
F32 = jnp.float32


def block_table():
    lane = np.arange(128)[None, :]
    g = 8 * (lane % 16) + lane // 16
    row = np.arange(128)[:, None] + 64
    a = 2.0 * np.pi * ((g * row) % 128) / 128
    c, s = np.cos(a), np.sin(a)
    return np.block([[c, -s], [s, c]]).astype(np.float32)


def subgrid_table():
    j = np.arange(SG)[None, :]
    k = np.arange(XC)[:, None]
    a = 2.0 * np.pi * ((j * k) % SG) / SG
    c, s = np.cos(a) / 64.0, np.sin(a) / 64.0
    return np.block([[c, s], [-s, c]]).astype(np.float32)


def facet_phase():
    f = np.arange(NF)[:, None]
    j = np.arange(128)[None, :]
    a = 2.0 * np.pi * ((j * (2 * f + 1)) % 64) / 64
    return np.stack([np.cos(a), np.sin(a)]).astype(np.float32)


def window():
    r = np.arange(FR)
    return (np.sin((r + 0.5) * np.pi / FR) / math.sqrt(FR)).astype(np.float32)[None, :]


def turn(n):
    q = (n + 256) >> 9
    x = (n - (q << 9)).astype(F32) * (math.pi / 1024.0)
    y = x * x
    c = 1.0 + y * (-0.5 + y * (1.0 / 24 + y * (-1.0 / 720 + y * (1.0 / 40320))))
    s = x * (1.0 + y * (-1.0 / 6 + y * (1.0 / 120 + y * (-1.0 / 5040 + y * (1.0 / 362880)))))
    odd = (q & 1) == 1
    cos = jnp.where(odd, s, c)
    sin = jnp.where(odd, c, s)
    cos = jnp.where(((q + 1) & 2) == 2, -cos, cos)
    sin = jnp.where((q & 2) == 2, -sin, sin)
    return cos, sin


def twiddles(facet):
    m = lax.broadcasted_iota(jnp.int32, (16, 128), 0)
    lane = lax.broadcasted_iota(jnp.int32, (16, 128), 1)
    return turn((m * (lane + 64 + 128 * facet)) & (FR - 1))


def cmul(a, w):
    wr, wi = w
    if abs(wi) < 1e-12:
        return a if abs(wr - 1) < 1e-12 else (a[0] * wr, a[1] * wr)
    if abs(wr) < 1e-12:
        return (-a[1], a[0]) if wi > 0 else (a[1], -a[0])
    return (a[0] * wr - a[1] * wi, a[0] * wi + a[1] * wr)


def real_transform(x):
    n = len(x)
    if n == 2:
        zero = jnp.zeros_like(x[0])
        return [(x[0] + x[1], zero), (x[0] - x[1], zero)]
    even, odd = real_transform(x[::2]), real_transform(x[1::2])
    out = [None] * (n // 2 + 1)
    for k in range(n // 4 + 1):
        a = 2.0 * math.pi * k / n
        o = cmul(odd[k], (math.cos(a), -math.sin(a)))
        e = even[k]
        out[k] = (e[0] + o[0], e[1] + o[1])
        if k != n // 2 - k:
            out[n // 2 - k] = (e[0] - o[0], o[1] - e[1])
    return out


def real_inverse(h):
    n = 2 * (len(h) - 1)
    if n == 2:
        return [h[0][0] + h[1][0], h[0][0] - h[1][0]]
    even, odd = [], []
    for k in range(n // 4 + 1):
        a, b = h[k], h[n // 2 - k]
        t = 2.0 * math.pi * k / n
        even.append((a[0] + b[0], a[1] - b[1]))
        odd.append(cmul((a[0] - b[0], a[1] + b[1]), (math.cos(t), math.sin(t))))
    even, odd = real_inverse(even), real_inverse(odd)
    return [v for pair in zip(even, odd) for v in pair]


def swap_index(x, lane):
    for bit in (1, 2, 4, 8):
        high = (lane & bit) != 0
        y = list(x)
        for i in range(16):
            if i & bit:
                continue
            y[i] = jnp.where(high, pltpu.roll(x[i + bit], bit, 1), x[i])
            y[i + bit] = jnp.where(high, x[i + bit], pltpu.roll(x[i], 128 - bit, 1))
        x = y
    return x


def halo_rows(after, before, axis):
    row = lax.broadcasted_iota(jnp.int32, after.shape, axis)
    return jnp.where(row < 3, after, jnp.where(row >= 5, before, jnp.zeros_like(after)))


def k1_body(
    offs_ref, order_ref, ck_ref, facet_ref, sky_ref, before_ref, after_ref, win_ref, tab_ref,
    out_ref, ext_ref, conv_ref, tw_ref, lhs_ref, u_ref, nat_ref,
):
    tw_ref[0], tw_ref[1] = twiddles(facet_ref[0])
    for b in range(16):
        lanes = slice(128 * b, 128 * (b + 1))
        win = win_ref[:, lanes]
        ext_ref[8:16, lanes] = before_ref[:, lanes].astype(F32) * win
        ext_ref[16:48, lanes] = sky_ref[:, lanes].astype(F32) * win
        ext_ref[48:56, lanes] = after_ref[:, lanes].astype(F32) * win
    for b in range(16):
        lanes = slice(128 * b, 128 * (b + 1))
        own = jnp.zeros((CB, 128), F32)
        lo = jnp.zeros((8, 128), F32)
        hi = jnp.zeros((8, 128), F32)
        for t in range(TAPS):
            k = ck_ref[t]
            own = own + k * ext_ref[13 + t : 45 + t, lanes]
            lo = lo + k * ext_ref[5 + t : 13 + t, lanes]
            hi = hi + k * ext_ref[45 + t : 53 + t, lanes]
        conv_ref[0:CB, lanes] = own
        conv_ref[CB:CE, lanes] = halo_rows(hi, lo, 0)
        conv_ref[CE : CE + 8, lanes] = jnp.zeros((8, 128), F32)

    for g in range(3):
        rows = slice(16 * g, 16 * (g + 1))
        a = real_transform([conv_ref[rows, 128 * b : 128 * (b + 1)] for b in range(16)])
        for m in range(16):
            ar, ai = a[m] if m <= 8 else (a[16 - m][0], -a[16 - m][1])
            c, s = tw_ref[0, m : m + 1, :], tw_ref[1, m : m + 1, :]
            lhs_ref[m, rows, 0:128] = (ar * c + ai * s).astype(BF)
            lhs_ref[m, rows, 128:256] = (ai * c - ar * s).astype(BF)
    u = jnp.dot(lhs_ref[...].reshape(16 * 48, 256), tab_ref[...], preferred_element_type=F32)
    u_ref[...] = u.reshape(16, 48, 256)

    lane = lax.broadcasted_iota(jnp.int32, (8, 128), 1)
    for g in range(5):
        rows = slice(8 * g, 8 * (g + 1))
        for p in range(2):
            x = swap_index([u_ref[m, rows, 128 * p : 128 * (p + 1)] for m in range(16)], lane)
            for b in range(16):
                nat_ref[b, rows, 128 * p : 128 * (p + 1)] = x[b]
            nat_ref[16, rows, 128 * p : 128 * (p + 1)] = x[0]

    lane = lax.broadcasted_iota(jnp.int32, (CE, 128), 1)
    for i in range(NF):
        off = offs_ref[order_ref[i]]
        b, s = off >> 7, off & 127
        back = (128 - s) & 127
        keep = lane >= s
        for p in range(2):
            cols = slice(128 * p, 128 * (p + 1))
            x = jnp.where(keep, nat_ref[b, :, cols], nat_ref[b + 1, :, cols])
            out_ref[i, :, cols] = pltpu.roll(x, back, 1).astype(BF)


SMEM = pl.BlockSpec(memory_space=pltpu.SMEM)
VMEM = pl.BlockSpec(memory_space=pltpu.VMEM)
PARAMS = pltpu.CompilerParams(vmem_limit_bytes=24 * 1024 * 1024)


def k1(offs, order, ck, facet, sky, before, after):
    return pl.pallas_call(
        k1_body,
        out_shape=jax.ShapeDtypeStruct((NF, CE, 2 * XC), BF),
        in_specs=[SMEM, SMEM, SMEM, SMEM] + [VMEM] * 5,
        out_specs=VMEM,
        scratch_shapes=[
            pltpu.VMEM((64, FR), F32),
            pltpu.VMEM((48, FR), F32),
            pltpu.VMEM((2, 16, 128), F32),
            pltpu.VMEM((16, 48, 256), BF),
            pltpu.VMEM((16, 48, 256), F32),
            pltpu.VMEM((17, CE, 256), F32),
        ],
        compiler_params=PARAMS,
        name="facet_to_slots",
    )(offs, order, ck, facet, sky, before, after, window(), jnp.asarray(block_table(), BF))


def k2_body(
    offs_ref, order_ref, facet_ref, count_ref, rk_ref, ck_ref, arr_ref, cell_ref, obs_ref, wt_ref,
    before_ref, after_ref, w_ref, wt_tab_ref, ph_ref,
    res_ref, out_ref, lhs_ref, u_ref, dt_ref, ext_ref, y_ref, pho_ref,
):
    for f in range(NF):
        lhs_ref[f, 0:CE, :] = arr_ref[f]
    off = offs_ref[order_ref[facet_ref[0]]]
    back = (128 - 2 * off) & 127
    pho_ref[0] = pltpu.roll(ph_ref[0], back, 1)
    pho_ref[1] = pltpu.roll(ph_ref[1], back, 1)

    cell = cell_ref[...]
    d = lax.broadcasted_iota(jnp.int32, (SG, VM), 0) - cell + 3
    m = jnp.zeros((SG, VM), F32)
    for t in range(TAPS):
        m = jnp.where(d == t, rk_ref[t], m)
    dt_ref[...] = m.astype(BF)

    u = jnp.dot(lhs_ref[...].reshape(NF * 48, 256), w_ref[...], preferred_element_type=F32)
    u_ref[...] = u.reshape(NF, 48, 2 * SG)
    res = []
    ims = []
    for h in range(2):
        re = jnp.zeros((CE, 128), F32)
        im = jnp.zeros((CE, 128), F32)
        for f in range(NF):
            ur = u_ref[f, 0:CE, 128 * h : 128 * (h + 1)]
            ui = u_ref[f, 0:CE, SG + 128 * h : SG + 128 * (h + 1)]
            pc = pho_ref[0, f : f + 1, :]
            ps = pho_ref[1, f : f + 1, :]
            re = re + (ur * pc - ui * ps)
            im = im + (ur * ps + ui * pc)
        res.append(re)
        ims.append(im)
    grid = jnp.concatenate(
        [jnp.concatenate(res, axis=1), jnp.concatenate(ims, axis=1)], axis=0
    ).astype(BF)
    model = jnp.dot(grid, dt_ref[...], preferred_element_type=F32)

    live = (lax.broadcasted_iota(jnp.int32, (1, VM), 1) < count_ref[0]).astype(F32)
    wt = wt_ref[...] * live
    wt_h = halo_rows(after_ref[:, FR + 2 * VM :], before_ref[:, FR + 2 * VM :], 0).astype(F32) * live
    parts = []
    for p in range(2):
        own = wt * (obs_ref[p].astype(F32) - model[p * CE : p * CE + CB])
        res_ref[p] = own
        cols = slice(FR + p * VM, FR + (p + 1) * VM)
        obs_h = halo_rows(after_ref[:, cols], before_ref[:, cols], 0).astype(F32)
        parts += [own, wt_h * (obs_h - model[p * CE + CB : (p + 1) * CE])]
    rr = jnp.concatenate(parts, axis=0).astype(BF)
    gridded = lax.dot_general(
        rr, dt_ref[...], (((1,), (1,)), ((), ())), preferred_element_type=F32
    )
    backs = []
    for p in range(2):
        halo = gridded[p * CE + CB : (p + 1) * CE]
        ext_ref[p, 0:8, :] = halo
        ext_ref[p, 8:40, :] = gridded[p * CE : p * CE + CB]
        ext_ref[p, 40:48, :] = halo
        b = jnp.zeros((CB, SG), F32)
        for t in range(TAPS):
            b = b + ck_ref[t] * ext_ref[p, 11 - t : 43 - t, :]
        backs.append(b)
    br, bi = backs
    for h in range(2):
        lanes = slice(128 * h, 128 * (h + 1))
        xr, xi = br[:, lanes], bi[:, lanes]
        for f in range(NF):
            pc = pho_ref[0, f : f + 1, :]
            ps = pho_ref[1, f : f + 1, :]
            y_ref[f, :, lanes] = (xr * pc + xi * ps).astype(BF)
            y_ref[f, :, SG + 128 * h : SG + 128 * (h + 1)] = (xi * pc - xr * ps).astype(BF)
    z = jnp.dot(y_ref[...].reshape(NF * CB, 2 * SG), wt_tab_ref[...], preferred_element_type=F32)
    out_ref[...] = z.astype(BF).reshape(NF, CB, 2 * XC)


def k2(offs, order, facet, count, rk, ck, arrived, cell, obs, wt, before, after):
    tab = subgrid_table()
    return pl.pallas_call(
        k2_body,
        out_shape=(
            jax.ShapeDtypeStruct((2, CB, VM), F32),
            jax.ShapeDtypeStruct((NF, CB, 2 * XC), BF),
        ),
        in_specs=[SMEM] * 6 + [VMEM] * 9,
        out_specs=(VMEM, VMEM),
        scratch_shapes=[
            pltpu.VMEM((NF, 48, 256), BF),
            pltpu.VMEM((NF, 48, 2 * SG), F32),
            pltpu.VMEM((SG, VM), BF),
            pltpu.VMEM((2, 48, SG), F32),
            pltpu.VMEM((NF, CB, 2 * SG), BF),
            pltpu.VMEM((2, NF, 128), F32),
        ],
        compiler_params=PARAMS,
        name="slot_round_trip",
    )(
        offs, order, facet, count, rk, ck, arrived, cell, obs, wt, before, after,
        jnp.asarray(tab, BF), jnp.asarray(tab.T, BF), facet_phase(),
    )


def k3_body(
    offs_ref, order_ref, facet_ref, bp_ref, win_ref, tab_ref,
    out_ref, nat_ref, tw_ref, lhs_ref, v_ref,
):
    tw_ref[0], tw_ref[1] = twiddles(facet_ref[0])
    nat_ref[...] = jnp.zeros_like(nat_ref)
    lane = lax.broadcasted_iota(jnp.int32, (CB, 128), 1)
    for i in range(NF):
        off = offs_ref[order_ref[i]]
        b, s = off >> 7, off & 127
        keep = lane >= s
        for p in range(2):
            cols = slice(128 * p, 128 * (p + 1))
            x = pltpu.roll(bp_ref[i, :, cols].astype(F32), s, 1)
            nat_ref[b, :, cols] += jnp.where(keep, x, 0.0)
            nat_ref[b + 1, :, cols] += jnp.where(keep, 0.0, x)
    nat_ref[0] += nat_ref[16]

    lane = lax.broadcasted_iota(jnp.int32, (16, 128), 1)
    for g in range(2):
        rows = slice(16 * g, 16 * (g + 1))
        for p in range(2):
            cols = slice(128 * p, 128 * (p + 1))
            x = swap_index([nat_ref[b, rows, cols] for b in range(16)], lane)
            for m in range(16):
                lhs_ref[m, rows, cols] = x[m].astype(BF)
    v = jnp.dot(lhs_ref[...].reshape(16 * CB, 256), tab_ref[...], preferred_element_type=F32)
    v_ref[...] = v.reshape(16, CB, 256)
    for g in range(4):
        rows = slice(8 * g, 8 * (g + 1))
        t = []
        for m in range(16):
            vr, vi = v_ref[m, rows, 0:128], v_ref[m, rows, 128:256]
            c, s = tw_ref[0, m : m + 1, :], tw_ref[1, m : m + 1, :]
            t.append((vr * c - vi * s, vr * s + vi * c))
        h = [(t[m][0] + t[-m % 16][0], t[m][1] - t[-m % 16][1]) for m in range(9)]
        x = real_inverse(h)
        for b in range(16):
            lanes = slice(128 * b, 128 * (b + 1))
            out_ref[rows, lanes] = x[b] * (0.5 * win_ref[:, lanes])


def k3(offs, order, facet, bp):
    return pl.pallas_call(
        k3_body,
        out_shape=jax.ShapeDtypeStruct((CB, FR), F32),
        in_specs=[SMEM, SMEM, SMEM, VMEM, VMEM, VMEM],
        out_specs=VMEM,
        scratch_shapes=[
            pltpu.VMEM((17, CB, 256), F32),
            pltpu.VMEM((2, 16, 128), F32),
            pltpu.VMEM((16, CB, 256), BF),
            pltpu.VMEM((16, CB, 256), F32),
        ],
        compiler_params=PARAMS,
        name="slots_to_facet",
    )(offs, order, facet, bp, window(), jnp.asarray(block_table().T, BF))


def neighbours(first, last):
    n = lax.axis_size("uv")
    up = [(i, i + 1) for i in range(n - 1)]
    down = [(i + 1, i) for i in range(n - 1)]
    return lax.ppermute(last, "uv", up), lax.ppermute(first, "uv", down)


def local(
    sky_image, subgrid_offsets, owner_order, visibility_count, visibility_cell, observed,
    visibility_weight, row_kernel, column_kernel,
):
    facet = lax.axis_index("facet").astype(jnp.int32).reshape(1)
    obs = observed[0]
    wt = visibility_weight[0]

    def edge(rows):
        return jnp.concatenate(
            [sky_image[rows], obs[0, rows], obs[1, rows], wt[rows].astype(BF)], axis=1
        )

    before, after = neighbours(edge(slice(0, 8)), edge(slice(24, 32)))
    out = k1(subgrid_offsets, owner_order, column_kernel, facet, sky_image, before, after)
    arrived = lax.all_to_all(out, "facet", split_axis=0, concat_axis=0, tiled=True)
    res, outgoing = k2(
        subgrid_offsets, owner_order, facet, visibility_count, row_kernel, column_kernel,
        arrived, visibility_cell, obs, wt, before, after,
    )
    back = lax.all_to_all(outgoing, "facet", split_axis=0, concat_axis=0, tiled=True)
    dirty = k3(subgrid_offsets, owner_order, facet, back)
    return (res[None], dirty)


def solution(mesh):
    in_specs = (
        P("uv", "facet"),
        P(),
        P(),
        P("facet"),
        P("facet", None),
        P("facet", None, "uv", None),
        P("facet", "uv", None),
        P(),
        P(),
    )
    out_specs = (P("facet", None, "uv", None), P("uv", "facet"))
    return jax.shard_map(local, mesh=mesh, in_specs=in_specs, out_specs=out_specs, check_vma=False)
```

```python
import math

import jax
import jax.numpy as jnp
import numpy as np
from jax import lax
from jax.experimental import pallas as pl
from jax.experimental.pallas import tpu as pltpu
from jax.sharding import PartitionSpec as P

FR = 2048
XC = 128
SG = 256
NF = 32
CB = 32
CE = 40
TAPS = 7
VM = 512
BF = jnp.bfloat16
F32 = jnp.float32


def block_table():
    lane = np.arange(128)[None, :]
    g = 8 * (lane % 16) + lane // 16
    row = np.arange(128)[:, None] + 64
    a = 2.0 * np.pi * ((g * row) % 128) / 128
    c, s = np.cos(a), np.sin(a)
    return np.block([[c, -s], [s, c]]).astype(np.float32)


def subgrid_table():
    j = np.arange(SG)[None, :]
    k = np.arange(XC)[:, None]
    a = 2.0 * np.pi * ((j * k) % SG) / SG
    c, s = np.cos(a) / 64.0, np.sin(a) / 64.0
    return np.block([[c, s], [-s, c]]).astype(np.float32)


def facet_phase():
    f = np.arange(NF)[:, None]
    j = np.arange(128)[None, :]
    a = 2.0 * np.pi * ((j * (2 * f + 1)) % 64) / 64
    return np.stack([np.cos(a), np.sin(a)]).astype(np.float32)


def window():
    r = np.arange(FR)
    return (np.sin((r + 0.5) * np.pi / FR) / math.sqrt(FR)).astype(np.float32)[None, :]


def turn(n):
    q = (n + 256) >> 9
    x = (n - (q << 9)).astype(F32) * (math.pi / 1024.0)
    y = x * x
    c = 1.0 + y * (-0.5 + y * (1.0 / 24 + y * (-1.0 / 720 + y * (1.0 / 40320))))
    s = x * (1.0 + y * (-1.0 / 6 + y * (1.0 / 120 + y * (-1.0 / 5040 + y * (1.0 / 362880)))))
    odd = (q & 1) == 1
    cos = jnp.where(odd, s, c)
    sin = jnp.where(odd, c, s)
    cos = jnp.where(((q + 1) & 2) == 2, -cos, cos)
    sin = jnp.where((q & 2) == 2, -sin, sin)
    return cos, sin


def twiddles(facet):
    m = lax.broadcasted_iota(jnp.int32, (16, 128), 0)
    lane = lax.broadcasted_iota(jnp.int32, (16, 128), 1)
    return turn((m * (lane + 64 + 128 * facet)) & (FR - 1))


def cmul(a, w):
    wr, wi = w
    if abs(wi) < 1e-12:
        return a if abs(wr - 1) < 1e-12 else (a[0] * wr, a[1] * wr)
    if abs(wr) < 1e-12:
        return (-a[1], a[0]) if wi > 0 else (a[1], -a[0])
    return (a[0] * wr - a[1] * wi, a[0] * wi + a[1] * wr)


def real_transform(x):
    n = len(x)
    if n == 2:
        zero = jnp.zeros_like(x[0])
        return [(x[0] + x[1], zero), (x[0] - x[1], zero)]
    even, odd = real_transform(x[::2]), real_transform(x[1::2])
    out = [None] * (n // 2 + 1)
    for k in range(n // 4 + 1):
        a = 2.0 * math.pi * k / n
        o = cmul(odd[k], (math.cos(a), -math.sin(a)))
        e = even[k]
        out[k] = (e[0] + o[0], e[1] + o[1])
        if k != n // 2 - k:
            out[n // 2 - k] = (e[0] - o[0], o[1] - e[1])
    return out


def real_inverse(h):
    n = 2 * (len(h) - 1)
    if n == 2:
        return [h[0][0] + h[1][0], h[0][0] - h[1][0]]
    even, odd = [], []
    for k in range(n // 4 + 1):
        a, b = h[k], h[n // 2 - k]
        t = 2.0 * math.pi * k / n
        even.append((a[0] + b[0], a[1] - b[1]))
        odd.append(cmul((a[0] - b[0], a[1] + b[1]), (math.cos(t), math.sin(t))))
    even, odd = real_inverse(even), real_inverse(odd)
    return [v for pair in zip(even, odd) for v in pair]


def swap_index(x, lane):
    for bit in (1, 2, 4, 8):
        high = (lane & bit) != 0
        y = list(x)
        for i in range(16):
            if i & bit:
                continue
            y[i] = jnp.where(high, pltpu.roll(x[i + bit], bit, 1), x[i])
            y[i + bit] = jnp.where(high, x[i + bit], pltpu.roll(x[i], 128 - bit, 1))
        x = y
    return x


def halo_rows(after, before, axis):
    row = lax.broadcasted_iota(jnp.int32, after.shape, axis)
    return jnp.where(row < 3, after, jnp.where(row >= 5, before, jnp.zeros_like(after)))


def k1_body(
    offs_ref, order_ref, ck_ref, facet_ref, count_ref, rk_ref, sky_ref, before_ref, after_ref,
    win_ref, tab_ref, cell_ref, out_ref, ext_ref, conv_ref, tw_ref, lhs_ref, u_ref, nat_ref,
):
    tw_ref[0], tw_ref[1] = twiddles(facet_ref[0])
    for b in range(16):
        lanes = slice(128 * b, 128 * (b + 1))
        win = win_ref[:, lanes]
        ext_ref[8:16, lanes] = before_ref[:, lanes].astype(F32) * win
        ext_ref[16:48, lanes] = sky_ref[:, lanes].astype(F32) * win
        ext_ref[48:56, lanes] = after_ref[:, lanes].astype(F32) * win
    for b in range(16):
        lanes = slice(128 * b, 128 * (b + 1))
        own = jnp.zeros((CB, 128), F32)
        lo = jnp.zeros((8, 128), F32)
        hi = jnp.zeros((8, 128), F32)
        for t in range(TAPS):
            k = ck_ref[t]
            own = own + k * ext_ref[13 + t : 45 + t, lanes]
            lo = lo + k * ext_ref[5 + t : 13 + t, lanes]
            hi = hi + k * ext_ref[45 + t : 53 + t, lanes]
        conv_ref[0:CB, lanes] = own
        conv_ref[CB:CE, lanes] = halo_rows(hi, lo, 0)
        conv_ref[CE : CE + 8, lanes] = jnp.zeros((8, 128), F32)

    for g in range(3):
        rows = slice(16 * g, 16 * (g + 1))
        a = real_transform([conv_ref[rows, 128 * b : 128 * (b + 1)] for b in range(16)])
        for m in range(16):
            ar, ai = a[m] if m <= 8 else (a[16 - m][0], -a[16 - m][1])
            c, s = tw_ref[0, m : m + 1, :], tw_ref[1, m : m + 1, :]
            lhs_ref[m, rows, 0:128] = (ar * c + ai * s).astype(BF)
            lhs_ref[m, rows, 128:256] = (ai * c - ar * s).astype(BF)
    u = jnp.dot(lhs_ref[...].reshape(16 * 48, 256), tab_ref[...], preferred_element_type=F32)
    u_ref[...] = u.reshape(16, 48, 256)

    lane = lax.broadcasted_iota(jnp.int32, (8, 128), 1)
    for g in range(5):
        rows = slice(8 * g, 8 * (g + 1))
        for p in range(2):
            x = swap_index([u_ref[m, rows, 128 * p : 128 * (p + 1)] for m in range(16)], lane)
            for b in range(16):
                nat_ref[b, rows, 128 * p : 128 * (p + 1)] = x[b]
            nat_ref[16, rows, 128 * p : 128 * (p + 1)] = x[0]

    lane = lax.broadcasted_iota(jnp.int32, (CE, 128), 1)
    for i in range(NF):
        off = offs_ref[order_ref[i]]
        b, s = off >> 7, off & 127
        back = (128 - s) & 127
        keep = lane >= s
        for p in range(2):
            cols = slice(128 * p, 128 * (p + 1))
            x = jnp.where(keep, nat_ref[b, :, cols], nat_ref[b + 1, :, cols])
            out_ref[i, :, cols] = pltpu.roll(x, back, 1).astype(BF)


SMEM = pl.BlockSpec(memory_space=pltpu.SMEM)
VMEM = pl.BlockSpec(memory_space=pltpu.VMEM)
PARAMS = pltpu.CompilerParams(vmem_limit_bytes=24 * 1024 * 1024)


def k1(offs, order, ck, facet, count, rk, sky, before, after, cell):
    return pl.pallas_call(
        k1_body,
        out_shape=jax.ShapeDtypeStruct((NF, CE, 2 * XC), BF),
        in_specs=[SMEM] * 6 + [VMEM] * 6,
        out_specs=VMEM,
        scratch_shapes=[
            pltpu.VMEM((64, FR), F32),
            pltpu.VMEM((48, FR), F32),
            pltpu.VMEM((2, 16, 128), F32),
            pltpu.VMEM((16, 48, 256), BF),
            pltpu.VMEM((16, 48, 256), F32),
            pltpu.VMEM((17, CE, 256), F32),
        ],
        compiler_params=PARAMS,
        name="facet_to_slots",
    )(
        offs, order, ck, facet, count, rk, sky, before, after, window(),
        jnp.asarray(block_table(), BF), cell,
    )


def k2_body(
    offs_ref, order_ref, facet_ref, count_ref, rk_ref, ck_ref, arr_ref, cell_ref, obs_ref, wt_ref,
    before_ref, after_ref, w_ref, wt_tab_ref, ph_ref,
    res_ref, out_ref, lhs_ref, u_ref, dt_ref, ext_ref, y_ref, pho_ref,
):
    for f in range(NF):
        lhs_ref[f, 0:CE, :] = arr_ref[f]
    off = offs_ref[order_ref[facet_ref[0]]]
    back = (128 - 2 * off) & 127
    pho_ref[0] = pltpu.roll(ph_ref[0], back, 1)
    pho_ref[1] = pltpu.roll(ph_ref[1], back, 1)

    cell = cell_ref[...]
    d = lax.broadcasted_iota(jnp.int32, (SG, VM), 0) - cell + 3
    m = jnp.zeros((SG, VM), F32)
    for t in range(TAPS):
        m = jnp.where(d == t, rk_ref[t], m)
    dt_ref[...] = m.astype(BF)

    u = jnp.dot(lhs_ref[...].reshape(NF * 48, 256), w_ref[...], preferred_element_type=F32)
    u_ref[...] = u.reshape(NF, 48, 2 * SG)
    res = []
    ims = []
    for h in range(2):
        re = jnp.zeros((CE, 128), F32)
        im = jnp.zeros((CE, 128), F32)
        for f in range(NF):
            ur = u_ref[f, 0:CE, 128 * h : 128 * (h + 1)]
            ui = u_ref[f, 0:CE, SG + 128 * h : SG + 128 * (h + 1)]
            pc = pho_ref[0, f : f + 1, :]
            ps = pho_ref[1, f : f + 1, :]
            re = re + (ur * pc - ui * ps)
            im = im + (ur * ps + ui * pc)
        res.append(re)
        ims.append(im)
    grid = jnp.concatenate(
        [jnp.concatenate(res, axis=1), jnp.concatenate(ims, axis=1)], axis=0
    ).astype(BF)
    model = jnp.dot(grid, dt_ref[...], preferred_element_type=F32)

    live = (lax.broadcasted_iota(jnp.int32, (1, VM), 1) < count_ref[0]).astype(F32)
    wt = wt_ref[...] * live
    wt_h = halo_rows(after_ref[:, FR + 2 * VM :], before_ref[:, FR + 2 * VM :], 0).astype(F32) * live
    parts = []
    for p in range(2):
        own = wt * (obs_ref[p].astype(F32) - model[p * CE : p * CE + CB])
        res_ref[p] = own
        cols = slice(FR + p * VM, FR + (p + 1) * VM)
        obs_h = halo_rows(after_ref[:, cols], before_ref[:, cols], 0).astype(F32)
        parts += [own, wt_h * (obs_h - model[p * CE + CB : (p + 1) * CE])]
    rr = jnp.concatenate(parts, axis=0).astype(BF)
    gridded = lax.dot_general(
        rr, dt_ref[...], (((1,), (1,)), ((), ())), preferred_element_type=F32
    )
    backs = []
    for p in range(2):
        halo = gridded[p * CE + CB : (p + 1) * CE]
        ext_ref[p, 0:8, :] = halo
        ext_ref[p, 8:40, :] = gridded[p * CE : p * CE + CB]
        ext_ref[p, 40:48, :] = halo
        b = jnp.zeros((CB, SG), F32)
        for t in range(TAPS):
            b = b + ck_ref[t] * ext_ref[p, 11 - t : 43 - t, :]
        backs.append(b)
    br, bi = backs
    for h in range(2):
        lanes = slice(128 * h, 128 * (h + 1))
        xr, xi = br[:, lanes], bi[:, lanes]
        for f in range(NF):
            pc = pho_ref[0, f : f + 1, :]
            ps = pho_ref[1, f : f + 1, :]
            y_ref[f, :, lanes] = (xr * pc + xi * ps).astype(BF)
            y_ref[f, :, SG + 128 * h : SG + 128 * (h + 1)] = (xi * pc - xr * ps).astype(BF)
    z = jnp.dot(y_ref[...].reshape(NF * CB, 2 * SG), wt_tab_ref[...], preferred_element_type=F32)
    out_ref[...] = z.astype(BF).reshape(NF, CB, 2 * XC)


def k2(offs, order, facet, count, rk, ck, arrived, cell, obs, wt, before, after):
    tab = subgrid_table()
    return pl.pallas_call(
        k2_body,
        out_shape=(
            jax.ShapeDtypeStruct((2, CB, VM), F32),
            jax.ShapeDtypeStruct((NF, CB, 2 * XC), BF),
        ),
        in_specs=[SMEM] * 6 + [VMEM] * 9,
        out_specs=(VMEM, VMEM),
        scratch_shapes=[
            pltpu.VMEM((NF, 48, 256), BF),
            pltpu.VMEM((NF, 48, 2 * SG), F32),
            pltpu.VMEM((SG, VM), BF),
            pltpu.VMEM((2, 48, SG), F32),
            pltpu.VMEM((NF, CB, 2 * SG), BF),
            pltpu.VMEM((2, NF, 128), F32),
        ],
        compiler_params=PARAMS,
        name="slot_round_trip",
    )(
        offs, order, facet, count, rk, ck, arrived, cell, obs, wt, before, after,
        jnp.asarray(tab, BF), jnp.asarray(tab.T, BF), facet_phase(),
    )


def k3_body(
    offs_ref, order_ref, facet_ref, bp_ref, win_ref, tab_ref,
    out_ref, nat_ref, tw_ref, lhs_ref, v_ref,
):
    tw_ref[0], tw_ref[1] = twiddles(facet_ref[0])
    nat_ref[...] = jnp.zeros_like(nat_ref)
    lane = lax.broadcasted_iota(jnp.int32, (CB, 128), 1)
    for i in range(NF):
        off = offs_ref[order_ref[i]]
        b, s = off >> 7, off & 127
        keep = lane >= s
        for p in range(2):
            cols = slice(128 * p, 128 * (p + 1))
            x = pltpu.roll(bp_ref[i, :, cols].astype(F32), s, 1)
            nat_ref[b, :, cols] += jnp.where(keep, x, 0.0)
            nat_ref[b + 1, :, cols] += jnp.where(keep, 0.0, x)
    nat_ref[0] += nat_ref[16]

    lane = lax.broadcasted_iota(jnp.int32, (16, 128), 1)
    for g in range(2):
        rows = slice(16 * g, 16 * (g + 1))
        for p in range(2):
            cols = slice(128 * p, 128 * (p + 1))
            x = swap_index([nat_ref[b, rows, cols] for b in range(16)], lane)
            for m in range(16):
                lhs_ref[m, rows, cols] = x[m].astype(BF)
    v = jnp.dot(lhs_ref[...].reshape(16 * CB, 256), tab_ref[...], preferred_element_type=F32)
    v_ref[...] = v.reshape(16, CB, 256)
    for g in range(4):
        rows = slice(8 * g, 8 * (g + 1))
        t = []
        for m in range(16):
            vr, vi = v_ref[m, rows, 0:128], v_ref[m, rows, 128:256]
            c, s = tw_ref[0, m : m + 1, :], tw_ref[1, m : m + 1, :]
            t.append((vr * c - vi * s, vr * s + vi * c))
        h = [(t[m][0] + t[-m % 16][0], t[m][1] - t[-m % 16][1]) for m in range(9)]
        x = real_inverse(h)
        for b in range(16):
            lanes = slice(128 * b, 128 * (b + 1))
            out_ref[rows, lanes] = x[b] * (0.5 * win_ref[:, lanes])


def k3(offs, order, facet, bp):
    return pl.pallas_call(
        k3_body,
        out_shape=jax.ShapeDtypeStruct((CB, FR), F32),
        in_specs=[SMEM, SMEM, SMEM, VMEM, VMEM, VMEM],
        out_specs=VMEM,
        scratch_shapes=[
            pltpu.VMEM((17, CB, 256), F32),
            pltpu.VMEM((2, 16, 128), F32),
            pltpu.VMEM((16, CB, 256), BF),
            pltpu.VMEM((16, CB, 256), F32),
        ],
        compiler_params=PARAMS,
        name="slots_to_facet",
    )(offs, order, facet, bp, window(), jnp.asarray(block_table().T, BF))


def neighbours(first, last):
    n = lax.axis_size("uv")
    up = [(i, i + 1) for i in range(n - 1)]
    down = [(i + 1, i) for i in range(n - 1)]
    return lax.ppermute(last, "uv", up), lax.ppermute(first, "uv", down)


def local(
    sky_image, subgrid_offsets, owner_order, visibility_count, visibility_cell, observed,
    visibility_weight, row_kernel, column_kernel,
):
    facet = lax.axis_index("facet").astype(jnp.int32).reshape(1)
    obs = observed[0]
    wt = visibility_weight[0]

    def edge(rows):
        return jnp.concatenate(
            [sky_image[rows], obs[0, rows], obs[1, rows], wt[rows].astype(BF)], axis=1
        )

    before, after = neighbours(edge(slice(0, 8)), edge(slice(24, 32)))
    out = k1(
        subgrid_offsets, owner_order, column_kernel, facet, visibility_count, row_kernel,
        sky_image, before, after, visibility_cell,
    )
    arrived = lax.all_to_all(out, "facet", split_axis=0, concat_axis=0, tiled=True)
    res, outgoing = k2(
        subgrid_offsets, owner_order, facet, visibility_count, row_kernel, column_kernel,
        arrived, visibility_cell, obs, wt, before, after,
    )
    back = lax.all_to_all(outgoing, "facet", split_axis=0, concat_axis=0, tiled=True)
    dirty = k3(subgrid_offsets, owner_order, facet, back)
    return (res[None], dirty)


def solution(mesh):
    in_specs = (
        P("uv", "facet"),
        P(),
        P(),
        P("facet"),
        P("facet", None),
        P("facet", None, "uv", None),
        P("facet", "uv", None),
        P(),
        P(),
    )
    out_specs = (P("facet", None, "uv", None), P("uv", "facet"))
    return jax.shard_map(local, mesh=mesh, in_specs=in_specs, out_specs=out_specs, check_vma=False)
```

```python
import math

import jax
import jax.numpy as jnp
import numpy as np
from jax import lax
from jax.experimental import pallas as pl
from jax.experimental.pallas import tpu as pltpu
from jax.sharding import PartitionSpec as P

FR = 2048
XC = 128
SG = 256
NF = 32
CB = 32
CE = 40
TAPS = 7
VM = 512
BF = jnp.bfloat16
F32 = jnp.float32


def block_table():
    lane = np.arange(128)[None, :]
    g = 8 * (lane % 16) + lane // 16
    row = np.arange(128)[:, None] + 64
    a = 2.0 * np.pi * ((g * row) % 128) / 128
    c, s = np.cos(a), np.sin(a)
    return np.block([[c, -s], [s, c]]).astype(np.float32)


def subgrid_table():
    j = np.arange(SG)[None, :]
    k = np.arange(XC)[:, None]
    a = 2.0 * np.pi * ((j * k) % SG) / SG
    c, s = np.cos(a) / 64.0, np.sin(a) / 64.0
    return np.block([[c, s], [-s, c]]).astype(np.float32)


def facet_phase():
    f = np.arange(NF)[:, None]
    j = np.arange(128)[None, :]
    a = 2.0 * np.pi * ((j * (2 * f + 1)) % 64) / 64
    return np.stack([np.cos(a), np.sin(a)]).astype(np.float32)


def window():
    r = np.arange(FR)
    return (np.sin((r + 0.5) * np.pi / FR) / math.sqrt(FR)).astype(np.float32)[None, :]


def turn(n):
    q = (n + 256) >> 9
    x = (n - (q << 9)).astype(F32) * (math.pi / 1024.0)
    y = x * x
    c = 1.0 + y * (-0.5 + y * (1.0 / 24 + y * (-1.0 / 720 + y * (1.0 / 40320))))
    s = x * (1.0 + y * (-1.0 / 6 + y * (1.0 / 120 + y * (-1.0 / 5040 + y * (1.0 / 362880)))))
    odd = (q & 1) == 1
    cos = jnp.where(odd, s, c)
    sin = jnp.where(odd, c, s)
    cos = jnp.where(((q + 1) & 2) == 2, -cos, cos)
    sin = jnp.where((q & 2) == 2, -sin, sin)
    return cos, sin


def twiddles(facet):
    m = lax.broadcasted_iota(jnp.int32, (16, 128), 0)
    lane = lax.broadcasted_iota(jnp.int32, (16, 128), 1)
    return turn((m * (lane + 64 + 128 * facet)) & (FR - 1))


def cmul(a, w):
    wr, wi = w
    if abs(wi) < 1e-12:
        return a if abs(wr - 1) < 1e-12 else (a[0] * wr, a[1] * wr)
    if abs(wr) < 1e-12:
        return (-a[1], a[0]) if wi > 0 else (a[1], -a[0])
    return (a[0] * wr - a[1] * wi, a[0] * wi + a[1] * wr)


def real_transform(x):
    n = len(x)
    if n == 2:
        zero = jnp.zeros_like(x[0])
        return [(x[0] + x[1], zero), (x[0] - x[1], zero)]
    even, odd = real_transform(x[::2]), real_transform(x[1::2])
    out = [None] * (n // 2 + 1)
    for k in range(n // 4 + 1):
        a = 2.0 * math.pi * k / n
        o = cmul(odd[k], (math.cos(a), -math.sin(a)))
        e = even[k]
        out[k] = (e[0] + o[0], e[1] + o[1])
        if k != n // 2 - k:
            out[n // 2 - k] = (e[0] - o[0], o[1] - e[1])
    return out


def real_inverse(h):
    n = 2 * (len(h) - 1)
    if n == 2:
        return [h[0][0] + h[1][0], h[0][0] - h[1][0]]
    even, odd = [], []
    for k in range(n // 4 + 1):
        a, b = h[k], h[n // 2 - k]
        t = 2.0 * math.pi * k / n
        even.append((a[0] + b[0], a[1] - b[1]))
        odd.append(cmul((a[0] - b[0], a[1] + b[1]), (math.cos(t), math.sin(t))))
    even, odd = real_inverse(even), real_inverse(odd)
    return [v for pair in zip(even, odd) for v in pair]


def swap_index(x, lane):
    for bit in (1, 2, 4, 8):
        high = (lane & bit) != 0
        y = list(x)
        for i in range(16):
            if i & bit:
                continue
            y[i] = jnp.where(high, pltpu.roll(x[i + bit], bit, 1), x[i])
            y[i + bit] = jnp.where(high, x[i + bit], pltpu.roll(x[i], 128 - bit, 1))
        x = y
    return x


def halo_rows(after, before, axis):
    row = lax.broadcasted_iota(jnp.int32, after.shape, axis)
    return jnp.where(row < 3, after, jnp.where(row >= 5, before, jnp.zeros_like(after)))


def k1_body(
    offs_ref, order_ref, facet_ref, count_ref, rk_ref, ck_ref, sky_ref, win_ref, tab_ref, cell_ref,
    out_ref, tw_ref, lhs_ref, u_ref, nat_ref,
):
    tw_ref[0], tw_ref[1] = twiddles(facet_ref[0])
    for g in range(2):
        rows = slice(16 * g, 16 * (g + 1))
        x = []
        for b in range(16):
            lanes = slice(128 * b, 128 * (b + 1))
            x.append(sky_ref[rows, lanes].astype(F32) * win_ref[:, lanes])
        a = real_transform(x)
        for m in range(16):
            ar, ai = a[m] if m <= 8 else (a[16 - m][0], -a[16 - m][1])
            c, s = tw_ref[0, m : m + 1, :], tw_ref[1, m : m + 1, :]
            lhs_ref[m, rows, 0:128] = (ar * c + ai * s).astype(BF)
            lhs_ref[m, rows, 128:256] = (ai * c - ar * s).astype(BF)
    u = jnp.dot(lhs_ref[...].reshape(16 * CB, 256), tab_ref[...], preferred_element_type=F32)
    u_ref[...] = u.reshape(16, CB, 256)

    lane = lax.broadcasted_iota(jnp.int32, (8, 128), 1)
    for g in range(4):
        rows = slice(8 * g, 8 * (g + 1))
        for p in range(2):
            cols = slice(128 * p, 128 * (p + 1))
            x = swap_index([u_ref[m, rows, cols] for m in range(16)], lane)
            for b in range(16):
                nat_ref[b, rows, cols] = x[b]
            nat_ref[16, rows, cols] = x[0]

    lane = lax.broadcasted_iota(jnp.int32, (CB, 128), 1)
    for i in range(NF):
        off = offs_ref[order_ref[i]]
        b, s = off >> 7, off & 127
        back = (128 - s) & 127
        keep = lane >= s
        for p in range(2):
            cols = slice(128 * p, 128 * (p + 1))
            x = jnp.where(keep, nat_ref[b, :, cols], nat_ref[b + 1, :, cols])
            out_ref[i, :, cols] = pltpu.roll(x, back, 1).astype(BF)


SMEM = pl.BlockSpec(memory_space=pltpu.SMEM)
VMEM = pl.BlockSpec(memory_space=pltpu.VMEM)
PARAMS = pltpu.CompilerParams(vmem_limit_bytes=24 * 1024 * 1024)


def k1(offs, order, facet, count, rk, ck, sky, cell):
    return pl.pallas_call(
        k1_body,
        out_shape=jax.ShapeDtypeStruct((NF, CB, 2 * XC), BF),
        in_specs=[SMEM] * 6 + [VMEM] * 4,
        out_specs=VMEM,
        scratch_shapes=[
            pltpu.VMEM((2, 16, 128), F32),
            pltpu.VMEM((16, CB, 256), BF),
            pltpu.VMEM((16, CB, 256), F32),
            pltpu.VMEM((17, CB, 256), F32),
        ],
        compiler_params=PARAMS,
        name="facet_to_slots",
    )(
        offs, order, facet, count, rk, ck, sky, window(), jnp.asarray(block_table(), BF), cell
    )


def slot_phases(offs_ref, order_ref, facet_ref, ph_ref, pho_ref):
    off = offs_ref[order_ref[facet_ref[0]]]
    back = (128 - 2 * off) & 127
    pho_ref[0] = pltpu.roll(ph_ref[0], back, 1)
    pho_ref[1] = pltpu.roll(ph_ref[1], back, 1)


def ka_body(
    offs_ref, order_ref, facet_ref, arr_ref, obs_ref, wt_ref, w_ref, ph_ref,
    sub_ref, first_ref, last_ref, u_ref, pho_ref,
):
    slot_phases(offs_ref, order_ref, facet_ref, ph_ref, pho_ref)
    u = jnp.dot(arr_ref[...].reshape(NF * CB, 256), w_ref[...], preferred_element_type=F32)
    u_ref[...] = u.reshape(NF, CB, 2 * SG)
    for h in range(2):
        re = jnp.zeros((CB, 128), F32)
        im = jnp.zeros((CB, 128), F32)
        for f in range(NF):
            ur = u_ref[f, :, 128 * h : 128 * (h + 1)]
            ui = u_ref[f, :, SG + 128 * h : SG + 128 * (h + 1)]
            pc = pho_ref[0, f : f + 1, :]
            ps = pho_ref[1, f : f + 1, :]
            re = re + (ur * pc - ui * ps)
            im = im + (ur * ps + ui * pc)
        sub_ref[:, 128 * h : 128 * (h + 1)] = re
        sub_ref[:, SG + 128 * h : SG + 128 * (h + 1)] = im
    for ref, rows in ((first_ref, slice(0, 8)), (last_ref, slice(24, 32))):
        ref[:, 0 : 2 * SG] = sub_ref[rows, :].astype(BF)
        ref[:, 2 * SG : 2 * SG + VM] = obs_ref[0, rows, :]
        ref[:, 2 * SG + VM : 2 * SG + 2 * VM] = obs_ref[1, rows, :]
        ref[:, 2 * SG + 2 * VM :] = wt_ref[rows, :].astype(BF)


EDGE = 2 * SG + 3 * VM


def ka(offs, order, facet, arrived, obs, wt):
    return pl.pallas_call(
        ka_body,
        out_shape=(
            jax.ShapeDtypeStruct((CB, 2 * SG), F32),
            jax.ShapeDtypeStruct((8, EDGE), BF),
            jax.ShapeDtypeStruct((8, EDGE), BF),
        ),
        in_specs=[SMEM] * 3 + [VMEM] * 5,
        out_specs=(VMEM, VMEM, VMEM),
        scratch_shapes=[
            pltpu.VMEM((NF, CB, 2 * SG), F32),
            pltpu.VMEM((2, NF, 128), F32),
        ],
        compiler_params=PARAMS,
        name="sum_facets",
    )(offs, order, facet, arrived, obs, wt, jnp.asarray(subgrid_table(), BF), facet_phase())


def kb_body(
    offs_ref, order_ref, facet_ref, count_ref, rk_ref, ck_ref, sub_ref, cell_ref, obs_ref, wt_ref,
    before_ref, after_ref, wt_tab_ref, ph_ref,
    res_ref, out_ref, dt_ref, sub_ext_ref, ext_ref, y_ref, pho_ref,
):
    slot_phases(offs_ref, order_ref, facet_ref, ph_ref, pho_ref)
    cell = cell_ref[...]
    d = lax.broadcasted_iota(jnp.int32, (SG, VM), 0) - cell + 3
    m = jnp.zeros((SG, VM), F32)
    for t in range(TAPS):
        m = jnp.where(d == t, rk_ref[t], m)
    dt_ref[...] = m.astype(BF)

    sub_ext_ref[8:16, :] = before_ref[:, 0 : 2 * SG].astype(F32)
    sub_ext_ref[16:48, :] = sub_ref[...]
    sub_ext_ref[48:56, :] = after_ref[:, 0 : 2 * SG].astype(F32)
    parts = []
    for p in range(2):
        lanes = slice(SG * p, SG * (p + 1))
        own = jnp.zeros((CB, SG), F32)
        lo = jnp.zeros((8, SG), F32)
        hi = jnp.zeros((8, SG), F32)
        for t in range(TAPS):
            k = ck_ref[t]
            own = own + k * sub_ext_ref[13 + t : 45 + t, lanes]
            lo = lo + k * sub_ext_ref[5 + t : 13 + t, lanes]
            hi = hi + k * sub_ext_ref[45 + t : 53 + t, lanes]
        parts += [own, halo_rows(hi, lo, 0)]
    grid = jnp.concatenate(parts, axis=0).astype(BF)
    model = jnp.dot(grid, dt_ref[...], preferred_element_type=F32)

    live = (lax.broadcasted_iota(jnp.int32, (1, VM), 1) < count_ref[0]).astype(F32)
    wt = wt_ref[...] * live
    cols = slice(2 * SG + 2 * VM, EDGE)
    wt_h = halo_rows(after_ref[:, cols].astype(F32), before_ref[:, cols].astype(F32), 0) * live
    parts = []
    for p in range(2):
        own = wt * (obs_ref[p].astype(F32) - model[p * CE : p * CE + CB])
        res_ref[p] = own
        cols = slice(2 * SG + p * VM, 2 * SG + (p + 1) * VM)
        obs_h = halo_rows(after_ref[:, cols].astype(F32), before_ref[:, cols].astype(F32), 0)
        parts += [own, wt_h * (obs_h - model[p * CE + CB : (p + 1) * CE])]
    rr = jnp.concatenate(parts, axis=0).astype(BF)
    gridded = lax.dot_general(
        rr, dt_ref[...], (((1,), (1,)), ((), ())), preferred_element_type=F32
    )
    backs = []
    for p in range(2):
        halo = gridded[p * CE + CB : (p + 1) * CE]
        ext_ref[p, 0:8, :] = halo
        ext_ref[p, 8:40, :] = gridded[p * CE : p * CE + CB]
        ext_ref[p, 40:48, :] = halo
        b = jnp.zeros((CB, SG), F32)
        for t in range(TAPS):
            b = b + ck_ref[t] * ext_ref[p, 11 - t : 43 - t, :]
        backs.append(b)
    br, bi = backs
    for h in range(2):
        lanes = slice(128 * h, 128 * (h + 1))
        xr, xi = br[:, lanes], bi[:, lanes]
        for f in range(NF):
            pc = pho_ref[0, f : f + 1, :]
            ps = pho_ref[1, f : f + 1, :]
            y_ref[f, :, lanes] = (xr * pc + xi * ps).astype(BF)
            y_ref[f, :, SG + 128 * h : SG + 128 * (h + 1)] = (xi * pc - xr * ps).astype(BF)
    z = jnp.dot(y_ref[...].reshape(NF * CB, 2 * SG), wt_tab_ref[...], preferred_element_type=F32)
    out_ref[...] = z.astype(BF).reshape(NF, CB, 2 * XC)


def kb(offs, order, facet, count, rk, ck, sub, cell, obs, wt, before, after):
    return pl.pallas_call(
        kb_body,
        out_shape=(
            jax.ShapeDtypeStruct((2, CB, VM), F32),
            jax.ShapeDtypeStruct((NF, CB, 2 * XC), BF),
        ),
        in_specs=[SMEM] * 6 + [VMEM] * 8,
        out_specs=(VMEM, VMEM),
        scratch_shapes=[
            pltpu.VMEM((SG, VM), BF),
            pltpu.VMEM((64, 2 * SG), F32),
            pltpu.VMEM((2, 48, SG), F32),
            pltpu.VMEM((NF, CB, 2 * SG), BF),
            pltpu.VMEM((2, NF, 128), F32),
        ],
        compiler_params=PARAMS,
        name="slot_round_trip",
    )(
        offs, order, facet, count, rk, ck, sub, cell, obs, wt, before, after,
        jnp.asarray(subgrid_table().T, BF), facet_phase(),
    )


def k3_body(
    offs_ref, order_ref, facet_ref, bp_ref, win_ref, tab_ref,
    out_ref, nat_ref, tw_ref, lhs_ref, v_ref,
):
    tw_ref[0], tw_ref[1] = twiddles(facet_ref[0])
    nat_ref[...] = jnp.zeros_like(nat_ref)
    lane = lax.broadcasted_iota(jnp.int32, (CB, 128), 1)
    for i in range(NF):
        off = offs_ref[order_ref[i]]
        b, s = off >> 7, off & 127
        keep = lane >= s
        for p in range(2):
            cols = slice(128 * p, 128 * (p + 1))
            x = pltpu.roll(bp_ref[i, :, cols].astype(F32), s, 1)
            nat_ref[b, :, cols] += jnp.where(keep, x, 0.0)
            nat_ref[b + 1, :, cols] += jnp.where(keep, 0.0, x)
    nat_ref[0] += nat_ref[16]

    lane = lax.broadcasted_iota(jnp.int32, (16, 128), 1)
    for g in range(2):
        rows = slice(16 * g, 16 * (g + 1))
        for p in range(2):
            cols = slice(128 * p, 128 * (p + 1))
            x = swap_index([nat_ref[b, rows, cols] for b in range(16)], lane)
            for m in range(16):
                lhs_ref[m, rows, cols] = x[m].astype(BF)
    v = jnp.dot(lhs_ref[...].reshape(16 * CB, 256), tab_ref[...], preferred_element_type=F32)
    v_ref[...] = v.reshape(16, CB, 256)
    for g in range(4):
        rows = slice(8 * g, 8 * (g + 1))
        t = []
        for m in range(16):
            vr, vi = v_ref[m, rows, 0:128], v_ref[m, rows, 128:256]
            c, s = tw_ref[0, m : m + 1, :], tw_ref[1, m : m + 1, :]
            t.append((vr * c - vi * s, vr * s + vi * c))
        h = [(t[m][0] + t[-m % 16][0], t[m][1] - t[-m % 16][1]) for m in range(9)]
        x = real_inverse(h)
        for b in range(16):
            lanes = slice(128 * b, 128 * (b + 1))
            out_ref[rows, lanes] = x[b] * (0.5 * win_ref[:, lanes])


def k3(offs, order, facet, bp):
    return pl.pallas_call(
        k3_body,
        out_shape=jax.ShapeDtypeStruct((CB, FR), F32),
        in_specs=[SMEM, SMEM, SMEM, VMEM, VMEM, VMEM],
        out_specs=VMEM,
        scratch_shapes=[
            pltpu.VMEM((17, CB, 256), F32),
            pltpu.VMEM((2, 16, 128), F32),
            pltpu.VMEM((16, CB, 256), BF),
            pltpu.VMEM((16, CB, 256), F32),
        ],
        compiler_params=PARAMS,
        name="slots_to_facet",
    )(offs, order, facet, bp, window(), jnp.asarray(block_table().T, BF))


def neighbours(first, last):
    n = lax.axis_size("uv")
    up = [(i, i + 1) for i in range(n - 1)]
    down = [(i + 1, i) for i in range(n - 1)]
    return lax.ppermute(last, "uv", up), lax.ppermute(first, "uv", down)


def local(
    sky_image, subgrid_offsets, owner_order, visibility_count, visibility_cell, observed,
    visibility_weight, row_kernel, column_kernel,
):
    facet = lax.axis_index("facet").astype(jnp.int32).reshape(1)
    obs = observed[0]
    wt = visibility_weight[0]

    out = k1(
        subgrid_offsets, owner_order, facet, visibility_count, row_kernel, column_kernel,
        sky_image, visibility_cell,
    )
    arrived = lax.all_to_all(out, "facet", split_axis=0, concat_axis=0, tiled=True)
    sub, first, last = ka(subgrid_offsets, owner_order, facet, arrived, obs, wt)
    before, after = neighbours(first, last)
    res, outgoing = kb(
        subgrid_offsets, owner_order, facet, visibility_count, row_kernel, column_kernel,
        sub, visibility_cell, obs, wt, before, after,
    )
    back = lax.all_to_all(outgoing, "facet", split_axis=0, concat_axis=0, tiled=True)
    dirty = k3(subgrid_offsets, owner_order, facet, back)
    return (res[None], dirty)


def solution(mesh):
    in_specs = (
        P("uv", "facet"),
        P(),
        P(),
        P("facet"),
        P("facet", None),
        P("facet", None, "uv", None),
        P("facet", "uv", None),
        P(),
        P(),
    )
    out_specs = (P("facet", None, "uv", None), P("uv", "facet"))
    return jax.shard_map(local, mesh=mesh, in_specs=in_specs, out_specs=out_specs, check_vma=False)
```

```python
import math

import jax
import jax.numpy as jnp
import numpy as np
from jax import lax
from jax.experimental import pallas as pl
from jax.experimental.pallas import tpu as pltpu
from jax.sharding import PartitionSpec as P

FR = 2048
XC = 128
SG = 256
NF = 32
CB = 32
CE = 40
TAPS = 7
VM = 512
BF = jnp.bfloat16
F32 = jnp.float32


def block_table():
    lane = np.arange(128)[None, :]
    g = 8 * (lane % 16) + lane // 16
    row = np.arange(128)[:, None] + 64
    a = 2.0 * np.pi * ((g * row) % 128) / 128
    c, s = np.cos(a), np.sin(a)
    return np.block([[c, -s], [s, c]]).astype(np.float32)


def subgrid_table():
    j = np.arange(SG)[None, :]
    k = np.arange(XC)[:, None]
    a = 2.0 * np.pi * ((j * k) % SG) / SG
    c, s = np.cos(a) / 64.0, np.sin(a) / 64.0
    return np.block([[c, s], [-s, c]]).astype(np.float32)


def facet_phase():
    f = np.arange(NF)[:, None]
    j = np.arange(128)[None, :]
    a = 2.0 * np.pi * ((j * (2 * f + 1)) % 64) / 64
    return np.stack([np.cos(a), np.sin(a)]).astype(np.float32)


def window():
    r = np.arange(FR)
    return (np.sin((r + 0.5) * np.pi / FR) / math.sqrt(FR)).astype(np.float32)[None, :]


def turn(n):
    q = (n + 256) >> 9
    x = (n - (q << 9)).astype(F32) * (math.pi / 1024.0)
    y = x * x
    c = 1.0 + y * (-0.5 + y * (1.0 / 24 + y * (-1.0 / 720 + y * (1.0 / 40320))))
    s = x * (1.0 + y * (-1.0 / 6 + y * (1.0 / 120 + y * (-1.0 / 5040 + y * (1.0 / 362880)))))
    odd = (q & 1) == 1
    cos = jnp.where(odd, s, c)
    sin = jnp.where(odd, c, s)
    cos = jnp.where(((q + 1) & 2) == 2, -cos, cos)
    sin = jnp.where((q & 2) == 2, -sin, sin)
    return cos, sin


def twiddles(facet):
    m = lax.broadcasted_iota(jnp.int32, (16, 128), 0)
    lane = lax.broadcasted_iota(jnp.int32, (16, 128), 1)
    return turn((m * (lane + 64 + 128 * facet)) & (FR - 1))


def make_window(win_ref):
    for b in range(16):
        r = lax.broadcasted_iota(jnp.int32, (8, 128), 1) + (128 * b)
        x = (r.astype(F32) - 1023.5) * (math.pi / FR)
        y = x * x
        c = 1.0 / 24 + y * (-1.0 / 720 + y * (1.0 / 40320 + y * (-1.0 / 3628800 + y / 479001600)))
        win_ref[:, 128 * b : 128 * (b + 1)] = (1.0 + y * (-0.5 + y * c)) * (1.0 / math.sqrt(FR))


def make_block_table(tab_ref, transposed=False):
    lane = lax.broadcasted_iota(jnp.int32, (128, 128), 0 if transposed else 1)
    row = lax.broadcasted_iota(jnp.int32, (128, 128), 1 if transposed else 0) + 64
    g = 8 * (lane & 15) + (lane >> 4)
    c, s = turn((16 * g * row) & (FR - 1))
    c, s, t = c.astype(BF), s.astype(BF), (-s).astype(BF)
    if transposed:
        s, t = t, s
    tab_ref[0:128, 0:128] = c
    tab_ref[0:128, 128:256] = t
    tab_ref[128:256, 0:128] = s
    tab_ref[128:256, 128:256] = c


def cmul(a, w):
    wr, wi = w
    if abs(wi) < 1e-12:
        return a if abs(wr - 1) < 1e-12 else (a[0] * wr, a[1] * wr)
    if abs(wr) < 1e-12:
        return (-a[1], a[0]) if wi > 0 else (a[1], -a[0])
    return (a[0] * wr - a[1] * wi, a[0] * wi + a[1] * wr)


def real_transform(x):
    n = len(x)
    if n == 2:
        zero = jnp.zeros_like(x[0])
        return [(x[0] + x[1], zero), (x[0] - x[1], zero)]
    even, odd = real_transform(x[::2]), real_transform(x[1::2])
    out = [None] * (n // 2 + 1)
    for k in range(n // 4 + 1):
        a = 2.0 * math.pi * k / n
        o = cmul(odd[k], (math.cos(a), -math.sin(a)))
        e = even[k]
        out[k] = (e[0] + o[0], e[1] + o[1])
        if k != n // 2 - k:
            out[n // 2 - k] = (e[0] - o[0], o[1] - e[1])
    return out


def real_inverse(h):
    n = 2 * (len(h) - 1)
    if n == 2:
        return [h[0][0] + h[1][0], h[0][0] - h[1][0]]
    even, odd = [], []
    for k in range(n // 4 + 1):
        a, b = h[k], h[n // 2 - k]
        t = 2.0 * math.pi * k / n
        even.append((a[0] + b[0], a[1] - b[1]))
        odd.append(cmul((a[0] - b[0], a[1] + b[1]), (math.cos(t), math.sin(t))))
    even, odd = real_inverse(even), real_inverse(odd)
    return [v for pair in zip(even, odd) for v in pair]


def swap_index(x, lane):
    for bit in (1, 2, 4, 8):
        high = (lane & bit) != 0
        y = list(x)
        for i in range(16):
            if i & bit:
                continue
            y[i] = jnp.where(high, pltpu.roll(x[i + bit], bit, 1), x[i])
            y[i + bit] = jnp.where(high, x[i + bit], pltpu.roll(x[i], 128 - bit, 1))
        x = y
    return x


def halo_rows(after, before, axis):
    row = lax.broadcasted_iota(jnp.int32, after.shape, axis)
    return jnp.where(row < 3, after, jnp.where(row >= 5, before, jnp.zeros_like(after)))


def k1_body(
    offs_ref, order_ref, sky_hbm,
    out_ref, tw_ref, lhs_ref, u_ref, nat_ref, sky_ref, win_ref, tab_ref, sem,
):
    copy = pltpu.make_async_copy(sky_hbm, sky_ref, sem)
    copy.start()
    tw_ref[0], tw_ref[1] = twiddles(lax.axis_index("facet"))
    make_window(win_ref)
    make_block_table(tab_ref)
    copy.wait()
    for g in range(2):
        rows = slice(16 * g, 16 * (g + 1))
        x = []
        for b in range(16):
            lanes = slice(128 * b, 128 * (b + 1))
            x.append(sky_ref[rows, lanes].astype(F32) * win_ref[0:1, lanes])
        a = real_transform(x)
        for m in range(16):
            ar, ai = a[m] if m <= 8 else (a[16 - m][0], -a[16 - m][1])
            c, s = tw_ref[0, m : m + 1, :], tw_ref[1, m : m + 1, :]
            lhs_ref[m, rows, 0:128] = (ar * c + ai * s).astype(BF)
            lhs_ref[m, rows, 128:256] = (ai * c - ar * s).astype(BF)
    u = jnp.dot(lhs_ref[...].reshape(16 * CB, 256), tab_ref[...], preferred_element_type=F32)
    u_ref[...] = u.reshape(16, CB, 256)

    lane = lax.broadcasted_iota(jnp.int32, (8, 128), 1)
    for g in range(4):
        rows = slice(8 * g, 8 * (g + 1))
        for p in range(2):
            cols = slice(128 * p, 128 * (p + 1))
            x = swap_index([u_ref[m, rows, cols] for m in range(16)], lane)
            for b in range(16):
                nat_ref[b, rows, cols] = x[b]
            nat_ref[16, rows, cols] = x[0]

    lane = lax.broadcasted_iota(jnp.int32, (CB, 128), 1)
    for i in range(NF):
        off = offs_ref[order_ref[i]]
        b, s = off >> 7, off & 127
        back = (128 - s) & 127
        keep = lane >= s
        for p in range(2):
            cols = slice(128 * p, 128 * (p + 1))
            x = jnp.where(keep, nat_ref[b, :, cols], nat_ref[b + 1, :, cols])
            out_ref[i, :, cols] = pltpu.roll(x, back, 1).astype(BF)


SMEM = pl.BlockSpec(memory_space=pltpu.SMEM)
VMEM = pl.BlockSpec(memory_space=pltpu.VMEM)
PARAMS = pltpu.CompilerParams(vmem_limit_bytes=24 * 1024 * 1024)


def k1(offs, order, sky):
    return pl.pallas_call(
        k1_body,
        out_shape=jax.ShapeDtypeStruct((NF, CB, 2 * XC), BF),
        in_specs=[SMEM] * 2 + [pl.BlockSpec(memory_space=pl.ANY)],
        out_specs=VMEM,
        scratch_shapes=[
            pltpu.VMEM((2, 16, 128), F32),
            pltpu.VMEM((16, CB, 256), BF),
            pltpu.VMEM((16, CB, 256), F32),
            pltpu.VMEM((17, CB, 256), F32),
            pltpu.VMEM((CB, FR), BF),
            pltpu.VMEM((8, FR), F32),
            pltpu.VMEM((256, 256), BF),
            pltpu.SemaphoreType.DMA,
        ],
        name="facet_to_slots",
    )(offs, order, sky)


def slot_phases(offs_ref, order_ref, ph_ref, pho_ref):
    off = offs_ref[order_ref[lax.axis_index("facet")]]
    back = (128 - 2 * off) & 127
    pho_ref[0] = pltpu.roll(ph_ref[0], back, 1)
    pho_ref[1] = pltpu.roll(ph_ref[1], back, 1)


def ka_body(
    offs_ref, order_ref, arr_ref, obs_ref, wt_ref, w_ref, ph_ref,
    sub_ref, sibling_ref, neighbour_ref, u_ref, pho_ref,
):
    slot_phases(offs_ref, order_ref, ph_ref, pho_ref)
    u = jnp.dot(arr_ref[...].reshape(NF * CB, 256), w_ref[...], preferred_element_type=F32)
    u_ref[...] = u.reshape(NF, CB, 2 * SG)
    for h in range(2):
        re = jnp.zeros((CB, 128), F32)
        im = jnp.zeros((CB, 128), F32)
        for f in range(NF):
            ur = u_ref[f, :, 128 * h : 128 * (h + 1)]
            ui = u_ref[f, :, SG + 128 * h : SG + 128 * (h + 1)]
            pc = pho_ref[0, f : f + 1, :]
            ps = pho_ref[1, f : f + 1, :]
            re = re + (ur * pc - ui * ps)
            im = im + (ur * ps + ui * pc)
        sub_ref[:, 128 * h : 128 * (h + 1)] = re
        sub_ref[:, SG + 128 * h : SG + 128 * (h + 1)] = im
    even = lax.rem(lax.axis_index("uv"), 2) == 0
    wide = 2 * SG

    def put(cols, first, last):
        sibling_ref[:, cols] = jnp.where(even, last, first).astype(BF)
        neighbour_ref[:, cols] = jnp.where(even, first, last).astype(BF)

    put(slice(0, wide), sub_ref[0:8, :], sub_ref[24:32, :])
    for p in range(2):
        put(
            slice(wide + p * VM, wide + (p + 1) * VM),
            obs_ref[p, 0:8, :].astype(F32),
            obs_ref[p, 24:32, :].astype(F32),
        )
    put(slice(wide + 2 * VM, EDGE), wt_ref[0:8, :], wt_ref[24:32, :])


EDGE = 2 * SG + 3 * VM


def ka(offs, order, arrived, obs, wt):
    return pl.pallas_call(
        ka_body,
        out_shape=(
            jax.ShapeDtypeStruct((CB, 2 * SG), F32),
            jax.ShapeDtypeStruct((8, EDGE), BF),
            jax.ShapeDtypeStruct((8, EDGE), BF),
        ),
        in_specs=[SMEM] * 2 + [VMEM] * 5,
        out_specs=(VMEM, VMEM, VMEM),
        scratch_shapes=[
            pltpu.VMEM((NF, CB, 2 * SG), F32),
            pltpu.VMEM((2, NF, 128), F32),
        ],
        compiler_params=PARAMS,
        name="sum_facets",
    )(offs, order, arrived, obs, wt, jnp.asarray(subgrid_table(), BF), facet_phase())


def kb_body(
    offs_ref, order_ref, count_ref, rk_ref, ck_ref, sub_ref, cell_ref, obs_ref, wt_ref,
    sibling_ref, neighbour_ref, wt_tab_ref, ph_ref,
    res_ref, out_ref, dt_ref, sub_ext_ref, ext_ref, y_ref, pho_ref,
):
    slot_phases(offs_ref, order_ref, ph_ref, pho_ref)
    cell = cell_ref[...]
    d = lax.broadcasted_iota(jnp.int32, (SG, VM), 0) - cell + 3
    m = jnp.zeros((SG, VM), F32)
    for t in range(TAPS):
        m = jnp.where(d == t, rk_ref[t], m)
    dt_ref[...] = m.astype(BF)

    uv = lax.axis_index("uv")
    even = lax.rem(uv, 2) == 0
    in_before, in_after = uv > 0, uv < 7

    def sides(cols):
        s, n = sibling_ref[:, cols].astype(F32), neighbour_ref[:, cols].astype(F32)
        before = jnp.where(in_before, jnp.where(even, n, s), 0.0)
        after = jnp.where(in_after, jnp.where(even, s, n), 0.0)
        return before, after

    before, after = sides(slice(0, 2 * SG))
    sub_ext_ref[8:16, :] = before
    sub_ext_ref[16:48, :] = sub_ref[...]
    sub_ext_ref[48:56, :] = after
    parts = []
    for p in range(2):
        lanes = slice(SG * p, SG * (p + 1))
        own = jnp.zeros((CB, SG), F32)
        lo = jnp.zeros((8, SG), F32)
        hi = jnp.zeros((8, SG), F32)
        for t in range(TAPS):
            k = ck_ref[t]
            own = own + k * sub_ext_ref[13 + t : 45 + t, lanes]
            lo = lo + k * sub_ext_ref[5 + t : 13 + t, lanes]
            hi = hi + k * sub_ext_ref[45 + t : 53 + t, lanes]
        parts += [own, halo_rows(hi, lo, 0)]
    grid = jnp.concatenate(parts, axis=0).astype(BF)
    model = jnp.dot(grid, dt_ref[...], preferred_element_type=F32)

    live = (lax.broadcasted_iota(jnp.int32, (1, VM), 1) < count_ref[0]).astype(F32)
    wt = wt_ref[...] * live
    before, after = sides(slice(2 * SG + 2 * VM, EDGE))
    wt_h = halo_rows(after, before, 0) * live
    parts = []
    for p in range(2):
        own = wt * (obs_ref[p].astype(F32) - model[p * CE : p * CE + CB])
        res_ref[p] = own
        before, after = sides(slice(2 * SG + p * VM, 2 * SG + (p + 1) * VM))
        obs_h = halo_rows(after, before, 0)
        parts += [own, wt_h * (obs_h - model[p * CE + CB : (p + 1) * CE])]
    rr = jnp.concatenate(parts, axis=0).astype(BF)
    gridded = lax.dot_general(
        rr, dt_ref[...], (((1,), (1,)), ((), ())), preferred_element_type=F32
    )
    backs = []
    for p in range(2):
        halo = gridded[p * CE + CB : (p + 1) * CE]
        ext_ref[p, 0:8, :] = halo
        ext_ref[p, 8:40, :] = gridded[p * CE : p * CE + CB]
        ext_ref[p, 40:48, :] = halo
        b = jnp.zeros((CB, SG), F32)
        for t in range(TAPS):
            b = b + ck_ref[t] * ext_ref[p, 11 - t : 43 - t, :]
        backs.append(b)
    br, bi = backs
    for h in range(2):
        lanes = slice(128 * h, 128 * (h + 1))
        xr, xi = br[:, lanes], bi[:, lanes]
        for f in range(NF):
            pc = pho_ref[0, f : f + 1, :]
            ps = pho_ref[1, f : f + 1, :]
            y_ref[f, :, lanes] = (xr * pc + xi * ps).astype(BF)
            y_ref[f, :, SG + 128 * h : SG + 128 * (h + 1)] = (xi * pc - xr * ps).astype(BF)
    z = jnp.dot(y_ref[...].reshape(NF * CB, 2 * SG), wt_tab_ref[...], preferred_element_type=F32)
    out_ref[...] = z.astype(BF).reshape(NF, CB, 2 * XC)


def kb(offs, order, count, rk, ck, sub, cell, obs, wt, sibling, neighbour):
    return pl.pallas_call(
        kb_body,
        out_shape=(
            jax.ShapeDtypeStruct((2, CB, VM), F32),
            jax.ShapeDtypeStruct((NF, CB, 2 * XC), BF),
        ),
        in_specs=[SMEM] * 5 + [VMEM] * 8,
        out_specs=(VMEM, VMEM),
        scratch_shapes=[
            pltpu.VMEM((SG, VM), BF),
            pltpu.VMEM((64, 2 * SG), F32),
            pltpu.VMEM((2, 48, SG), F32),
            pltpu.VMEM((NF, CB, 2 * SG), BF),
            pltpu.VMEM((2, NF, 128), F32),
        ],
        compiler_params=PARAMS,
        name="slot_round_trip",
    )(
        offs, order, count, rk, ck, sub, cell, obs, wt, sibling, neighbour,
        jnp.asarray(subgrid_table().T, BF), facet_phase(),
    )


def k3_body(
    offs_ref, order_ref, bp_ref, win_ref, tab_ref,
    out_ref, nat_ref, tw_ref, lhs_ref, v_ref,
):
    tw_ref[0], tw_ref[1] = twiddles(lax.axis_index("facet"))
    nat_ref[...] = jnp.zeros_like(nat_ref)
    lane = lax.broadcasted_iota(jnp.int32, (CB, 128), 1)
    for i in range(NF):
        off = offs_ref[order_ref[i]]
        b, s = off >> 7, off & 127
        keep = lane >= s
        for p in range(2):
            cols = slice(128 * p, 128 * (p + 1))
            x = pltpu.roll(bp_ref[i, :, cols].astype(F32), s, 1)
            nat_ref[b, :, cols] += jnp.where(keep, x, 0.0)
            nat_ref[b + 1, :, cols] += jnp.where(keep, 0.0, x)
    nat_ref[0] += nat_ref[16]

    lane = lax.broadcasted_iota(jnp.int32, (16, 128), 1)
    for g in range(2):
        rows = slice(16 * g, 16 * (g + 1))
        for p in range(2):
            cols = slice(128 * p, 128 * (p + 1))
            x = swap_index([nat_ref[b, rows, cols] for b in range(16)], lane)
            for m in range(16):
                lhs_ref[m, rows, cols] = x[m].astype(BF)
    v = jnp.dot(lhs_ref[...].reshape(16 * CB, 256), tab_ref[...], preferred_element_type=F32)
    v_ref[...] = v.reshape(16, CB, 256)
    for g in range(4):
        rows = slice(8 * g, 8 * (g + 1))
        t = []
        for m in range(16):
            vr, vi = v_ref[m, rows, 0:128], v_ref[m, rows, 128:256]
            c, s = tw_ref[0, m : m + 1, :], tw_ref[1, m : m + 1, :]
            t.append((vr * c - vi * s, vr * s + vi * c))
        h = [(t[m][0] + t[-m % 16][0], t[m][1] - t[-m % 16][1]) for m in range(9)]
        x = real_inverse(h)
        for b in range(16):
            lanes = slice(128 * b, 128 * (b + 1))
            out_ref[rows, lanes] = x[b] * (0.5 * win_ref[:, lanes])


def k3(offs, order, bp):
    return pl.pallas_call(
        k3_body,
        out_shape=jax.ShapeDtypeStruct((CB, FR), F32),
        in_specs=[SMEM, SMEM, VMEM, VMEM, VMEM],
        out_specs=VMEM,
        scratch_shapes=[
            pltpu.VMEM((17, CB, 256), F32),
            pltpu.VMEM((2, 16, 128), F32),
            pltpu.VMEM((16, CB, 256), BF),
            pltpu.VMEM((16, CB, 256), F32),
        ],
        compiler_params=PARAMS,
        name="slots_to_facet",
    )(offs, order, bp, window(), jnp.asarray(block_table().T, BF))


def swapped(sibling, neighbour):
    n = lax.axis_size("uv")
    near = [(i, i ^ 1) for i in range(n)]
    far = [(i, (i - 1 if i % 2 == 0 else i + 1) % n) for i in range(n)]
    return lax.ppermute(sibling, "uv", near), lax.ppermute(neighbour, "uv", far)


def local(
    sky_image, subgrid_offsets, owner_order, visibility_count, visibility_cell, observed,
    visibility_weight, row_kernel, column_kernel,
):
    obs = observed[0]
    wt = visibility_weight[0]

    out = k1(subgrid_offsets, owner_order, sky_image)
    arrived = lax.all_to_all(out, "facet", split_axis=0, concat_axis=0, tiled=True)
    sub, sibling, neighbour = ka(subgrid_offsets, owner_order, arrived, obs, wt)
    sibling, neighbour = swapped(sibling, neighbour)
    res, outgoing = kb(
        subgrid_offsets, owner_order, visibility_count, row_kernel, column_kernel,
        sub, visibility_cell, obs, wt, sibling, neighbour,
    )
    back = lax.all_to_all(outgoing, "facet", split_axis=0, concat_axis=0, tiled=True)
    dirty = k3(subgrid_offsets, owner_order, back)
    return (res[None], dirty)


def solution(mesh):
    in_specs = (
        P("uv", "facet"),
        P(),
        P(),
        P("facet"),
        P("facet", None),
        P("facet", None, "uv", None),
        P("facet", "uv", None),
        P(),
        P(),
    )
    out_specs = (P("facet", None, "uv", None), P("uv", "facet"))
    return jax.shard_map(local, mesh=mesh, in_specs=in_specs, out_specs=out_specs, check_vma=False)
```

```python
import math

import jax
import jax.numpy as jnp
import numpy as np
from jax import lax
from jax.experimental import pallas as pl
from jax.experimental.pallas import tpu as pltpu
from jax.sharding import PartitionSpec as P

FR = 2048
XC = 128
SG = 256
NF = 32
CB = 32
CE = 40
TAPS = 7
VM = 512
BF = jnp.bfloat16
F32 = jnp.float32


def block_table():
    lane = np.arange(128)[None, :]
    g = 8 * (lane % 16) + lane // 16
    row = np.arange(128)[:, None] + 64
    a = 2.0 * np.pi * ((g * row) % 128) / 128
    c, s = np.cos(a), np.sin(a)
    return np.block([[c, -s], [s, c]]).astype(np.float32)


def subgrid_table():
    j = np.arange(SG)[None, :]
    k = np.arange(XC)[:, None]
    a = 2.0 * np.pi * ((j * k) % SG) / SG
    c, s = np.cos(a) / 64.0, np.sin(a) / 64.0
    return np.block([[c, s], [-s, c]]).astype(np.float32)


def facet_phase():
    f = np.arange(NF)[:, None]
    j = np.arange(128)[None, :]
    a = 2.0 * np.pi * ((j * (2 * f + 1)) % 64) / 64
    return np.stack([np.cos(a), np.sin(a)]).astype(np.float32)


def window():
    r = np.arange(FR)
    return (np.sin((r + 0.5) * np.pi / FR) / math.sqrt(FR)).astype(np.float32)[None, :]


def turn(n):
    q = (n + 256) >> 9
    x = (n - (q << 9)).astype(F32) * (math.pi / 1024.0)
    y = x * x
    c = 1.0 + y * (-0.5 + y * (1.0 / 24 + y * (-1.0 / 720 + y * (1.0 / 40320))))
    s = x * (1.0 + y * (-1.0 / 6 + y * (1.0 / 120 + y * (-1.0 / 5040 + y * (1.0 / 362880)))))
    odd = (q & 1) == 1
    cos = jnp.where(odd, s, c)
    sin = jnp.where(odd, c, s)
    cos = jnp.where(((q + 1) & 2) == 2, -cos, cos)
    sin = jnp.where((q & 2) == 2, -sin, sin)
    return cos, sin


def twiddles(facet):
    m = lax.broadcasted_iota(jnp.int32, (16, 128), 0)
    lane = lax.broadcasted_iota(jnp.int32, (16, 128), 1)
    return turn((m * (lane + 64 + 128 * facet)) & (FR - 1))


def make_window(win_ref):
    for b in range(16):
        r = lax.broadcasted_iota(jnp.int32, (8, 128), 1) + (128 * b)
        x = (r.astype(F32) - 1023.5) * (math.pi / FR)
        y = x * x
        c = 1.0 / 24 + y * (-1.0 / 720 + y * (1.0 / 40320 + y * (-1.0 / 3628800 + y / 479001600)))
        win_ref[:, 128 * b : 128 * (b + 1)] = (1.0 + y * (-0.5 + y * c)) * (1.0 / math.sqrt(FR))


def make_block_table(tab_ref, transposed=False):
    lane = lax.broadcasted_iota(jnp.int32, (128, 128), 0 if transposed else 1)
    row = lax.broadcasted_iota(jnp.int32, (128, 128), 1 if transposed else 0) + 64
    g = 8 * (lane & 15) + (lane >> 4)
    c, s = turn((16 * g * row) & (FR - 1))
    c, s, t = c.astype(BF), s.astype(BF), (-s).astype(BF)
    if transposed:
        s, t = t, s
    tab_ref[0:128, 0:128] = c
    tab_ref[0:128, 128:256] = t
    tab_ref[128:256, 0:128] = s
    tab_ref[128:256, 128:256] = c


def cmul(a, w):
    wr, wi = w
    if abs(wi) < 1e-12:
        return a if abs(wr - 1) < 1e-12 else (a[0] * wr, a[1] * wr)
    if abs(wr) < 1e-12:
        return (-a[1], a[0]) if wi > 0 else (a[1], -a[0])
    return (a[0] * wr - a[1] * wi, a[0] * wi + a[1] * wr)


def real_transform(x):
    n = len(x)
    if n == 2:
        zero = jnp.zeros_like(x[0])
        return [(x[0] + x[1], zero), (x[0] - x[1], zero)]
    even, odd = real_transform(x[::2]), real_transform(x[1::2])
    out = [None] * (n // 2 + 1)
    for k in range(n // 4 + 1):
        a = 2.0 * math.pi * k / n
        o = cmul(odd[k], (math.cos(a), -math.sin(a)))
        e = even[k]
        out[k] = (e[0] + o[0], e[1] + o[1])
        if k != n // 2 - k:
            out[n // 2 - k] = (e[0] - o[0], o[1] - e[1])
    return out


def real_inverse(h):
    n = 2 * (len(h) - 1)
    if n == 2:
        return [h[0][0] + h[1][0], h[0][0] - h[1][0]]
    even, odd = [], []
    for k in range(n // 4 + 1):
        a, b = h[k], h[n // 2 - k]
        t = 2.0 * math.pi * k / n
        even.append((a[0] + b[0], a[1] - b[1]))
        odd.append(cmul((a[0] - b[0], a[1] + b[1]), (math.cos(t), math.sin(t))))
    even, odd = real_inverse(even), real_inverse(odd)
    return [v for pair in zip(even, odd) for v in pair]


def lanes_of(shape):
    return lax.broadcasted_iota(jnp.int32, shape, 1).astype(F32).astype(BF)


def swap_index(x):
    lane = lax.broadcasted_iota(jnp.int32, x[0].shape, 1)
    for bit in (1, 2, 4, 8):
        high = (lane & bit).astype(F32).astype(BF) > 0
        y = list(x)
        for i in range(16):
            if i & bit:
                continue
            y[i] = jnp.where(high, pltpu.roll(x[i + bit], bit, 1), x[i])
            y[i + bit] = jnp.where(high, x[i + bit], pltpu.roll(x[i], 128 - bit, 1))
        x = y
    return x


def halo_rows(after, before, axis):
    row = lax.broadcasted_iota(jnp.int32, after.shape, axis)
    return jnp.where(row < 3, after, jnp.where(row >= 5, before, jnp.zeros_like(after)))


def k1_body(
    offs_hbm, order_hbm, sky_hbm,
    out_hbm, offs_ref, order_ref, tw_ref, lhs_ref, u_ref, nat_ref, sky_ref, win_ref, tab_ref,
    out_ref, sky_sem, small_sem, out_sem,
):
    halves = [
        pltpu.make_async_copy(
            sky_hbm.at[pl.ds(16 * g, 16), :], sky_ref.at[pl.ds(16 * g, 16), :], sky_sem.at[g]
        )
        for g in range(2)
    ]
    small = [
        pltpu.make_async_copy(offs_hbm, offs_ref, small_sem.at[0]),
        pltpu.make_async_copy(order_hbm, order_ref, small_sem.at[1]),
    ]
    for copy in halves + small:
        copy.start()
    tw_ref[0], tw_ref[1] = twiddles(lax.axis_index("facet"))
    make_window(win_ref)
    make_block_table(tab_ref)
    for g in range(2):
        halves[g].wait()
        rows = slice(16 * g, 16 * (g + 1))
        x = []
        for b in range(16):
            lanes = slice(128 * b, 128 * (b + 1))
            x.append(sky_ref[rows, lanes].astype(F32) * win_ref[0:1, lanes])
        a = real_transform(x)
        for m in range(16):
            ar, ai = a[m] if m <= 8 else (a[16 - m][0], -a[16 - m][1])
            c, s = tw_ref[0, m : m + 1, :], tw_ref[1, m : m + 1, :]
            lhs_ref[m, rows, 0:128] = (ar * c + ai * s).astype(BF)
            lhs_ref[m, rows, 128:256] = (ai * c - ar * s).astype(BF)
    u = jnp.dot(lhs_ref[...].reshape(16 * CB, 256), tab_ref[...], preferred_element_type=F32)
    u_ref[...] = u.astype(BF).reshape(16, CB, 256)

    for g in range(2):
        rows = slice(16 * g, 16 * (g + 1))
        for p in range(2):
            cols = slice(128 * p, 128 * (p + 1))
            x = swap_index([u_ref[m, rows, cols] for m in range(16)])
            for b in range(16):
                nat_ref[b, rows, cols] = x[b]
            nat_ref[16, rows, cols] = x[0]

    for copy in small:
        copy.wait()
    lane = lanes_of((CB, 128))
    done = []
    for i in range(NF):
        off = offs_ref[order_ref[i]]
        b, s = off >> 7, off & 127
        back = (128 - s) & 127
        keep = lane >= s.astype(F32).astype(BF)
        for p in range(2):
            cols = slice(128 * p, 128 * (p + 1))
            x = jnp.where(keep, nat_ref[b, :, cols], nat_ref[b + 1, :, cols])
            out_ref[i, :, cols] = pltpu.roll(x, back, 1)
        if i % 8 == 7:
            part = pl.ds(i - 7, 8)
            copy = pltpu.make_async_copy(out_ref.at[part], out_hbm.at[part], out_sem.at[i // 8])
            copy.start()
            done.append(copy)
    for copy in done:
        copy.wait()


SMEM = pl.BlockSpec(memory_space=pltpu.SMEM)
VMEM = pl.BlockSpec(memory_space=pltpu.VMEM)
ANY = pl.BlockSpec(memory_space=pl.ANY)
PARAMS = pltpu.CompilerParams(vmem_limit_bytes=24 * 1024 * 1024)


def k1(offs, order, sky):
    return pl.pallas_call(
        k1_body,
        out_shape=jax.ShapeDtypeStruct((NF, CB, 2 * XC), BF),
        in_specs=[ANY] * 3,
        out_specs=ANY,
        scratch_shapes=[
            pltpu.SMEM((NF,), jnp.int32),
            pltpu.SMEM((NF,), jnp.int32),
            pltpu.VMEM((2, 16, 128), F32),
            pltpu.VMEM((16, CB, 256), BF),
            pltpu.VMEM((16, CB, 256), BF),
            pltpu.VMEM((17, CB, 256), BF),
            pltpu.VMEM((CB, FR), BF),
            pltpu.VMEM((8, FR), F32),
            pltpu.VMEM((256, 256), BF),
            pltpu.VMEM((NF, CB, 256), BF),
            pltpu.SemaphoreType.DMA((2,)),
            pltpu.SemaphoreType.DMA((2,)),
            pltpu.SemaphoreType.DMA((4,)),
        ],
        name="facet_to_slots",
    )(offs, order, sky)


def kt_body(
    offs_ref, order_ref, rk_ref, ck_ref, count_ref, cell_ref, ph_ref,
    dt_ref, pho_ref, live_ref,
):
    off = offs_ref[order_ref[lax.axis_index("facet")]]
    back = (128 - 2 * off) & 127
    pho_ref[0] = pltpu.roll(ph_ref[0], back, 1)
    pho_ref[1] = pltpu.roll(ph_ref[1], back, 1)
    d = lax.broadcasted_iota(jnp.int32, (SG, VM), 0) - cell_ref[...] + 3
    m = jnp.zeros((SG, VM), F32)
    for t in range(TAPS):
        m = jnp.where(d == t, rk_ref[t], m)
    dt_ref[...] = m.astype(BF)
    live_ref[...] = (lax.broadcasted_iota(jnp.int32, (1, VM), 1) < count_ref[0]).astype(F32)


def kt(offs, order, rk, ck, count, cell):
    return pl.pallas_call(
        kt_body,
        out_shape=(
            jax.ShapeDtypeStruct((SG, VM), BF),
            jax.ShapeDtypeStruct((2, NF, 128), F32),
            jax.ShapeDtypeStruct((1, VM), F32),
        ),
        in_specs=[SMEM] * 5 + [VMEM] * 2,
        out_specs=(VMEM, VMEM, VMEM),
        compiler_params=PARAMS,
        cost_estimate=pl.CostEstimate(flops=2000000, bytes_accessed=400000, transcendentals=0),
        name="slot_tables",
    )(offs, order, rk, ck, count, cell, facet_phase())


def ka_body(
    arr_ref, obs_ref, wt_ref, w_ref, pho_ref,
    sub_ref, sibling_ref, neighbour_ref, u_ref,
):
    u = jnp.dot(arr_ref[...].reshape(NF * CB, 256), w_ref[...], preferred_element_type=F32)
    u_ref[...] = u.reshape(NF, CB, 2 * SG)
    for h in range(2):
        re = jnp.zeros((CB, 128), F32)
        im = jnp.zeros((CB, 128), F32)
        for f in range(NF):
            ur = u_ref[f, :, 128 * h : 128 * (h + 1)]
            ui = u_ref[f, :, SG + 128 * h : SG + 128 * (h + 1)]
            pc = pho_ref[0, f : f + 1, :]
            ps = pho_ref[1, f : f + 1, :]
            re = re + (ur * pc - ui * ps)
            im = im + (ur * ps + ui * pc)
        sub_ref[:, 128 * h : 128 * (h + 1)] = re
        sub_ref[:, SG + 128 * h : SG + 128 * (h + 1)] = im
    even = lax.rem(lax.axis_index("uv"), 2) == 0
    wide = 2 * SG

    def put(cols, first, last):
        sibling_ref[:, cols] = jnp.where(even, last, first).astype(BF)
        neighbour_ref[:, cols] = jnp.where(even, first, last).astype(BF)

    put(slice(0, wide), sub_ref[0:8, :], sub_ref[24:32, :])
    for p in range(2):
        put(
            slice(wide + p * VM, wide + (p + 1) * VM),
            obs_ref[p, 0:8, :].astype(F32),
            obs_ref[p, 24:32, :].astype(F32),
        )
    put(slice(wide + 2 * VM, EDGE), wt_ref[0:8, :], wt_ref[24:32, :])


EDGE = 2 * SG + 3 * VM


def ka(arrived, obs, wt, phases):
    return pl.pallas_call(
        ka_body,
        out_shape=(
            jax.ShapeDtypeStruct((CB, 2 * SG), F32),
            jax.ShapeDtypeStruct((8, EDGE), BF),
            jax.ShapeDtypeStruct((8, EDGE), BF),
        ),
        in_specs=[VMEM] * 5,
        out_specs=(VMEM, VMEM, VMEM),
        scratch_shapes=[pltpu.VMEM((NF, CB, 2 * SG), F32)],
        compiler_params=PARAMS,
        name="sum_facets",
    )(arrived, obs, wt, jnp.asarray(subgrid_table(), BF), phases)


def kb_body(
    ck_ref, sub_ref, obs_ref, wt_ref, sibling_ref, neighbour_ref, wt_tab_ref, dt_ref, pho_ref,
    live_ref,
    res_hbm, out_ref, sub_ext_ref, conv_ref, res_ref, ext_ref, back_ref, y_ref, sem,
):
    uv = lax.axis_index("uv")
    even = lax.rem(uv, 2) == 0
    in_before, in_after = uv > 0, uv < 7

    def sides(cols):
        s, n = sibling_ref[:, cols].astype(F32), neighbour_ref[:, cols].astype(F32)
        before = jnp.where(in_before, jnp.where(even, n, s), 0.0)
        after = jnp.where(in_after, jnp.where(even, s, n), 0.0)
        return before, after

    before, after = sides(slice(0, 2 * SG))
    sub_ext_ref[8:16, :] = before
    sub_ext_ref[16:48, :] = sub_ref[...]
    sub_ext_ref[48:56, :] = after
    for p in range(2):
        lanes = slice(SG * p, SG * (p + 1))
        own = jnp.zeros((CB, SG), F32)
        lo = jnp.zeros((8, SG), F32)
        hi = jnp.zeros((8, SG), F32)
        for t in range(TAPS):
            k = ck_ref[t]
            own = own + k * sub_ext_ref[13 + t : 45 + t, lanes]
            lo = lo + k * sub_ext_ref[5 + t : 13 + t, lanes]
            hi = hi + k * sub_ext_ref[45 + t : 53 + t, lanes]
        conv_ref[p * CE : p * CE + CB, :] = own
        conv_ref[p * CE + CB : (p + 1) * CE, :] = halo_rows(hi, lo, 0)
    model = jnp.dot(conv_ref[...].astype(BF), dt_ref[...], preferred_element_type=F32)

    live = live_ref[...]
    wt = wt_ref[...] * live
    before, after = sides(slice(2 * SG + 2 * VM, EDGE))
    wt_h = halo_rows(after, before, 0) * live
    parts = []
    for p in range(2):
        own = wt * (obs_ref[p].astype(F32) - model[p * CE : p * CE + CB])
        res_ref[p] = own
        before, after = sides(slice(2 * SG + p * VM, 2 * SG + (p + 1) * VM))
        obs_h = halo_rows(after, before, 0)
        parts += [own, wt_h * (obs_h - model[p * CE + CB : (p + 1) * CE])]
    copy = pltpu.make_async_copy(res_ref, res_hbm, sem)
    copy.start()
    rr = jnp.concatenate(parts, axis=0).astype(BF)
    gridded = lax.dot_general(
        rr, dt_ref[...], (((1,), (1,)), ((), ())), preferred_element_type=F32
    )
    for p in range(2):
        halo = gridded[p * CE + CB : (p + 1) * CE]
        ext_ref[p, 0:8, :] = halo
        ext_ref[p, 8:40, :] = gridded[p * CE : p * CE + CB]
        ext_ref[p, 40:48, :] = halo
        b = jnp.zeros((CB, SG), F32)
        for t in range(TAPS):
            b = b + ck_ref[t] * ext_ref[p, 11 - t : 43 - t, :]
        back_ref[p] = b
    for h in range(2):
        lanes = slice(128 * h, 128 * (h + 1))
        xr, xi = back_ref[0, :, lanes], back_ref[1, :, lanes]
        for f in range(NF):
            pc = pho_ref[0, f : f + 1, :]
            ps = pho_ref[1, f : f + 1, :]
            y_ref[f, :, lanes] = (xr * pc + xi * ps).astype(BF)
            y_ref[f, :, SG + 128 * h : SG + 128 * (h + 1)] = (xi * pc - xr * ps).astype(BF)
    z = jnp.dot(y_ref[...].reshape(NF * CB, 2 * SG), wt_tab_ref[...], preferred_element_type=F32)
    out_ref[...] = z.astype(BF).reshape(NF, CB, 2 * XC)
    copy.wait()


def kb(ck, sub, obs, wt, sibling, neighbour, table, phases, live):
    return pl.pallas_call(
        kb_body,
        out_shape=(
            jax.ShapeDtypeStruct((2, CB, VM), F32),
            jax.ShapeDtypeStruct((NF, CB, 2 * XC), BF),
        ),
        in_specs=[SMEM] + [VMEM] * 9,
        out_specs=(ANY, VMEM),
        scratch_shapes=[
            pltpu.VMEM((64, 2 * SG), F32),
            pltpu.VMEM((2 * CE, SG), F32),
            pltpu.VMEM((2, CB, VM), F32),
            pltpu.VMEM((2, 48, SG), F32),
            pltpu.VMEM((2, CB, SG), F32),
            pltpu.VMEM((NF, CB, 2 * SG), BF),
            pltpu.SemaphoreType.DMA,
        ],
        compiler_params=PARAMS,
        name="slot_round_trip",
    )(
        ck, sub, obs, wt, sibling, neighbour, jnp.asarray(subgrid_table().T, BF), table, phases,
        live,
    )


def k3_body(
    offs_ref, order_ref, bp_ref, win_ref, tab_ref,
    out_hbm, nat_ref, tw_ref, lhs_ref, v_ref, out_ref, sem,
):
    tw_ref[0], tw_ref[1] = twiddles(lax.axis_index("facet"))
    nat_ref[...] = jnp.zeros_like(nat_ref)
    lane = lax.broadcasted_iota(jnp.int32, (CB, 128), 1)
    for i in range(NF):
        off = offs_ref[order_ref[i]]
        b, s = off >> 7, off & 127
        keep = lane >= s
        for p in range(2):
            cols = slice(128 * p, 128 * (p + 1))
            x = pltpu.roll(bp_ref[i, :, cols], s, 1).astype(F32)
            nat_ref[b, :, cols] += jnp.where(keep, x, 0.0)
            nat_ref[b + 1, :, cols] += jnp.where(keep, 0.0, x)
    nat_ref[0] += nat_ref[16]

    for g in range(2):
        rows = slice(16 * g, 16 * (g + 1))
        for p in range(2):
            cols = slice(128 * p, 128 * (p + 1))
            x = swap_index([nat_ref[b, rows, cols].astype(BF) for b in range(16)])
            for m in range(16):
                lhs_ref[m, rows, cols] = x[m]
    v = jnp.dot(lhs_ref[...].reshape(16 * CB, 256), tab_ref[...], preferred_element_type=F32)
    v_ref[...] = v.reshape(16, CB, 256)
    done = []
    for g in range(4):
        rows = slice(8 * g, 8 * (g + 1))
        t = []
        for m in range(16):
            vr, vi = v_ref[m, rows, 0:128], v_ref[m, rows, 128:256]
            c, s = tw_ref[0, m : m + 1, :], tw_ref[1, m : m + 1, :]
            t.append((vr * c - vi * s, vr * s + vi * c))
        h = [(t[m][0] + t[-m % 16][0], t[m][1] - t[-m % 16][1]) for m in range(9)]
        x = real_inverse(h)
        for b in range(16):
            lanes = slice(128 * b, 128 * (b + 1))
            out_ref[rows, lanes] = x[b] * (0.5 * win_ref[:, lanes])
        part = pl.ds(8 * g, 8)
        copy = pltpu.make_async_copy(out_ref.at[part, :], out_hbm.at[part, :], sem.at[g])
        copy.start()
        done.append(copy)
    for copy in done:
        copy.wait()


def k3(offs, order, bp):
    return pl.pallas_call(
        k3_body,
        out_shape=jax.ShapeDtypeStruct((CB, FR), F32),
        in_specs=[SMEM, SMEM, VMEM, VMEM, VMEM],
        out_specs=ANY,
        scratch_shapes=[
            pltpu.VMEM((17, CB, 256), F32),
            pltpu.VMEM((2, 16, 128), F32),
            pltpu.VMEM((16, CB, 256), BF),
            pltpu.VMEM((16, CB, 256), F32),
            pltpu.VMEM((CB, FR), F32),
            pltpu.SemaphoreType.DMA((4,)),
        ],
        compiler_params=PARAMS,
        name="slots_to_facet",
    )(offs, order, bp, window(), jnp.asarray(block_table().T, BF))


def swapped(sibling, neighbour):
    n = lax.axis_size("uv")
    near = [(i, i ^ 1) for i in range(n)]
    far = [(i, (i - 1 if i % 2 == 0 else i + 1) % n) for i in range(n)]
    return lax.ppermute(sibling, "uv", near), lax.ppermute(neighbour, "uv", far)


def local(
    sky_image, subgrid_offsets, owner_order, visibility_count, visibility_cell, observed,
    visibility_weight, row_kernel, column_kernel,
):
    obs = observed[0]
    wt = visibility_weight[0]

    out = k1(subgrid_offsets, owner_order, sky_image)
    arrived = lax.all_to_all(out, "facet", split_axis=0, concat_axis=0, tiled=True)
    table, phases, live = kt(
        subgrid_offsets, owner_order, row_kernel, column_kernel, visibility_count, visibility_cell
    )
    sub, sibling, neighbour = ka(arrived, obs, wt, phases)
    sibling, neighbour = swapped(sibling, neighbour)
    res, outgoing = kb(
        column_kernel, sub, obs, wt, sibling, neighbour, table, phases, live
    )
    back = lax.all_to_all(outgoing, "facet", split_axis=0, concat_axis=0, tiled=True)
    dirty = k3(subgrid_offsets, owner_order, back)
    return (res[None], dirty)


def solution(mesh):
    in_specs = (
        P("uv", "facet"),
        P(),
        P(),
        P("facet"),
        P("facet", None),
        P("facet", None, "uv", None),
        P("facet", "uv", None),
        P(),
        P(),
    )
    out_specs = (P("facet", None, "uv", None), P("uv", "facet"))
    return jax.shard_map(local, mesh=mesh, in_specs=in_specs, out_specs=out_specs, check_vma=False)
```

```python
import math

import jax
import jax.numpy as jnp
import numpy as np
from jax import lax
from jax.experimental import pallas as pl
from jax.experimental.pallas import tpu as pltpu
from jax.sharding import PartitionSpec as P

FR = 2048
XC = 128
SG = 256
NF = 32
CB = 32
CE = 40
TAPS = 7
VM = 512
BF = jnp.bfloat16
F32 = jnp.float32


def block_table():
    lane = np.arange(128)[None, :]
    g = 8 * (lane % 16) + lane // 16
    row = np.arange(128)[:, None] + 64
    a = 2.0 * np.pi * ((g * row) % 128) / 128
    c, s = np.cos(a), np.sin(a)
    return np.block([[c, -s], [s, c]]).astype(np.float32)


def facet_phase():
    f = np.arange(NF)[:, None]
    j = np.arange(128)[None, :]
    a = 2.0 * np.pi * ((j * (2 * f + 1)) % 64) / 64
    return np.stack([np.cos(a), np.sin(a)]).astype(np.float32)


def window():
    r = np.arange(FR)
    return (np.sin((r + 0.5) * np.pi / FR) / math.sqrt(FR)).astype(np.float32)[None, :]


def turn(n):
    q = (n + 256) >> 9
    x = (n - (q << 9)).astype(F32) * (math.pi / 1024.0)
    y = x * x
    c = 1.0 + y * (-0.5 + y * (1.0 / 24 + y * (-1.0 / 720 + y * (1.0 / 40320))))
    s = x * (1.0 + y * (-1.0 / 6 + y * (1.0 / 120 + y * (-1.0 / 5040 + y * (1.0 / 362880)))))
    odd = (q & 1) == 1
    cos = jnp.where(odd, s, c)
    sin = jnp.where(odd, c, s)
    cos = jnp.where(((q + 1) & 2) == 2, -cos, cos)
    sin = jnp.where((q & 2) == 2, -sin, sin)
    return cos, sin


def twiddles(facet):
    m = lax.broadcasted_iota(jnp.int32, (16, 128), 0)
    lane = lax.broadcasted_iota(jnp.int32, (16, 128), 1)
    return turn((m * (lane + 64 + 128 * facet)) & (FR - 1))


def make_window(win_ref):
    for b in range(16):
        r = lax.broadcasted_iota(jnp.int32, (8, 128), 1) + (128 * b)
        x = (r.astype(F32) - 1023.5) * (math.pi / FR)
        y = x * x
        c = 1.0 / 24 + y * (-1.0 / 720 + y * (1.0 / 40320 + y * (-1.0 / 3628800 + y / 479001600)))
        win_ref[:, 128 * b : 128 * (b + 1)] = (1.0 + y * (-0.5 + y * c)) * (1.0 / math.sqrt(FR))


def make_block_table(tab_ref, transposed=False):
    lane = lax.broadcasted_iota(jnp.int32, (128, 128), 0 if transposed else 1)
    row = lax.broadcasted_iota(jnp.int32, (128, 128), 1 if transposed else 0) + 64
    g = 8 * (lane & 15) + (lane >> 4)
    c, s = turn((16 * g * row) & (FR - 1))
    c, s, t = c.astype(BF), s.astype(BF), (-s).astype(BF)
    if transposed:
        s, t = t, s
    tab_ref[0:128, 0:128] = c
    tab_ref[0:128, 128:256] = t
    tab_ref[128:256, 0:128] = s
    tab_ref[128:256, 128:256] = c


def cmul(a, w):
    wr, wi = w
    if abs(wi) < 1e-12:
        return a if abs(wr - 1) < 1e-12 else (a[0] * wr, a[1] * wr)
    if abs(wr) < 1e-12:
        return (-a[1], a[0]) if wi > 0 else (a[1], -a[0])
    return (a[0] * wr - a[1] * wi, a[0] * wi + a[1] * wr)


def real_transform(x):
    n = len(x)
    if n == 2:
        zero = jnp.zeros_like(x[0])
        return [(x[0] + x[1], zero), (x[0] - x[1], zero)]
    even, odd = real_transform(x[::2]), real_transform(x[1::2])
    out = [None] * (n // 2 + 1)
    for k in range(n // 4 + 1):
        a = 2.0 * math.pi * k / n
        o = cmul(odd[k], (math.cos(a), -math.sin(a)))
        e = even[k]
        out[k] = (e[0] + o[0], e[1] + o[1])
        if k != n // 2 - k:
            out[n // 2 - k] = (e[0] - o[0], o[1] - e[1])
    return out


def real_inverse(h):
    n = 2 * (len(h) - 1)
    if n == 2:
        return [h[0][0] + h[1][0], h[0][0] - h[1][0]]
    even, odd = [], []
    for k in range(n // 4 + 1):
        a, b = h[k], h[n // 2 - k]
        t = 2.0 * math.pi * k / n
        even.append((a[0] + b[0], a[1] - b[1]))
        odd.append(cmul((a[0] - b[0], a[1] + b[1]), (math.cos(t), math.sin(t))))
    even, odd = real_inverse(even), real_inverse(odd)
    return [v for pair in zip(even, odd) for v in pair]


def lanes_of(shape):
    return lax.broadcasted_iota(jnp.int32, shape, 1).astype(F32).astype(BF)


def swap_index(x):
    lane = lax.broadcasted_iota(jnp.int32, x[0].shape, 1)
    for bit in (1, 2, 4, 8):
        high = (lane & bit).astype(F32).astype(BF) > 0
        y = list(x)
        for i in range(16):
            if i & bit:
                continue
            y[i] = jnp.where(high, pltpu.roll(x[i + bit], bit, 1), x[i])
            y[i + bit] = jnp.where(high, x[i + bit], pltpu.roll(x[i], 128 - bit, 1))
        x = y
    return x


def halo_rows(after, before, axis):
    row = lax.broadcasted_iota(jnp.int32, after.shape, axis)
    return jnp.where(row < 3, after, jnp.where(row >= 5, before, jnp.zeros_like(after)))


def k1_body(
    offs_hbm, order_hbm, sky_hbm,
    out_hbm, offs_ref, order_ref, tw_ref, lhs_ref, u_ref, nat_ref, sky_ref, win_ref, tab_ref,
    out_ref, sky_sem, small_sem, out_sem,
):
    halves = [
        pltpu.make_async_copy(
            sky_hbm.at[pl.ds(16 * g, 16), :], sky_ref.at[pl.ds(16 * g, 16), :], sky_sem.at[g]
        )
        for g in range(2)
    ]
    small = [
        pltpu.make_async_copy(offs_hbm, offs_ref, small_sem.at[0]),
        pltpu.make_async_copy(order_hbm, order_ref, small_sem.at[1]),
    ]
    for copy in halves + small:
        copy.start()
    tw_ref[0], tw_ref[1] = twiddles(lax.axis_index("facet"))
    make_window(win_ref)
    make_block_table(tab_ref)
    for g in range(2):
        halves[g].wait()
        rows = slice(16 * g, 16 * (g + 1))
        x = []
        for b in range(16):
            lanes = slice(128 * b, 128 * (b + 1))
            x.append(sky_ref[rows, lanes].astype(F32) * win_ref[0:1, lanes])
        a = real_transform(x)
        for m in range(16):
            ar, ai = a[m] if m <= 8 else (a[16 - m][0], -a[16 - m][1])
            c, s = tw_ref[0, m : m + 1, :], tw_ref[1, m : m + 1, :]
            lhs_ref[m, rows, 0:128] = (ar * c + ai * s).astype(BF)
            lhs_ref[m, rows, 128:256] = (ai * c - ar * s).astype(BF)
    u = jnp.dot(lhs_ref[...].reshape(16 * CB, 256), tab_ref[...], preferred_element_type=F32)
    u_ref[...] = u.astype(BF).reshape(16, CB, 256)

    for g in range(2):
        rows = slice(16 * g, 16 * (g + 1))
        for p in range(2):
            cols = slice(128 * p, 128 * (p + 1))
            x = swap_index([u_ref[m, rows, cols] for m in range(16)])
            for b in range(16):
                nat_ref[b, rows, cols] = x[b]
            nat_ref[16, rows, cols] = x[0]

    for copy in small:
        copy.wait()
    lane = lanes_of((CB, 128))
    done = []
    for i in range(NF):
        off = offs_ref[order_ref[i]]
        b, s = off >> 7, off & 127
        keep = lane >= s.astype(F32).astype(BF)
        for p in range(2):
            cols = slice(128 * p, 128 * (p + 1))
            out_ref[i, :, cols] = jnp.where(keep, nat_ref[b, :, cols], nat_ref[b + 1, :, cols])
        if i % 8 == 7:
            part = pl.ds(i - 7, 8)
            copy = pltpu.make_async_copy(out_ref.at[part], out_hbm.at[part], out_sem.at[i // 8])
            copy.start()
            done.append(copy)
    for copy in done:
        copy.wait()


SMEM = pl.BlockSpec(memory_space=pltpu.SMEM)
VMEM = pl.BlockSpec(memory_space=pltpu.VMEM)
ANY = pl.BlockSpec(memory_space=pl.ANY)
PARAMS = pltpu.CompilerParams(vmem_limit_bytes=24 * 1024 * 1024)


def k1(offs, order, sky):
    return pl.pallas_call(
        k1_body,
        out_shape=jax.ShapeDtypeStruct((NF, CB, 2 * XC), BF),
        in_specs=[ANY] * 3,
        out_specs=ANY,
        scratch_shapes=[
            pltpu.SMEM((NF,), jnp.int32),
            pltpu.SMEM((NF,), jnp.int32),
            pltpu.VMEM((2, 16, 128), F32),
            pltpu.VMEM((16, CB, 256), BF),
            pltpu.VMEM((16, CB, 256), BF),
            pltpu.VMEM((17, CB, 256), BF),
            pltpu.VMEM((CB, FR), BF),
            pltpu.VMEM((8, FR), F32),
            pltpu.VMEM((256, 256), BF),
            pltpu.VMEM((NF, CB, 256), BF),
            pltpu.SemaphoreType.DMA((2,)),
            pltpu.SemaphoreType.DMA((2,)),
            pltpu.SemaphoreType.DMA((4,)),
        ],
        name="facet_to_slots",
    )(offs, order, sky)


def kt_body(
    offs_ref, order_ref, rk_ref, ck_ref, count_ref, cell_ref, ph_ref,
    dt_ref, pho_ref, live_ref, w_ref, back_ref, taps_ref,
):
    off = offs_ref[order_ref[lax.axis_index("facet")]]
    back = (128 - 2 * off) & 127
    pho_ref[0] = pltpu.roll(ph_ref[0], back, 1)
    pho_ref[1] = pltpu.roll(ph_ref[1], back, 1)
    d = lax.broadcasted_iota(jnp.int32, (SG, VM), 0) - cell_ref[...] + 3
    m = jnp.zeros((SG, VM), F32)
    for t in range(TAPS):
        m = jnp.where(d == t, rk_ref[t], m)
        taps_ref[t : t + 1, :] = jnp.full((1, SG), ck_ref[t], F32)
    taps_ref[TAPS : TAPS + 1, :] = jnp.zeros((1, SG), F32)
    dt_ref[...] = m.astype(BF)
    live_ref[...] = (lax.broadcasted_iota(jnp.int32, (1, VM), 1) < count_ref[0]).astype(F32)
    for ref, shape, axis in ((w_ref, (XC, SG), 0), (back_ref, (SG, XC), 1)):
        k = (lax.broadcasted_iota(jnp.int32, shape, axis) - off) & (XC - 1)
        j = lax.broadcasted_iota(jnp.int32, shape, 1 - axis)
        c, s = turn((8 * j * k) & (FR - 1))
        c, s, t = (x.astype(BF) for x in (c * (1 / 64), s * (1 / 64), s * (-1 / 64)))
        rows, cols = shape
        ref[0:rows, 0:cols] = c
        ref[rows:, cols:] = c
        ref[0:rows, cols:] = s if axis == 0 else t
        ref[rows:, 0:cols] = t if axis == 0 else s


def kt(offs, order, rk, ck, count, cell):
    return pl.pallas_call(
        kt_body,
        out_shape=(
            jax.ShapeDtypeStruct((SG, VM), BF),
            jax.ShapeDtypeStruct((2, NF, 128), F32),
            jax.ShapeDtypeStruct((1, VM), F32),
            jax.ShapeDtypeStruct((2 * XC, 2 * SG), BF),
            jax.ShapeDtypeStruct((2 * SG, 2 * XC), BF),
            jax.ShapeDtypeStruct((8, SG), F32),
        ),
        in_specs=[SMEM] * 5 + [VMEM] * 2,
        out_specs=(VMEM,) * 6,
        compiler_params=PARAMS,
        cost_estimate=pl.CostEstimate(flops=4000000, bytes_accessed=1000000, transcendentals=0),
        name="slot_tables",
    )(offs, order, rk, ck, count, cell, facet_phase())


def ka_body(
    arr_ref, obs_ref, wt_ref, w_ref, pho_ref,
    sub_ref, sibling_ref, neighbour_ref, u_ref,
):
    u = jnp.dot(arr_ref[...].reshape(NF * CB, 256), w_ref[...], preferred_element_type=F32)
    u_ref[...] = u.reshape(NF, CB, 2 * SG)
    for h in range(2):
        re = jnp.zeros((CB, 128), F32)
        im = jnp.zeros((CB, 128), F32)
        for f in range(NF):
            ur = u_ref[f, :, 128 * h : 128 * (h + 1)]
            ui = u_ref[f, :, SG + 128 * h : SG + 128 * (h + 1)]
            pc = pho_ref[0, f : f + 1, :]
            ps = pho_ref[1, f : f + 1, :]
            re = re + (ur * pc - ui * ps)
            im = im + (ur * ps + ui * pc)
        sub_ref[:, 128 * h : 128 * (h + 1)] = re
        sub_ref[:, SG + 128 * h : SG + 128 * (h + 1)] = im
    even = lax.rem(lax.axis_index("uv"), 2) == 0
    wide = 2 * SG

    def put(cols, first, last):
        sibling_ref[:, cols] = jnp.where(even, last, first).astype(BF)
        neighbour_ref[:, cols] = jnp.where(even, first, last).astype(BF)

    put(slice(0, wide), sub_ref[0:8, :], sub_ref[24:32, :])
    for p in range(2):
        put(
            slice(wide + p * VM, wide + (p + 1) * VM),
            obs_ref[p, 0:8, :].astype(F32),
            obs_ref[p, 24:32, :].astype(F32),
        )
    put(slice(wide + 2 * VM, EDGE), wt_ref[0:8, :], wt_ref[24:32, :])


EDGE = 2 * SG + 3 * VM


def ka(arrived, obs, wt, table, phases):
    return pl.pallas_call(
        ka_body,
        out_shape=(
            jax.ShapeDtypeStruct((CB, 2 * SG), F32),
            jax.ShapeDtypeStruct((8, EDGE), BF),
            jax.ShapeDtypeStruct((8, EDGE), BF),
        ),
        in_specs=[VMEM] * 5,
        out_specs=(VMEM, VMEM, VMEM),
        scratch_shapes=[pltpu.VMEM((NF, CB, 2 * SG), F32)],
        compiler_params=PARAMS,
        name="sum_facets",
    )(arrived, obs, wt, table, phases)


def kb_body(
    taps_ref, sub_ref, obs_ref, wt_ref, sibling_ref, neighbour_ref, wt_tab_ref, dt_ref, pho_ref,
    live_ref,
    res_hbm, out_ref, sub_ext_ref, conv_ref, res_ref, ext_ref, back_ref, y_ref, sem,
):
    uv = lax.axis_index("uv")
    even = lax.rem(uv, 2) == 0
    in_before, in_after = uv > 0, uv < 7

    def sides(cols):
        s, n = sibling_ref[:, cols].astype(F32), neighbour_ref[:, cols].astype(F32)
        before = jnp.where(in_before, jnp.where(even, n, s), 0.0)
        after = jnp.where(in_after, jnp.where(even, s, n), 0.0)
        return before, after

    before, after = sides(slice(0, 2 * SG))
    sub_ext_ref[8:16, :] = before
    sub_ext_ref[16:48, :] = sub_ref[...]
    sub_ext_ref[48:56, :] = after
    for p in range(2):
        lanes = slice(SG * p, SG * (p + 1))
        own = jnp.zeros((CB, SG), F32)
        lo = jnp.zeros((8, SG), F32)
        hi = jnp.zeros((8, SG), F32)
        for t in range(TAPS):
            k = taps_ref[t : t + 1, :]
            own = own + k * sub_ext_ref[13 + t : 45 + t, lanes]
            lo = lo + k * sub_ext_ref[5 + t : 13 + t, lanes]
            hi = hi + k * sub_ext_ref[45 + t : 53 + t, lanes]
        conv_ref[p * CE : p * CE + CB, :] = own
        conv_ref[p * CE + CB : (p + 1) * CE, :] = halo_rows(hi, lo, 0)
    model = jnp.dot(conv_ref[...].astype(BF), dt_ref[...], preferred_element_type=F32)

    live = live_ref[...]
    wt = wt_ref[...] * live
    before, after = sides(slice(2 * SG + 2 * VM, EDGE))
    wt_h = halo_rows(after, before, 0) * live
    parts = []
    for p in range(2):
        own = wt * (obs_ref[p].astype(F32) - model[p * CE : p * CE + CB])
        res_ref[p] = own
        before, after = sides(slice(2 * SG + p * VM, 2 * SG + (p + 1) * VM))
        obs_h = halo_rows(after, before, 0)
        parts += [own, wt_h * (obs_h - model[p * CE + CB : (p + 1) * CE])]
    copy = pltpu.make_async_copy(res_ref, res_hbm, sem)
    copy.start()
    rr = jnp.concatenate(parts, axis=0).astype(BF)
    gridded = lax.dot_general(
        rr, dt_ref[...], (((1,), (1,)), ((), ())), preferred_element_type=F32
    )
    for p in range(2):
        halo = gridded[p * CE + CB : (p + 1) * CE]
        ext_ref[p, 0:8, :] = halo
        ext_ref[p, 8:40, :] = gridded[p * CE : p * CE + CB]
        ext_ref[p, 40:48, :] = halo
        b = jnp.zeros((CB, SG), F32)
        for t in range(TAPS):
            b = b + taps_ref[t : t + 1, :] * ext_ref[p, 11 - t : 43 - t, :]
        back_ref[p] = b
    for h in range(2):
        lanes = slice(128 * h, 128 * (h + 1))
        xr, xi = back_ref[0, :, lanes], back_ref[1, :, lanes]
        for f in range(NF):
            pc = pho_ref[0, f : f + 1, :]
            ps = pho_ref[1, f : f + 1, :]
            y_ref[f, :, lanes] = (xr * pc + xi * ps).astype(BF)
            y_ref[f, :, SG + 128 * h : SG + 128 * (h + 1)] = (xi * pc - xr * ps).astype(BF)
    z = jnp.dot(y_ref[...].reshape(NF * CB, 2 * SG), wt_tab_ref[...], preferred_element_type=F32)
    out_ref[...] = z.astype(BF).reshape(NF, CB, 2 * XC)
    copy.wait()


def kb(taps, sub, obs, wt, sibling, neighbour, back, table, phases, live):
    return pl.pallas_call(
        kb_body,
        out_shape=(
            jax.ShapeDtypeStruct((2, CB, VM), F32),
            jax.ShapeDtypeStruct((NF, CB, 2 * XC), BF),
        ),
        in_specs=[VMEM] * 10,
        out_specs=(ANY, VMEM),
        scratch_shapes=[
            pltpu.VMEM((64, 2 * SG), F32),
            pltpu.VMEM((2 * CE, SG), F32),
            pltpu.VMEM((2, CB, VM), F32),
            pltpu.VMEM((2, 48, SG), F32),
            pltpu.VMEM((2, CB, SG), F32),
            pltpu.VMEM((NF, CB, 2 * SG), BF),
            pltpu.SemaphoreType.DMA,
        ],
        compiler_params=PARAMS,
        name="slot_round_trip",
    )(
        taps, sub, obs, wt, sibling, neighbour, back, table, phases, live
    )


def k3_body(
    offs_hbm, order_hbm, bp_ref, win_ref, tab_ref,
    out_hbm, offs_ref, order_ref, nat_ref, tw_ref, lhs_ref, v_ref, out_ref, small_sem, sem,
):
    small = [
        pltpu.make_async_copy(offs_hbm, offs_ref, small_sem.at[0]),
        pltpu.make_async_copy(order_hbm, order_ref, small_sem.at[1]),
    ]
    for copy in small:
        copy.start()
    tw_ref[0], tw_ref[1] = twiddles(lax.axis_index("facet"))
    nat_ref[...] = jnp.zeros_like(nat_ref)
    for copy in small:
        copy.wait()
    lane = lax.broadcasted_iota(jnp.int32, (CB, 128), 1)
    for i in range(NF):
        off = offs_ref[order_ref[i]]
        b, s = off >> 7, off & 127
        keep = lane >= s
        for p in range(2):
            cols = slice(128 * p, 128 * (p + 1))
            x = bp_ref[i, :, cols].astype(F32)
            nat_ref[b, :, cols] += jnp.where(keep, x, 0.0)
            nat_ref[b + 1, :, cols] += jnp.where(keep, 0.0, x)
    nat_ref[0] += nat_ref[16]

    for g in range(2):
        rows = slice(16 * g, 16 * (g + 1))
        for p in range(2):
            cols = slice(128 * p, 128 * (p + 1))
            x = swap_index([nat_ref[b, rows, cols].astype(BF) for b in range(16)])
            for m in range(16):
                lhs_ref[m, rows, cols] = x[m]
    v = jnp.dot(lhs_ref[...].reshape(16 * CB, 256), tab_ref[...], preferred_element_type=F32)
    v_ref[...] = v.reshape(16, CB, 256)
    done = []
    for g in range(4):
        rows = slice(8 * g, 8 * (g + 1))
        t = []
        for m in range(16):
            vr, vi = v_ref[m, rows, 0:128], v_ref[m, rows, 128:256]
            c, s = tw_ref[0, m : m + 1, :], tw_ref[1, m : m + 1, :]
            t.append((vr * c - vi * s, vr * s + vi * c))
        h = [(t[m][0] + t[-m % 16][0], t[m][1] - t[-m % 16][1]) for m in range(9)]
        x = real_inverse(h)
        for b in range(16):
            lanes = slice(128 * b, 128 * (b + 1))
            out_ref[rows, lanes] = x[b] * (0.5 * win_ref[:, lanes])
        part = pl.ds(8 * g, 8)
        copy = pltpu.make_async_copy(out_ref.at[part, :], out_hbm.at[part, :], sem.at[g])
        copy.start()
        done.append(copy)
    for copy in done:
        copy.wait()


def k3(offs, order, bp):
    return pl.pallas_call(
        k3_body,
        out_shape=jax.ShapeDtypeStruct((CB, FR), F32),
        in_specs=[ANY, ANY, VMEM, VMEM, VMEM],
        out_specs=ANY,
        scratch_shapes=[
            pltpu.SMEM((NF,), jnp.int32),
            pltpu.SMEM((NF,), jnp.int32),
            pltpu.VMEM((17, CB, 256), F32),
            pltpu.VMEM((2, 16, 128), F32),
            pltpu.VMEM((16, CB, 256), BF),
            pltpu.VMEM((16, CB, 256), F32),
            pltpu.VMEM((CB, FR), F32),
            pltpu.SemaphoreType.DMA((2,)),
            pltpu.SemaphoreType.DMA((4,)),
        ],
        compiler_params=PARAMS,
        name="slots_to_facet",
    )(offs, order, bp, window(), jnp.asarray(block_table().T, BF))


def swapped(sibling, neighbour):
    n = lax.axis_size("uv")
    near = [(i, i ^ 1) for i in range(n)]
    far = [(i, (i - 1 if i % 2 == 0 else i + 1) % n) for i in range(n)]
    return lax.ppermute(sibling, "uv", near), lax.ppermute(neighbour, "uv", far)


def local(
    sky_image, subgrid_offsets, owner_order, visibility_count, visibility_cell, observed,
    visibility_weight, row_kernel, column_kernel,
):
    obs = observed[0]
    wt = visibility_weight[0]

    out = k1(subgrid_offsets, owner_order, sky_image)
    arrived = lax.all_to_all(out, "facet", split_axis=0, concat_axis=0, tiled=True)
    table, phases, live, there, back, taps = kt(
        subgrid_offsets, owner_order, row_kernel, column_kernel, visibility_count, visibility_cell
    )
    sub, sibling, neighbour = ka(arrived, obs, wt, there, phases)
    sibling, neighbour = swapped(sibling, neighbour)
    res, outgoing = kb(
        taps, sub, obs, wt, sibling, neighbour, back, table, phases, live
    )
    returned = lax.all_to_all(outgoing, "facet", split_axis=0, concat_axis=0, tiled=True)
    dirty = k3(subgrid_offsets, owner_order, returned)
    return (res[None], dirty)


def solution(mesh):
    in_specs = (
        P("uv", "facet"),
        P(),
        P(),
        P("facet"),
        P("facet", None),
        P("facet", None, "uv", None),
        P("facet", "uv", None),
        P(),
        P(),
    )
    out_specs = (P("facet", None, "uv", None), P("uv", "facet"))
    return jax.shard_map(local, mesh=mesh, in_specs=in_specs, out_specs=out_specs, check_vma=False)
```

```python
import math

import jax
import jax.numpy as jnp
import numpy as np
from jax import lax
from jax.experimental import pallas as pl
from jax.experimental.pallas import tpu as pltpu
from jax.sharding import PartitionSpec as P

FR = 2048
XC = 128
SG = 256
NF = 32
CB = 32
CE = 40
TAPS = 7
VM = 512
BF = jnp.bfloat16
F32 = jnp.float32


def block_table():
    lane = np.arange(128)[None, :]
    g = 8 * (lane % 16) + lane // 16
    row = np.arange(128)[:, None] + 64
    a = 2.0 * np.pi * ((g * row) % 128) / 128
    c, s = np.cos(a), np.sin(a)
    return np.block([[c, -s], [s, c]]).astype(np.float32)


def facet_phase():
    f = np.arange(NF)[:, None]
    j = np.arange(128)[None, :]
    a = 2.0 * np.pi * ((j * (2 * f + 1)) % 64) / 64
    return np.stack([np.cos(a), np.sin(a)]).astype(np.float32)


def window():
    r = np.arange(FR)
    return (np.sin((r + 0.5) * np.pi / FR) / math.sqrt(FR)).astype(np.float32)[None, :]


def turn(n):
    q = (n + 256) >> 9
    x = (n - (q << 9)).astype(F32) * (math.pi / 1024.0)
    y = x * x
    c = 1.0 + y * (-0.5 + y * (1.0 / 24 + y * (-1.0 / 720 + y * (1.0 / 40320))))
    s = x * (1.0 + y * (-1.0 / 6 + y * (1.0 / 120 + y * (-1.0 / 5040 + y * (1.0 / 362880)))))
    odd = (q & 1) == 1
    cos = jnp.where(odd, s, c)
    sin = jnp.where(odd, c, s)
    cos = jnp.where(((q + 1) & 2) == 2, -cos, cos)
    sin = jnp.where((q & 2) == 2, -sin, sin)
    return cos, sin


def twiddles(facet):
    m = lax.broadcasted_iota(jnp.int32, (16, 128), 0)
    lane = lax.broadcasted_iota(jnp.int32, (16, 128), 1)
    return turn((m * (lane + 64 + 128 * facet)) & (FR - 1))


def make_window(win_ref):
    for b in range(16):
        r = lax.broadcasted_iota(jnp.int32, (8, 128), 1) + (128 * b)
        x = (r.astype(F32) - 1023.5) * (math.pi / FR)
        y = x * x
        c = 1.0 / 24 + y * (-1.0 / 720 + y * (1.0 / 40320 + y * (-1.0 / 3628800 + y / 479001600)))
        win_ref[:, 128 * b : 128 * (b + 1)] = (1.0 + y * (-0.5 + y * c)) * (1.0 / math.sqrt(FR))


def make_block_table(tab_ref, transposed=False):
    lane = lax.broadcasted_iota(jnp.int32, (128, 128), 0 if transposed else 1)
    row = lax.broadcasted_iota(jnp.int32, (128, 128), 1 if transposed else 0) + 64
    g = 8 * (lane & 15) + (lane >> 4)
    c, s = turn((16 * g * row) & (FR - 1))
    c, s, t = c.astype(BF), s.astype(BF), (-s).astype(BF)
    if transposed:
        s, t = t, s
    tab_ref[0:128, 0:128] = c
    tab_ref[0:128, 128:256] = t
    tab_ref[128:256, 0:128] = s
    tab_ref[128:256, 128:256] = c


def cmul(a, w):
    wr, wi = w
    if abs(wi) < 1e-12:
        return a if abs(wr - 1) < 1e-12 else (a[0] * wr, a[1] * wr)
    if abs(wr) < 1e-12:
        return (-a[1], a[0]) if wi > 0 else (a[1], -a[0])
    return (a[0] * wr - a[1] * wi, a[0] * wi + a[1] * wr)


def real_transform(x):
    n = len(x)
    if n == 2:
        zero = jnp.zeros_like(x[0])
        return [(x[0] + x[1], zero), (x[0] - x[1], zero)]
    even, odd = real_transform(x[::2]), real_transform(x[1::2])
    out = [None] * (n // 2 + 1)
    for k in range(n // 4 + 1):
        a = 2.0 * math.pi * k / n
        o = cmul(odd[k], (math.cos(a), -math.sin(a)))
        e = even[k]
        out[k] = (e[0] + o[0], e[1] + o[1])
        if k != n // 2 - k:
            out[n // 2 - k] = (e[0] - o[0], o[1] - e[1])
    return out


def real_inverse(h):
    n = 2 * (len(h) - 1)
    if n == 2:
        return [h[0][0] + h[1][0], h[0][0] - h[1][0]]
    even, odd = [], []
    for k in range(n // 4 + 1):
        a, b = h[k], h[n // 2 - k]
        t = 2.0 * math.pi * k / n
        even.append((a[0] + b[0], a[1] - b[1]))
        odd.append(cmul((a[0] - b[0], a[1] + b[1]), (math.cos(t), math.sin(t))))
    even, odd = real_inverse(even), real_inverse(odd)
    return [v for pair in zip(even, odd) for v in pair]


def lanes_of(shape):
    return lax.broadcasted_iota(jnp.int32, shape, 1).astype(F32).astype(BF)


def swap_index(x):
    lane = lax.broadcasted_iota(jnp.int32, x[0].shape, 1)
    for bit in (1, 2, 4, 8):
        high = (lane & bit).astype(F32).astype(BF) > 0
        y = list(x)
        for i in range(16):
            if i & bit:
                continue
            y[i] = jnp.where(high, pltpu.roll(x[i + bit], bit, 1), x[i])
            y[i + bit] = jnp.where(high, x[i + bit], pltpu.roll(x[i], 128 - bit, 1))
        x = y
    return x


def halo_rows(after, before, axis):
    row = lax.broadcasted_iota(jnp.int32, after.shape, axis)
    return jnp.where(row < 3, after, jnp.where(row >= 5, before, jnp.zeros_like(after)))


def k1_body(
    offs_hbm, order_hbm, sky_hbm,
    out_hbm, offs_ref, order_ref, tw_ref, lhs_ref, u_ref, nat_ref, sky_ref, win_ref, tab_ref,
    out_ref, sky_sem, small_sem, out_sem,
):
    halves = [
        pltpu.make_async_copy(
            sky_hbm.at[pl.ds(16 * g, 16), :], sky_ref.at[pl.ds(16 * g, 16), :], sky_sem.at[g]
        )
        for g in range(2)
    ]
    small = [
        pltpu.make_async_copy(offs_hbm, offs_ref, small_sem.at[0]),
        pltpu.make_async_copy(order_hbm, order_ref, small_sem.at[1]),
    ]
    for copy in halves + small:
        copy.start()
    tw_ref[0], tw_ref[1] = twiddles(lax.axis_index("facet"))
    make_window(win_ref)
    make_block_table(tab_ref)
    for g in range(2):
        halves[g].wait()
        rows = slice(16 * g, 16 * (g + 1))
        x = []
        for b in range(16):
            lanes = slice(128 * b, 128 * (b + 1))
            x.append(sky_ref[rows, lanes].astype(F32) * win_ref[0:1, lanes])
        a = real_transform(x)
        for m in range(16):
            ar, ai = a[m] if m <= 8 else (a[16 - m][0], -a[16 - m][1])
            c, s = tw_ref[0, m : m + 1, :], tw_ref[1, m : m + 1, :]
            lhs_ref[m, rows, 0:128] = (ar * c + ai * s).astype(BF)
            lhs_ref[m, rows, 128:256] = (ai * c - ar * s).astype(BF)
    u = jnp.dot(lhs_ref[...].reshape(16 * CB, 256), tab_ref[...], preferred_element_type=F32)
    u_ref[...] = u.astype(BF).reshape(16, CB, 256)

    for g in range(2):
        rows = slice(16 * g, 16 * (g + 1))
        for p in range(2):
            cols = slice(128 * p, 128 * (p + 1))
            x = swap_index([u_ref[m, rows, cols] for m in range(16)])
            for b in range(16):
                nat_ref[b, rows, cols] = x[b]
            nat_ref[16, rows, cols] = x[0]

    for copy in small:
        copy.wait()
    lane = lanes_of((CB, 128))
    done = []
    for i in range(NF):
        off = offs_ref[order_ref[i]]
        b, s = off >> 7, off & 127
        keep = lane >= s.astype(F32).astype(BF)
        for p in range(2):
            cols = slice(128 * p, 128 * (p + 1))
            out_ref[i, :, cols] = jnp.where(keep, nat_ref[b, :, cols], nat_ref[b + 1, :, cols])
        if i % 8 == 7:
            part = pl.ds(i - 7, 8)
            copy = pltpu.make_async_copy(out_ref.at[part], out_hbm.at[part], out_sem.at[i // 8])
            copy.start()
            done.append(copy)
    for copy in done:
        copy.wait()


SMEM = pl.BlockSpec(memory_space=pltpu.SMEM)
VMEM = pl.BlockSpec(memory_space=pltpu.VMEM)
ANY = pl.BlockSpec(memory_space=pl.ANY)
PARAMS = pltpu.CompilerParams(vmem_limit_bytes=24 * 1024 * 1024)


def k1(offs, order, sky):
    return pl.pallas_call(
        k1_body,
        out_shape=jax.ShapeDtypeStruct((NF, CB, 2 * XC), BF),
        in_specs=[ANY] * 3,
        out_specs=ANY,
        scratch_shapes=[
            pltpu.SMEM((NF,), jnp.int32),
            pltpu.SMEM((NF,), jnp.int32),
            pltpu.VMEM((2, 16, 128), F32),
            pltpu.VMEM((16, CB, 256), BF),
            pltpu.VMEM((16, CB, 256), BF),
            pltpu.VMEM((17, CB, 256), BF),
            pltpu.VMEM((CB, FR), BF),
            pltpu.VMEM((8, FR), F32),
            pltpu.VMEM((256, 256), BF),
            pltpu.VMEM((NF, CB, 256), BF),
            pltpu.SemaphoreType.DMA((2,)),
            pltpu.SemaphoreType.DMA((2,)),
            pltpu.SemaphoreType.DMA((4,)),
        ],
        name="facet_to_slots",
    )(offs, order, sky)


def kt_body(
    offs_ref, order_ref, rk_ref, ck_ref, count_ref, cell_ref, ph_ref, obs_ref, wt_ref,
    dt_ref, pho_ref, live_ref, w_ref, back_ref, taps_ref, offset_ref,
    sibling_ref, neighbour_ref,
):
    off = offs_ref[order_ref[lax.axis_index("facet")]]
    back = (128 - 2 * off) & 127
    pho_ref[0] = pltpu.roll(ph_ref[0], back, 1)
    pho_ref[1] = pltpu.roll(ph_ref[1], back, 1)
    even = lax.rem(lax.axis_index("uv"), 2) == 0
    for p in range(3):
        edges = obs_ref[p].astype(F32) if p < 2 else wt_ref[...]
        first, last = edges[0:8], edges[24:32]
        sibling_ref[:, p * VM : (p + 1) * VM] = jnp.where(even, last, first).astype(BF)
        neighbour_ref[:, p * VM : (p + 1) * VM] = jnp.where(even, first, last).astype(BF)
    lane = lax.broadcasted_iota(jnp.int32, (8, 128), 1)
    offsets = jnp.zeros((8, 128), jnp.int32)
    for i in range(NF):
        offsets = jnp.where(lane == i, offs_ref[order_ref[i]], offsets)
    offset_ref[...] = offsets
    d = lax.broadcasted_iota(jnp.int32, (SG, VM), 0) - cell_ref[...] + 3
    m = jnp.zeros((SG, VM), F32)
    for t in range(TAPS):
        m = jnp.where(d == t, rk_ref[t], m)
        taps_ref[t : t + 1, :] = jnp.full((1, SG), ck_ref[t], F32)
    taps_ref[TAPS : TAPS + 1, :] = jnp.zeros((1, SG), F32)
    dt_ref[...] = m.astype(BF)
    live_ref[...] = (lax.broadcasted_iota(jnp.int32, (1, VM), 1) < count_ref[0]).astype(F32)
    for ref, shape, axis in ((w_ref, (XC, SG), 0), (back_ref, (SG, XC), 1)):
        k = (lax.broadcasted_iota(jnp.int32, shape, axis) - off) & (XC - 1)
        j = lax.broadcasted_iota(jnp.int32, shape, 1 - axis)
        c, s = turn((8 * j * k) & (FR - 1))
        c, s, t = (x.astype(BF) for x in (c * (1 / 64), s * (1 / 64), s * (-1 / 64)))
        rows, cols = shape
        ref[0:rows, 0:cols] = c
        ref[rows:, cols:] = c
        ref[0:rows, cols:] = s if axis == 0 else t
        ref[rows:, 0:cols] = t if axis == 0 else s


def kt(offs, order, rk, ck, count, cell, obs, wt):
    return pl.pallas_call(
        kt_body,
        out_shape=(
            jax.ShapeDtypeStruct((SG, VM), BF),
            jax.ShapeDtypeStruct((2, NF, 128), F32),
            jax.ShapeDtypeStruct((1, VM), F32),
            jax.ShapeDtypeStruct((2 * XC, 2 * SG), BF),
            jax.ShapeDtypeStruct((2 * SG, 2 * XC), BF),
            jax.ShapeDtypeStruct((8, SG), F32),
            jax.ShapeDtypeStruct((8, 128), jnp.int32),
            jax.ShapeDtypeStruct((8, EDGE), BF),
            jax.ShapeDtypeStruct((8, EDGE), BF),
        ),
        in_specs=[SMEM] * 5 + [VMEM] * 4,
        out_specs=(VMEM,) * 9,
        compiler_params=PARAMS,
        cost_estimate=pl.CostEstimate(flops=4000000, bytes_accessed=1000000, transcendentals=0),
        name="slot_tables",
    )(offs, order, rk, ck, count, cell, facet_phase(), obs, wt)


def ka_body(
    arr_ref, w_ref, pho_ref,
    sub_ref, sibling_ref, neighbour_ref, u_ref,
):
    u = jnp.dot(arr_ref[...].reshape(NF * CB, 256), w_ref[...], preferred_element_type=F32)
    u_ref[...] = u.reshape(NF, CB, 2 * SG)
    for h in range(2):
        re = jnp.zeros((CB, 128), F32)
        im = jnp.zeros((CB, 128), F32)
        for f in range(NF):
            ur = u_ref[f, :, 128 * h : 128 * (h + 1)]
            ui = u_ref[f, :, SG + 128 * h : SG + 128 * (h + 1)]
            pc = pho_ref[0, f : f + 1, :]
            ps = pho_ref[1, f : f + 1, :]
            re = re + (ur * pc - ui * ps)
            im = im + (ur * ps + ui * pc)
        sub_ref[:, 128 * h : 128 * (h + 1)] = re
        sub_ref[:, SG + 128 * h : SG + 128 * (h + 1)] = im
    even = lax.rem(lax.axis_index("uv"), 2) == 0
    first, last = sub_ref[0:8, :], sub_ref[24:32, :]
    sibling_ref[...] = jnp.where(even, last, first).astype(BF)
    neighbour_ref[...] = jnp.where(even, first, last).astype(BF)


EDGE = 3 * VM


def ka(arrived, table, phases):
    return pl.pallas_call(
        ka_body,
        out_shape=(
            jax.ShapeDtypeStruct((CB, 2 * SG), F32),
            jax.ShapeDtypeStruct((8, 2 * SG), BF),
            jax.ShapeDtypeStruct((8, 2 * SG), BF),
        ),
        in_specs=[VMEM] * 3,
        out_specs=(VMEM, VMEM, VMEM),
        scratch_shapes=[pltpu.VMEM((NF, CB, 2 * SG), F32)],
        compiler_params=PARAMS,
        name="sum_facets",
    )(arrived, table, phases)


def kb_body(
    taps_ref, sub_ref, obs_ref, wt_ref, sibling_ref, neighbour_ref, wt_tab_ref, dt_ref, pho_ref,
    live_ref, sibling_vis_ref, neighbour_vis_ref,
    res_hbm, out_ref, sub_ext_ref, conv_ref, res_ref, ext_ref, back_ref, y_ref, sem,
):
    uv = lax.axis_index("uv")
    even = lax.rem(uv, 2) == 0
    in_before, in_after = uv > 0, uv < 7

    def sides(s, n):
        s, n = s.astype(F32), n.astype(F32)
        before = jnp.where(in_before, jnp.where(even, n, s), 0.0)
        after = jnp.where(in_after, jnp.where(even, s, n), 0.0)
        return before, after

    before, after = sides(sibling_ref[...], neighbour_ref[...])
    sub_ext_ref[8:16, :] = before
    sub_ext_ref[16:48, :] = sub_ref[...]
    sub_ext_ref[48:56, :] = after
    for p in range(2):
        lanes = slice(SG * p, SG * (p + 1))
        own = jnp.zeros((CB, SG), F32)
        lo = jnp.zeros((8, SG), F32)
        hi = jnp.zeros((8, SG), F32)
        for t in range(TAPS):
            k = taps_ref[t : t + 1, :]
            own = own + k * sub_ext_ref[13 + t : 45 + t, lanes]
            lo = lo + k * sub_ext_ref[5 + t : 13 + t, lanes]
            hi = hi + k * sub_ext_ref[45 + t : 53 + t, lanes]
        conv_ref[p * CE : p * CE + CB, :] = own
        conv_ref[p * CE + CB : (p + 1) * CE, :] = halo_rows(hi, lo, 0)
    model = jnp.dot(conv_ref[...].astype(BF), dt_ref[...], preferred_element_type=F32)

    live = live_ref[...]
    wt = wt_ref[...] * live
    cols = slice(2 * VM, EDGE)
    before, after = sides(sibling_vis_ref[:, cols], neighbour_vis_ref[:, cols])
    wt_h = halo_rows(after, before, 0) * live
    parts = []
    for p in range(2):
        own = wt * (obs_ref[p].astype(F32) - model[p * CE : p * CE + CB])
        res_ref[p] = own
        cols = slice(p * VM, (p + 1) * VM)
        before, after = sides(sibling_vis_ref[:, cols], neighbour_vis_ref[:, cols])
        obs_h = halo_rows(after, before, 0)
        parts += [own, wt_h * (obs_h - model[p * CE + CB : (p + 1) * CE])]
    copy = pltpu.make_async_copy(res_ref, res_hbm, sem)
    copy.start()
    rr = jnp.concatenate(parts, axis=0).astype(BF)
    gridded = lax.dot_general(
        rr, dt_ref[...], (((1,), (1,)), ((), ())), preferred_element_type=F32
    )
    for p in range(2):
        halo = gridded[p * CE + CB : (p + 1) * CE]
        ext_ref[p, 0:8, :] = halo
        ext_ref[p, 8:40, :] = gridded[p * CE : p * CE + CB]
        ext_ref[p, 40:48, :] = halo
        b = jnp.zeros((CB, SG), F32)
        for t in range(TAPS):
            b = b + taps_ref[t : t + 1, :] * ext_ref[p, 11 - t : 43 - t, :]
        back_ref[p] = b
    for h in range(2):
        lanes = slice(128 * h, 128 * (h + 1))
        xr, xi = back_ref[0, :, lanes], back_ref[1, :, lanes]
        for f in range(NF):
            pc = pho_ref[0, f : f + 1, :]
            ps = pho_ref[1, f : f + 1, :]
            y_ref[f, :, lanes] = (xr * pc + xi * ps).astype(BF)
            y_ref[f, :, SG + 128 * h : SG + 128 * (h + 1)] = (xi * pc - xr * ps).astype(BF)
    z = jnp.dot(y_ref[...].reshape(NF * CB, 2 * SG), wt_tab_ref[...], preferred_element_type=F32)
    out_ref[...] = z.astype(BF).reshape(NF, CB, 2 * XC)
    copy.wait()


def kb(taps, sub, obs, wt, sibling, neighbour, back, table, phases, live, *edges):
    return pl.pallas_call(
        kb_body,
        out_shape=(
            jax.ShapeDtypeStruct((2, CB, VM), F32),
            jax.ShapeDtypeStruct((NF, CB, 2 * XC), BF),
        ),
        in_specs=[VMEM] * 12,
        out_specs=(ANY, VMEM),
        scratch_shapes=[
            pltpu.VMEM((64, 2 * SG), F32),
            pltpu.VMEM((2 * CE, SG), F32),
            pltpu.VMEM((2, CB, VM), F32),
            pltpu.VMEM((2, 48, SG), F32),
            pltpu.VMEM((2, CB, SG), F32),
            pltpu.VMEM((NF, CB, 2 * SG), BF),
            pltpu.SemaphoreType.DMA,
        ],
        compiler_params=PARAMS,
        name="slot_round_trip",
    )(
        taps, sub, obs, wt, sibling, neighbour, back, table, phases, live, *edges
    )


def k3_body(
    offset_ref, bp_ref, win_ref, tab_ref,
    out_hbm, nat_ref, tw_ref, lhs_ref, v_ref, out_ref, sem,
):
    offsets = offset_ref[...]
    tw_ref[0], tw_ref[1] = twiddles(lax.axis_index("facet"))
    nat_ref[...] = jnp.zeros_like(nat_ref)
    lane = lax.broadcasted_iota(jnp.int32, (CB, 128), 1)
    for i in range(NF):
        off = offsets[0, i]
        b, s = off >> 7, off & 127
        keep = lane >= s
        for p in range(2):
            cols = slice(128 * p, 128 * (p + 1))
            x = bp_ref[i, :, cols].astype(F32)
            nat_ref[b, :, cols] += jnp.where(keep, x, 0.0)
            nat_ref[b + 1, :, cols] += jnp.where(keep, 0.0, x)
    nat_ref[0] += nat_ref[16]

    for g in range(2):
        rows = slice(16 * g, 16 * (g + 1))
        for p in range(2):
            cols = slice(128 * p, 128 * (p + 1))
            x = swap_index([nat_ref[b, rows, cols].astype(BF) for b in range(16)])
            for m in range(16):
                lhs_ref[m, rows, cols] = x[m]
    v = jnp.dot(lhs_ref[...].reshape(16 * CB, 256), tab_ref[...], preferred_element_type=F32)
    v_ref[...] = v.reshape(16, CB, 256)
    done = []
    for g in range(4):
        rows = slice(8 * g, 8 * (g + 1))
        t = []
        for m in range(16):
            vr, vi = v_ref[m, rows, 0:128], v_ref[m, rows, 128:256]
            c, s = tw_ref[0, m : m + 1, :], tw_ref[1, m : m + 1, :]
            t.append((vr * c - vi * s, vr * s + vi * c))
        h = [(t[m][0] + t[-m % 16][0], t[m][1] - t[-m % 16][1]) for m in range(9)]
        x = real_inverse(h)
        for b in range(16):
            lanes = slice(128 * b, 128 * (b + 1))
            out_ref[rows, lanes] = x[b] * (0.5 * win_ref[:, lanes])
        part = pl.ds(8 * g, 8)
        copy = pltpu.make_async_copy(out_ref.at[part, :], out_hbm.at[part, :], sem.at[g])
        copy.start()
        done.append(copy)
    for copy in done:
        copy.wait()


def k3(offsets, bp):
    return pl.pallas_call(
        k3_body,
        out_shape=jax.ShapeDtypeStruct((CB, FR), F32),
        in_specs=[VMEM] * 4,
        out_specs=ANY,
        scratch_shapes=[
            pltpu.VMEM((17, CB, 256), F32),
            pltpu.VMEM((2, 16, 128), F32),
            pltpu.VMEM((16, CB, 256), BF),
            pltpu.VMEM((16, CB, 256), F32),
            pltpu.VMEM((CB, FR), F32),
            pltpu.SemaphoreType.DMA((4,)),
        ],
        compiler_params=PARAMS,
        name="slots_to_facet",
    )(offsets, bp, window(), jnp.asarray(block_table().T, BF))


def swapped(sibling, neighbour):
    n = lax.axis_size("uv")
    near = [(i, i ^ 1) for i in range(n)]
    far = [(i, (i - 1 if i % 2 == 0 else i + 1) % n) for i in range(n)]
    return lax.ppermute(sibling, "uv", near), lax.ppermute(neighbour, "uv", far)


def local(
    sky_image, subgrid_offsets, owner_order, visibility_count, visibility_cell, observed,
    visibility_weight, row_kernel, column_kernel,
):
    obs = observed[0]
    wt = visibility_weight[0]

    out = k1(subgrid_offsets, owner_order, sky_image)
    arrived = lax.all_to_all(out, "facet", split_axis=0, concat_axis=0, tiled=True)
    table, phases, live, there, back, taps, offsets, *edges = kt(
        subgrid_offsets, owner_order, row_kernel, column_kernel, visibility_count,
        visibility_cell, obs, wt,
    )
    edges = swapped(*edges)
    sub, sibling, neighbour = ka(arrived, there, phases)
    sibling, neighbour = swapped(sibling, neighbour)
    res, outgoing = kb(
        taps, sub, obs, wt, sibling, neighbour, back, table, phases, live, *edges
    )
    returned = lax.all_to_all(outgoing, "facet", split_axis=0, concat_axis=0, tiled=True)
    dirty = k3(offsets, returned)
    return (res[None], dirty)


def solution(mesh):
    in_specs = (
        P("uv", "facet"),
        P(),
        P(),
        P("facet"),
        P("facet", None),
        P("facet", None, "uv", None),
        P("facet", "uv", None),
        P(),
        P(),
    )
    out_specs = (P("facet", None, "uv", None), P("uv", "facet"))
    return jax.shard_map(local, mesh=mesh, in_specs=in_specs, out_specs=out_specs, check_vma=False)
```

```python
import math

import jax
import jax.numpy as jnp
import numpy as np
from jax import lax
from jax.experimental import pallas as pl
from jax.experimental.pallas import tpu as pltpu
from jax.sharding import PartitionSpec as P

FR = 2048
XC = 128
SG = 256
NF = 32
CB = 32
CE = 40
TAPS = 7
VM = 512
BF = jnp.bfloat16
F32 = jnp.float32


def block_table():
    lane = np.arange(128)[None, :]
    g = 8 * (lane % 16) + lane // 16
    row = np.arange(128)[:, None] + 64
    a = 2.0 * np.pi * ((g * row) % 128) / 128
    c, s = np.cos(a), np.sin(a)
    return np.block([[c, -s], [s, c]]).astype(np.float32)


def facet_phase():
    f = np.arange(NF)[:, None]
    j = np.arange(128)[None, :]
    a = 2.0 * np.pi * ((j * (2 * f + 1)) % 64) / 64
    return np.stack([np.cos(a), np.sin(a)]).astype(np.float32)


def window():
    r = np.arange(FR)
    return (np.sin((r + 0.5) * np.pi / FR) / math.sqrt(FR)).astype(np.float32)[None, :]


def turn(n):
    q = (n + 256) >> 9
    x = (n - (q << 9)).astype(F32) * (math.pi / 1024.0)
    y = x * x
    c = 1.0 + y * (-0.5 + y * (1.0 / 24 + y * (-1.0 / 720 + y * (1.0 / 40320))))
    s = x * (1.0 + y * (-1.0 / 6 + y * (1.0 / 120 + y * (-1.0 / 5040 + y * (1.0 / 362880)))))
    odd = (q & 1) == 1
    cos = jnp.where(odd, s, c)
    sin = jnp.where(odd, c, s)
    cos = jnp.where(((q + 1) & 2) == 2, -cos, cos)
    sin = jnp.where((q & 2) == 2, -sin, sin)
    return cos, sin


def twiddles(facet):
    m = lax.broadcasted_iota(jnp.int32, (16, 128), 0)
    lane = lax.broadcasted_iota(jnp.int32, (16, 128), 1)
    return turn((m * (lane + 64 + 128 * facet)) & (FR - 1))


def make_window(win_ref):
    for b in range(16):
        r = lax.broadcasted_iota(jnp.int32, (8, 128), 1) + (128 * b)
        x = (r.astype(F32) - 1023.5) * (math.pi / FR)
        y = x * x
        c = 1.0 / 24 + y * (-1.0 / 720 + y * (1.0 / 40320 + y * (-1.0 / 3628800 + y / 479001600)))
        win_ref[:, 128 * b : 128 * (b + 1)] = (1.0 + y * (-0.5 + y * c)) * (1.0 / math.sqrt(FR))


def make_block_table(tab_ref, transposed=False):
    lane = lax.broadcasted_iota(jnp.int32, (128, 128), 0 if transposed else 1)
    row = lax.broadcasted_iota(jnp.int32, (128, 128), 1 if transposed else 0) + 64
    g = 8 * (lane & 15) + (lane >> 4)
    c, s = turn((16 * g * row) & (FR - 1))
    c, s, t = c.astype(BF), s.astype(BF), (-s).astype(BF)
    if transposed:
        s, t = t, s
    tab_ref[0:128, 0:128] = c
    tab_ref[0:128, 128:256] = t
    tab_ref[128:256, 0:128] = s
    tab_ref[128:256, 128:256] = c


def cmul(a, w):
    wr, wi = w
    if abs(wi) < 1e-12:
        return a if abs(wr - 1) < 1e-12 else (a[0] * wr, a[1] * wr)
    if abs(wr) < 1e-12:
        return (-a[1], a[0]) if wi > 0 else (a[1], -a[0])
    return (a[0] * wr - a[1] * wi, a[0] * wi + a[1] * wr)


def real_transform(x):
    n = len(x)
    if n == 2:
        zero = jnp.zeros_like(x[0])
        return [(x[0] + x[1], zero), (x[0] - x[1], zero)]
    even, odd = real_transform(x[::2]), real_transform(x[1::2])
    out = [None] * (n // 2 + 1)
    for k in range(n // 4 + 1):
        a = 2.0 * math.pi * k / n
        o = cmul(odd[k], (math.cos(a), -math.sin(a)))
        e = even[k]
        out[k] = (e[0] + o[0], e[1] + o[1])
        if k != n // 2 - k:
            out[n // 2 - k] = (e[0] - o[0], o[1] - e[1])
    return out


def real_inverse(h):
    n = 2 * (len(h) - 1)
    if n == 2:
        return [h[0][0] + h[1][0], h[0][0] - h[1][0]]
    even, odd = [], []
    for k in range(n // 4 + 1):
        a, b = h[k], h[n // 2 - k]
        t = 2.0 * math.pi * k / n
        even.append((a[0] + b[0], a[1] - b[1]))
        odd.append(cmul((a[0] - b[0], a[1] + b[1]), (math.cos(t), math.sin(t))))
    even, odd = real_inverse(even), real_inverse(odd)
    return [v for pair in zip(even, odd) for v in pair]


def lanes_of(shape):
    return lax.broadcasted_iota(jnp.int32, shape, 1).astype(F32).astype(BF)


def swap_index(x):
    lane = lax.broadcasted_iota(jnp.int32, x[0].shape, 1)
    for bit in (1, 2, 4, 8):
        high = (lane & bit).astype(F32).astype(BF) > 0
        y = list(x)
        for i in range(16):
            if i & bit:
                continue
            y[i] = jnp.where(high, pltpu.roll(x[i + bit], bit, 1), x[i])
            y[i + bit] = jnp.where(high, x[i + bit], pltpu.roll(x[i], 128 - bit, 1))
        x = y
    return x


def halo_rows(after, before, axis):
    row = lax.broadcasted_iota(jnp.int32, after.shape, axis)
    return jnp.where(row < 3, after, jnp.where(row >= 5, before, jnp.zeros_like(after)))


def k1_body(
    offs_hbm, order_hbm, sky_hbm,
    out_hbm, offs_ref, order_ref, tw_ref, lhs_ref, u_ref, nat_ref, sky_ref, win_ref, tab_ref,
    out_ref, sky_sem, small_sem, out_sem,
):
    halves = [
        pltpu.make_async_copy(
            sky_hbm.at[pl.ds(16 * g, 16), :], sky_ref.at[pl.ds(16 * g, 16), :], sky_sem.at[g]
        )
        for g in range(2)
    ]
    small = [
        pltpu.make_async_copy(offs_hbm, offs_ref, small_sem.at[0]),
        pltpu.make_async_copy(order_hbm, order_ref, small_sem.at[1]),
    ]
    for copy in halves + small:
        copy.start()
    tw_ref[0], tw_ref[1] = twiddles(lax.axis_index("facet"))
    make_window(win_ref)
    make_block_table(tab_ref)
    for g in range(2):
        halves[g].wait()
        rows = slice(16 * g, 16 * (g + 1))
        x = []
        for b in range(16):
            lanes = slice(128 * b, 128 * (b + 1))
            x.append(sky_ref[rows, lanes].astype(F32) * win_ref[0:1, lanes])
        a = real_transform(x)
        for m in range(16):
            ar, ai = a[m] if m <= 8 else (a[16 - m][0], -a[16 - m][1])
            c, s = tw_ref[0, m : m + 1, :], tw_ref[1, m : m + 1, :]
            lhs_ref[m, rows, 0:128] = (ar * c + ai * s).astype(BF)
            lhs_ref[m, rows, 128:256] = (ai * c - ar * s).astype(BF)
    u = jnp.dot(lhs_ref[...].reshape(16 * CB, 256), tab_ref[...], preferred_element_type=F32)
    u_ref[...] = u.astype(BF).reshape(16, CB, 256)

    for g in range(2):
        rows = slice(16 * g, 16 * (g + 1))
        for p in range(2):
            cols = slice(128 * p, 128 * (p + 1))
            x = swap_index([u_ref[m, rows, cols] for m in range(16)])
            for b in range(16):
                nat_ref[b, rows, cols] = x[b]
            nat_ref[16, rows, cols] = x[0]

    for copy in small:
        copy.wait()
    lane = lanes_of((CB, 128))
    done = []
    for i in range(NF):
        off = offs_ref[order_ref[i]]
        b, s = off >> 7, off & 127
        keep = lane >= s.astype(F32).astype(BF)
        for p in range(2):
            cols = slice(128 * p, 128 * (p + 1))
            out_ref[i, :, cols] = jnp.where(keep, nat_ref[b, :, cols], nat_ref[b + 1, :, cols])
        if i % 8 == 7:
            part = pl.ds(i - 7, 8)
            copy = pltpu.make_async_copy(out_ref.at[part], out_hbm.at[part], out_sem.at[i // 8])
            copy.start()
            done.append(copy)
    for copy in done:
        copy.wait()


SMEM = pl.BlockSpec(memory_space=pltpu.SMEM)
VMEM = pl.BlockSpec(memory_space=pltpu.VMEM)
ANY = pl.BlockSpec(memory_space=pl.ANY)
PARAMS = pltpu.CompilerParams(vmem_limit_bytes=24 * 1024 * 1024)


def k1(offs, order, sky):
    return pl.pallas_call(
        k1_body,
        out_shape=jax.ShapeDtypeStruct((NF, CB, 2 * XC), BF),
        in_specs=[ANY] * 3,
        out_specs=ANY,
        scratch_shapes=[
            pltpu.SMEM((NF,), jnp.int32),
            pltpu.SMEM((NF,), jnp.int32),
            pltpu.VMEM((2, 16, 128), F32),
            pltpu.VMEM((16, CB, 256), BF),
            pltpu.VMEM((16, CB, 256), BF),
            pltpu.VMEM((17, CB, 256), BF),
            pltpu.VMEM((CB, FR), BF),
            pltpu.VMEM((8, FR), F32),
            pltpu.VMEM((256, 256), BF),
            pltpu.VMEM((NF, CB, 256), BF),
            pltpu.SemaphoreType.DMA((2,)),
            pltpu.SemaphoreType.DMA((2,)),
            pltpu.SemaphoreType.DMA((4,)),
        ],
        name="facet_to_slots",
    )(offs, order, sky)


def kt_body(
    offs_ref, order_ref, rk_ref, ck_ref, count_ref, cell_ref, ph_ref, obs_ref, wt_ref,
    dt_ref, pho_ref, live_ref, w_ref, back_ref, taps_ref, offset_ref,
    sibling_ref, neighbour_ref,
):
    off = offs_ref[order_ref[lax.axis_index("facet")]]
    back = (128 - 2 * off) & 127
    pho_ref[0] = pltpu.roll(ph_ref[0], back, 1)
    pho_ref[1] = pltpu.roll(ph_ref[1], back, 1)
    even = lax.rem(lax.axis_index("uv"), 2) == 0
    for p in range(3):
        edges = obs_ref[p].astype(F32) if p < 2 else wt_ref[...]
        first, last = edges[0:8], edges[24:32]
        sibling_ref[:, p * VM : (p + 1) * VM] = jnp.where(even, last, first).astype(BF)
        neighbour_ref[:, p * VM : (p + 1) * VM] = jnp.where(even, first, last).astype(BF)
    lane = lax.broadcasted_iota(jnp.int32, (8, 128), 1)
    offsets = jnp.zeros((8, 128), jnp.int32)
    for i in range(NF):
        offsets = jnp.where(lane == i, offs_ref[order_ref[i]], offsets)
    offset_ref[...] = offsets
    d = lax.broadcasted_iota(jnp.int32, (SG, VM), 0) - cell_ref[...] + 3
    m = jnp.zeros((SG, VM), F32)
    for t in range(TAPS):
        m = jnp.where(d == t, rk_ref[t], m)
        taps_ref[t : t + 1, :] = jnp.full((1, SG), ck_ref[t], F32)
    taps_ref[TAPS : TAPS + 1, :] = jnp.zeros((1, SG), F32)
    dt_ref[...] = m.astype(BF)
    live_ref[...] = (lax.broadcasted_iota(jnp.int32, (1, VM), 1) < count_ref[0]).astype(F32)
    for ref, shape, axis in ((w_ref, (XC, SG), 0), (back_ref, (SG, XC), 1)):
        k = (lax.broadcasted_iota(jnp.int32, shape, axis) - off) & (XC - 1)
        j = lax.broadcasted_iota(jnp.int32, shape, 1 - axis)
        c, s = turn((8 * j * k) & (FR - 1))
        c, s, t = (x.astype(BF) for x in (c * (1 / 64), s * (1 / 64), s * (-1 / 64)))
        rows, cols = shape
        ref[0:rows, 0:cols] = c
        ref[rows:, cols:] = c
        ref[0:rows, cols:] = s if axis == 0 else t
        ref[rows:, 0:cols] = t if axis == 0 else s


def kt(offs, order, rk, ck, count, cell, obs, wt):
    return pl.pallas_call(
        kt_body,
        out_shape=(
            jax.ShapeDtypeStruct((SG, VM), BF),
            jax.ShapeDtypeStruct((2, NF, 128), F32),
            jax.ShapeDtypeStruct((1, VM), F32),
            jax.ShapeDtypeStruct((2 * XC, 2 * SG), BF),
            jax.ShapeDtypeStruct((2 * SG, 2 * XC), BF),
            jax.ShapeDtypeStruct((8, SG), F32),
            jax.ShapeDtypeStruct((8, 128), jnp.int32),
            jax.ShapeDtypeStruct((8, EDGE), BF),
            jax.ShapeDtypeStruct((8, EDGE), BF),
        ),
        in_specs=[SMEM] * 5 + [VMEM] * 4,
        out_specs=(VMEM,) * 9,
        compiler_params=PARAMS,
        cost_estimate=pl.CostEstimate(flops=4000000, bytes_accessed=1000000, transcendentals=0),
        name="slot_tables",
    )(offs, order, rk, ck, count, cell, facet_phase(), obs, wt)


def facet_sum(arr, w_ref, pho_ref, u_ref, out_ref):
    u = jnp.dot(arr.reshape(NF * 16, 256), w_ref[...], preferred_element_type=F32)
    u_ref[...] = u.reshape(NF, 16, 2 * SG)
    for h in range(2):
        re = jnp.zeros((16, 128), F32)
        im = jnp.zeros((16, 128), F32)
        for f in range(NF):
            ur = u_ref[f, :, 128 * h : 128 * (h + 1)]
            ui = u_ref[f, :, SG + 128 * h : SG + 128 * (h + 1)]
            pc = pho_ref[0, f : f + 1, :]
            ps = pho_ref[1, f : f + 1, :]
            re = re + (ur * pc - ui * ps)
            im = im + (ur * ps + ui * pc)
        out_ref[:, 128 * h : 128 * (h + 1)] = re
        out_ref[:, SG + 128 * h : SG + 128 * (h + 1)] = im


def project(back_ref, pho_ref, table_ref, y_ref):
    for h in range(2):
        lanes = slice(128 * h, 128 * (h + 1))
        xr, xi = back_ref[0, :, lanes], back_ref[1, :, lanes]
        for f in range(NF):
            pc = pho_ref[0, f : f + 1, :]
            ps = pho_ref[1, f : f + 1, :]
            y_ref[f, :, lanes] = (xr * pc + xi * ps).astype(BF)
            y_ref[f, :, SG + 128 * h : SG + 128 * (h + 1)] = (xi * pc - xr * ps).astype(BF)
    z = jnp.dot(y_ref[...].reshape(NF * 16, 2 * SG), table_ref[...], preferred_element_type=F32)
    return z.astype(BF).reshape(NF, 16, 2 * XC)


def ka_body(arr_ref, w_ref, pho_ref, edge_ref, sibling_ref, neighbour_ref, u_ref):
    arr = jnp.concatenate([arr_ref[:, 0:8, :], arr_ref[:, 24:32, :]], axis=1)
    facet_sum(arr, w_ref, pho_ref, u_ref, edge_ref)
    even = lax.rem(lax.axis_index("uv"), 2) == 0
    first, last = edge_ref[0:8, :], edge_ref[8:16, :]
    sibling_ref[...] = jnp.where(even, last, first).astype(BF)
    neighbour_ref[...] = jnp.where(even, first, last).astype(BF)


EDGE = 3 * VM


def ka(arrived, table, phases):
    return pl.pallas_call(
        ka_body,
        out_shape=(
            jax.ShapeDtypeStruct((16, 2 * SG), F32),
            jax.ShapeDtypeStruct((8, 2 * SG), BF),
            jax.ShapeDtypeStruct((8, 2 * SG), BF),
        ),
        in_specs=[VMEM] * 3,
        out_specs=(VMEM, VMEM, VMEM),
        scratch_shapes=[pltpu.VMEM((NF, 16, 2 * SG), F32)],
        compiler_params=PARAMS,
        name="sum_edges",
    )(arrived, table, phases)


def sides(s, n):
    uv = lax.axis_index("uv")
    even = lax.rem(uv, 2) == 0
    s, n = s.astype(F32), n.astype(F32)
    before = jnp.where(uv > 0, jnp.where(even, n, s), 0.0)
    after = jnp.where(uv < 7, jnp.where(even, s, n), 0.0)
    return before, after


def km_body(
    arr_ref, w_ref, pho_ref, edge_ref, taps_ref, dt_ref, live_ref, obs_ref, wt_ref, back_tab_ref,
    sibling_vis_ref, neighbour_vis_ref,
    mid_ref, vis_ref, res_ref, out_ref, u_ref, s_ref, c_ref, g_ref, back_ref, y_ref, v_ref,
):
    facet_sum(arr_ref[:, 8:24, :], w_ref, pho_ref, u_ref, mid_ref)
    s_ref[0:8, :] = jnp.zeros((8, 2 * SG), F32)
    s_ref[8:16, :] = edge_ref[0:8, :]
    s_ref[16:32, :] = mid_ref[...]
    s_ref[32:40, :] = edge_ref[8:16, :]
    s_ref[40:48, :] = jnp.zeros((8, 2 * SG), F32)
    for p in range(2):
        c = jnp.zeros((CB, SG), F32)
        for t in range(TAPS):
            c = c + taps_ref[t : t + 1, :] * s_ref[5 + t : 37 + t, SG * p : SG * (p + 1)]
        c_ref[p * CB : (p + 1) * CB, :] = c
    model = jnp.dot(c_ref[...].astype(BF), dt_ref[...], preferred_element_type=F32)
    wt = wt_ref[...] * live_ref[...]
    parts = []
    for p in range(2):
        r = wt * (obs_ref[p].astype(F32) - model[p * CB : (p + 1) * CB])
        res_ref[p] = r[8:24]
        parts.append(r)
    rr = jnp.concatenate(parts, axis=0).astype(BF)
    g_ref[...] = lax.dot_general(
        rr, dt_ref[...], (((1,), (1,)), ((), ())), preferred_element_type=F32
    )
    for p in range(2):
        b = jnp.zeros((16, SG), F32)
        for t in range(TAPS):
            first = p * CB + 11 - t
            b = b + taps_ref[t : t + 1, :] * g_ref[first : first + 16, :]
        back_ref[p] = b
    out_ref[...] = project(back_ref, pho_ref, back_tab_ref, y_ref)
    for p in range(3):
        cols = slice(p * VM, (p + 1) * VM)
        before, after = sides(sibling_vis_ref[:, cols], neighbour_vis_ref[:, cols])
        own = obs_ref[p].astype(F32) if p < 2 else wt
        if p == 2:
            before, after = before * live_ref[...], after * live_ref[...]
        v_ref[0:8, :] = before
        v_ref[8:40, :] = own
        v_ref[40:48, :] = after
        vis_ref[p, 0:16, :] = v_ref[4:20, :]
        vis_ref[p, 16:32, :] = v_ref[28:44, :]


def km(arrived, table, phases, edge, taps, grid, live, obs, wt, back, *vis):
    return pl.pallas_call(
        km_body,
        out_shape=(
            jax.ShapeDtypeStruct((16, 2 * SG), F32),
            jax.ShapeDtypeStruct((3, 32, VM), F32),
            jax.ShapeDtypeStruct((2, 16, VM), F32),
            jax.ShapeDtypeStruct((NF, 16, 2 * XC), BF),
        ),
        in_specs=[VMEM] * 12,
        out_specs=(VMEM,) * 4,
        scratch_shapes=[
            pltpu.VMEM((NF, 16, 2 * SG), F32),
            pltpu.VMEM((48, 2 * SG), F32),
            pltpu.VMEM((2 * CB, SG), F32),
            pltpu.VMEM((2 * CB, SG), F32),
            pltpu.VMEM((2, 16, SG), F32),
            pltpu.VMEM((NF, 16, 2 * SG), BF),
            pltpu.VMEM((48, VM), F32),
        ],
        compiler_params=PARAMS,
        cost_estimate=pl.CostEstimate(flops=300000000, bytes_accessed=2000000, transcendentals=0),
        name="inner_columns",
    )(arrived, table, phases, edge, taps, grid, live, obs, wt, back, *vis)


def kb_body(
    taps_ref, edge_ref, mid_ref, vis_ref, sibling_ref, neighbour_ref, back_tab_ref, dt_ref,
    pho_ref, res_mid_ref, out_mid_ref,
    res_hbm, out_ref, s_ref, c_ref, g_ref, res_ref, back_ref, y_ref, sem,
):
    middle = pltpu.make_async_copy(res_mid_ref, res_hbm.at[:, pl.ds(8, 16), :], sem.at[0])
    middle.start()
    before, after = sides(sibling_ref[...], neighbour_ref[...])
    s_ref[0, 0:8, :] = before
    s_ref[0, 8:16, :] = edge_ref[0:8, :]
    s_ref[0, 16:24, :] = mid_ref[0:8, :]
    s_ref[1, 0:8, :] = mid_ref[8:16, :]
    s_ref[1, 8:16, :] = edge_ref[8:16, :]
    s_ref[1, 16:24, :] = after
    for p in range(2):
        for side in range(2):
            c = jnp.zeros((16, SG), F32)
            for t in range(TAPS):
                c = c + taps_ref[t : t + 1, :] * s_ref[side, 1 + t : 17 + t, SG * p : SG * (p + 1)]
            c_ref[32 * p + 16 * side : 32 * p + 16 * (side + 1), :] = c
    model = jnp.dot(c_ref[...].astype(BF), dt_ref[...], preferred_element_type=F32)
    parts = []
    for p in range(2):
        r = vis_ref[2] * (vis_ref[p] - model[32 * p : 32 * (p + 1)])
        res_ref[0, p] = r[4:12]
        res_ref[1, p] = r[20:28]
        parts.append(r)
    copies = [middle]
    for side in range(2):
        copy = pltpu.make_async_copy(
            res_ref.at[side], res_hbm.at[:, pl.ds(24 * side, 8), :], sem.at[1 + side]
        )
        copy.start()
        copies.append(copy)
    rr = jnp.concatenate(parts, axis=0).astype(BF)
    g_ref[...] = lax.dot_general(
        rr, dt_ref[...], (((1,), (1,)), ((), ())), preferred_element_type=F32
    )
    for p in range(2):
        for side in range(2):
            b = jnp.zeros((8, SG), F32)
            for t in range(TAPS):
                first = 32 * p + 16 * side + 7 - t
                b = b + taps_ref[t : t + 1, :] * g_ref[first : first + 8, :]
            back_ref[p, 8 * side : 8 * (side + 1), :] = b
    out_ref[:, 8:24, :] = out_mid_ref[...]
    z = project(back_ref, pho_ref, back_tab_ref, y_ref)
    out_ref[:, 0:8, :] = z[:, 0:8, :]
    out_ref[:, 24:32, :] = z[:, 8:16, :]
    for copy in copies:
        copy.wait()


def kb(taps, edge, mid, vis, sibling, neighbour, back, grid, phases, res_mid, out_mid):
    return pl.pallas_call(
        kb_body,
        out_shape=(
            jax.ShapeDtypeStruct((2, CB, VM), F32),
            jax.ShapeDtypeStruct((NF, CB, 2 * XC), BF),
        ),
        in_specs=[VMEM] * 11,
        out_specs=(ANY, VMEM),
        scratch_shapes=[
            pltpu.VMEM((2, 24, 2 * SG), F32),
            pltpu.VMEM((64, SG), F32),
            pltpu.VMEM((64, SG), F32),
            pltpu.VMEM((2, 2, 8, VM), F32),
            pltpu.VMEM((2, 16, SG), F32),
            pltpu.VMEM((NF, 16, 2 * SG), BF),
            pltpu.SemaphoreType.DMA((3,)),
        ],
        compiler_params=PARAMS,
        name="edge_columns",
    )(taps, edge, mid, vis, sibling, neighbour, back, grid, phases, res_mid, out_mid)


def k3_body(
    offset_ref, bp_ref, win_ref, tab_ref,
    out_hbm, nat_ref, tw_ref, lhs_ref, v_ref, out_ref, sem,
):
    offsets = offset_ref[...]
    tw_ref[0], tw_ref[1] = twiddles(lax.axis_index("facet"))
    nat_ref[...] = jnp.zeros_like(nat_ref)
    lane = lax.broadcasted_iota(jnp.int32, (CB, 128), 1)
    for i in range(NF):
        off = offsets[0, i]
        b, s = off >> 7, off & 127
        keep = lane >= s
        for p in range(2):
            cols = slice(128 * p, 128 * (p + 1))
            x = bp_ref[i, :, cols].astype(F32)
            nat_ref[b, :, cols] += jnp.where(keep, x, 0.0)
            nat_ref[b + 1, :, cols] += jnp.where(keep, 0.0, x)
    nat_ref[0] += nat_ref[16]

    for g in range(2):
        rows = slice(16 * g, 16 * (g + 1))
        for p in range(2):
            cols = slice(128 * p, 128 * (p + 1))
            x = swap_index([nat_ref[b, rows, cols].astype(BF) for b in range(16)])
            for m in range(16):
                lhs_ref[m, rows, cols] = x[m]
    v = jnp.dot(lhs_ref[...].reshape(16 * CB, 256), tab_ref[...], preferred_element_type=F32)
    v_ref[...] = v.reshape(16, CB, 256)
    done = []
    for g in range(4):
        rows = slice(8 * g, 8 * (g + 1))
        t = []
        for m in range(16):
            vr, vi = v_ref[m, rows, 0:128], v_ref[m, rows, 128:256]
            c, s = tw_ref[0, m : m + 1, :], tw_ref[1, m : m + 1, :]
            t.append((vr * c - vi * s, vr * s + vi * c))
        h = [(t[m][0] + t[-m % 16][0], t[m][1] - t[-m % 16][1]) for m in range(9)]
        x = real_inverse(h)
        for b in range(16):
            lanes = slice(128 * b, 128 * (b + 1))
            out_ref[rows, lanes] = x[b] * (0.5 * win_ref[:, lanes])
        part = pl.ds(8 * g, 8)
        copy = pltpu.make_async_copy(out_ref.at[part, :], out_hbm.at[part, :], sem.at[g])
        copy.start()
        done.append(copy)
    for copy in done:
        copy.wait()


def k3(offsets, bp):
    return pl.pallas_call(
        k3_body,
        out_shape=jax.ShapeDtypeStruct((CB, FR), F32),
        in_specs=[VMEM] * 4,
        out_specs=ANY,
        scratch_shapes=[
            pltpu.VMEM((17, CB, 256), F32),
            pltpu.VMEM((2, 16, 128), F32),
            pltpu.VMEM((16, CB, 256), BF),
            pltpu.VMEM((16, CB, 256), F32),
            pltpu.VMEM((CB, FR), F32),
            pltpu.SemaphoreType.DMA((4,)),
        ],
        compiler_params=PARAMS,
        name="slots_to_facet",
    )(offsets, bp, window(), jnp.asarray(block_table().T, BF))


def swapped(sibling, neighbour):
    n = lax.axis_size("uv")
    near = [(i, i ^ 1) for i in range(n)]
    far = [(i, (i - 1 if i % 2 == 0 else i + 1) % n) for i in range(n)]
    return lax.ppermute(sibling, "uv", near), lax.ppermute(neighbour, "uv", far)


def local(
    sky_image, subgrid_offsets, owner_order, visibility_count, visibility_cell, observed,
    visibility_weight, row_kernel, column_kernel,
):
    obs = observed[0]
    wt = visibility_weight[0]

    out = k1(subgrid_offsets, owner_order, sky_image)
    arrived = lax.all_to_all(out, "facet", split_axis=0, concat_axis=0, tiled=True)
    table, phases, live, there, back, taps, offsets, *edges = kt(
        subgrid_offsets, owner_order, row_kernel, column_kernel, visibility_count,
        visibility_cell, obs, wt,
    )
    edges = swapped(*edges)
    edge, sibling, neighbour = ka(arrived, there, phases)
    sibling, neighbour = swapped(sibling, neighbour)
    mid, vis, res_mid, out_mid = km(
        arrived, there, phases, edge, taps, table, live, obs, wt, back, *edges
    )
    res, outgoing = kb(
        taps, edge, mid, vis, sibling, neighbour, back, table, phases, res_mid, out_mid
    )
    returned = lax.all_to_all(outgoing, "facet", split_axis=0, concat_axis=0, tiled=True)
    dirty = k3(offsets, returned)
    return (res[None], dirty)


def solution(mesh):
    in_specs = (
        P("uv", "facet"),
        P(),
        P(),
        P("facet"),
        P("facet", None),
        P("facet", None, "uv", None),
        P("facet", "uv", None),
        P(),
        P(),
    )
    out_specs = (P("facet", None, "uv", None), P("uv", "facet"))
    return jax.shard_map(local, mesh=mesh, in_specs=in_specs, out_specs=out_specs, check_vma=False)
```

```python
import math

import jax
import jax.numpy as jnp
import numpy as np
from jax import lax
from jax.experimental import pallas as pl
from jax.experimental.pallas import tpu as pltpu
from jax.sharding import PartitionSpec as P

FR = 2048
XC = 128
SG = 256
NF = 32
CB = 32
CE = 40
TAPS = 7
VM = 512
BF = jnp.bfloat16
F32 = jnp.float32


def block_table():
    lane = np.arange(128)[None, :]
    g = 8 * (lane % 16) + lane // 16
    row = np.arange(128)[:, None] + 64
    a = 2.0 * np.pi * ((g * row) % 128) / 128
    c, s = np.cos(a), np.sin(a)
    return np.block([[c, -s], [s, c]]).astype(np.float32)


def facet_phase():
    f = np.arange(NF)[:, None]
    j = np.arange(128)[None, :]
    a = 2.0 * np.pi * ((j * (2 * f + 1)) % 64) / 64
    return np.stack([np.cos(a), np.sin(a)]).astype(np.float32)


def window():
    r = np.arange(FR)
    return (np.sin((r + 0.5) * np.pi / FR) / math.sqrt(FR)).astype(np.float32)[None, :]


def turn(n):
    q = (n + 256) >> 9
    x = (n - (q << 9)).astype(F32) * (math.pi / 1024.0)
    y = x * x
    c = 1.0 + y * (-0.5 + y * (1.0 / 24 + y * (-1.0 / 720 + y * (1.0 / 40320))))
    s = x * (1.0 + y * (-1.0 / 6 + y * (1.0 / 120 + y * (-1.0 / 5040 + y * (1.0 / 362880)))))
    odd = (q & 1) == 1
    cos = jnp.where(odd, s, c)
    sin = jnp.where(odd, c, s)
    cos = jnp.where(((q + 1) & 2) == 2, -cos, cos)
    sin = jnp.where((q & 2) == 2, -sin, sin)
    return cos, sin


def twiddles(facet):
    m = lax.broadcasted_iota(jnp.int32, (16, 128), 0)
    lane = lax.broadcasted_iota(jnp.int32, (16, 128), 1)
    return turn((m * (lane + 64 + 128 * facet)) & (FR - 1))


def make_window(win_ref):
    for b in range(16):
        r = lax.broadcasted_iota(jnp.int32, (8, 128), 1) + (128 * b)
        x = (r.astype(F32) - 1023.5) * (math.pi / FR)
        y = x * x
        c = 1.0 / 24 + y * (-1.0 / 720 + y * (1.0 / 40320 + y * (-1.0 / 3628800 + y / 479001600)))
        win_ref[:, 128 * b : 128 * (b + 1)] = (1.0 + y * (-0.5 + y * c)) * (1.0 / math.sqrt(FR))


def make_block_table(tab_ref, transposed=False):
    lane = lax.broadcasted_iota(jnp.int32, (128, 128), 0 if transposed else 1)
    row = lax.broadcasted_iota(jnp.int32, (128, 128), 1 if transposed else 0) + 64
    g = 8 * (lane & 15) + (lane >> 4)
    c, s = turn((16 * g * row) & (FR - 1))
    c, s, t = c.astype(BF), s.astype(BF), (-s).astype(BF)
    if transposed:
        s, t = t, s
    tab_ref[0:128, 0:128] = c
    tab_ref[0:128, 128:256] = t
    tab_ref[128:256, 0:128] = s
    tab_ref[128:256, 128:256] = c


def cmul(a, w):
    wr, wi = w
    if abs(wi) < 1e-12:
        return a if abs(wr - 1) < 1e-12 else (a[0] * wr, a[1] * wr)
    if abs(wr) < 1e-12:
        return (-a[1], a[0]) if wi > 0 else (a[1], -a[0])
    return (a[0] * wr - a[1] * wi, a[0] * wi + a[1] * wr)


def real_transform(x):
    n = len(x)
    if n == 2:
        zero = jnp.zeros_like(x[0])
        return [(x[0] + x[1], zero), (x[0] - x[1], zero)]
    even, odd = real_transform(x[::2]), real_transform(x[1::2])
    out = [None] * (n // 2 + 1)
    for k in range(n // 4 + 1):
        a = 2.0 * math.pi * k / n
        o = cmul(odd[k], (math.cos(a), -math.sin(a)))
        e = even[k]
        out[k] = (e[0] + o[0], e[1] + o[1])
        if k != n // 2 - k:
            out[n // 2 - k] = (e[0] - o[0], o[1] - e[1])
    return out


def real_inverse(h):
    n = 2 * (len(h) - 1)
    if n == 2:
        return [h[0][0] + h[1][0], h[0][0] - h[1][0]]
    even, odd = [], []
    for k in range(n // 4 + 1):
        a, b = h[k], h[n // 2 - k]
        t = 2.0 * math.pi * k / n
        even.append((a[0] + b[0], a[1] - b[1]))
        odd.append(cmul((a[0] - b[0], a[1] + b[1]), (math.cos(t), math.sin(t))))
    even, odd = real_inverse(even), real_inverse(odd)
    return [v for pair in zip(even, odd) for v in pair]


def lanes_of(shape):
    return lax.broadcasted_iota(jnp.int32, shape, 1).astype(F32).astype(BF)


def swap_index(x):
    lane = lax.broadcasted_iota(jnp.int32, x[0].shape, 1)
    for bit in (1, 2, 4, 8):
        high = (lane & bit).astype(F32).astype(BF) > 0
        y = list(x)
        for i in range(16):
            if i & bit:
                continue
            y[i] = jnp.where(high, pltpu.roll(x[i + bit], bit, 1), x[i])
            y[i + bit] = jnp.where(high, x[i + bit], pltpu.roll(x[i], 128 - bit, 1))
        x = y
    return x


def halo_rows(after, before, axis):
    row = lax.broadcasted_iota(jnp.int32, after.shape, axis)
    return jnp.where(row < 3, after, jnp.where(row >= 5, before, jnp.zeros_like(after)))


def k1_body(
    offs_hbm, order_hbm, sky_hbm,
    out_hbm, offs_ref, order_ref, tw_ref, lhs_ref, u_ref, nat_ref, sky_ref, win_ref, tab_ref,
    out_ref, sky_sem, small_sem, out_sem,
):
    halves = [
        pltpu.make_async_copy(
            sky_hbm.at[pl.ds(16 * g, 16), :], sky_ref.at[pl.ds(16 * g, 16), :], sky_sem.at[g]
        )
        for g in range(2)
    ]
    small = [
        pltpu.make_async_copy(offs_hbm, offs_ref, small_sem.at[0]),
        pltpu.make_async_copy(order_hbm, order_ref, small_sem.at[1]),
    ]
    for copy in halves + small:
        copy.start()
    tw_ref[0], tw_ref[1] = twiddles(lax.axis_index("facet"))
    make_window(win_ref)
    make_block_table(tab_ref)
    for g in range(2):
        halves[g].wait()
        rows = slice(16 * g, 16 * (g + 1))
        x = []
        for b in range(16):
            lanes = slice(128 * b, 128 * (b + 1))
            x.append(sky_ref[rows, lanes].astype(F32) * win_ref[0:1, lanes])
        a = real_transform(x)
        for m in range(16):
            ar, ai = a[m] if m <= 8 else (a[16 - m][0], -a[16 - m][1])
            c, s = tw_ref[0, m : m + 1, :], tw_ref[1, m : m + 1, :]
            lhs_ref[m, rows, 0:128] = (ar * c + ai * s).astype(BF)
            lhs_ref[m, rows, 128:256] = (ai * c - ar * s).astype(BF)
    u = jnp.dot(lhs_ref[...].reshape(16 * CB, 256), tab_ref[...], preferred_element_type=F32)
    u_ref[...] = u.astype(BF).reshape(16, CB, 256)

    for g in range(2):
        rows = slice(16 * g, 16 * (g + 1))
        for p in range(2):
            cols = slice(128 * p, 128 * (p + 1))
            x = swap_index([u_ref[m, rows, cols] for m in range(16)])
            for b in range(16):
                nat_ref[b, rows, cols] = x[b]
            nat_ref[16, rows, cols] = x[0]

    for copy in small:
        copy.wait()
    lane = lanes_of((CB, 128))
    done = []
    for i in range(NF):
        off = offs_ref[order_ref[i]]
        b, s = off >> 7, off & 127
        keep = lane >= s.astype(F32).astype(BF)
        for p in range(2):
            cols = slice(128 * p, 128 * (p + 1))
            out_ref[i, :, cols] = jnp.where(keep, nat_ref[b, :, cols], nat_ref[b + 1, :, cols])
        if i % 8 == 7:
            part = pl.ds(i - 7, 8)
            copy = pltpu.make_async_copy(out_ref.at[part], out_hbm.at[part], out_sem.at[i // 8])
            copy.start()
            done.append(copy)
    for copy in done:
        copy.wait()


SMEM = pl.BlockSpec(memory_space=pltpu.SMEM)
VMEM = pl.BlockSpec(memory_space=pltpu.VMEM)
ANY = pl.BlockSpec(memory_space=pl.ANY)
PARAMS = pltpu.CompilerParams(vmem_limit_bytes=24 * 1024 * 1024)


def k1(offs, order, sky):
    return pl.pallas_call(
        k1_body,
        out_shape=jax.ShapeDtypeStruct((NF, CB, 2 * XC), BF),
        in_specs=[ANY] * 3,
        out_specs=ANY,
        scratch_shapes=[
            pltpu.SMEM((NF,), jnp.int32),
            pltpu.SMEM((NF,), jnp.int32),
            pltpu.VMEM((2, 16, 128), F32),
            pltpu.VMEM((16, CB, 256), BF),
            pltpu.VMEM((16, CB, 256), BF),
            pltpu.VMEM((17, CB, 256), BF),
            pltpu.VMEM((CB, FR), BF),
            pltpu.VMEM((8, FR), F32),
            pltpu.VMEM((256, 256), BF),
            pltpu.VMEM((NF, CB, 256), BF),
            pltpu.SemaphoreType.DMA((2,)),
            pltpu.SemaphoreType.DMA((2,)),
            pltpu.SemaphoreType.DMA((4,)),
        ],
        name="facet_to_slots",
    )(offs, order, sky)


def kt_body(
    offs_ref, order_ref, rk_ref, ck_ref, count_ref, cell_ref, ph_ref, obs_ref, wt_ref,
    dt_ref, pho_ref, live_ref, w_ref, back_ref, taps_ref, offset_ref,
    sibling_ref, neighbour_ref,
):
    off = offs_ref[order_ref[lax.axis_index("facet")]]
    back = (128 - 2 * off) & 127
    pho_ref[0] = pltpu.roll(ph_ref[0], back, 1)
    pho_ref[1] = pltpu.roll(ph_ref[1], back, 1)
    even = lax.rem(lax.axis_index("uv"), 2) == 0
    for p in range(3):
        edges = obs_ref[p].astype(F32) if p < 2 else wt_ref[...]
        first, last = edges[0:8], edges[24:32]
        sibling_ref[:, p * VM : (p + 1) * VM] = jnp.where(even, last, first).astype(BF)
        neighbour_ref[:, p * VM : (p + 1) * VM] = jnp.where(even, first, last).astype(BF)
    lane = lax.broadcasted_iota(jnp.int32, (8, 128), 1)
    offsets = jnp.zeros((8, 128), jnp.int32)
    for i in range(NF):
        offsets = jnp.where(lane == i, offs_ref[order_ref[i]], offsets)
    offset_ref[...] = offsets
    d = lax.broadcasted_iota(jnp.int32, (SG, VM), 0) - cell_ref[...] + 3
    m = jnp.zeros((SG, VM), F32)
    for t in range(TAPS):
        m = jnp.where(d == t, rk_ref[t], m)
        taps_ref[t : t + 1, :] = jnp.full((1, SG), ck_ref[t], F32)
    taps_ref[TAPS : TAPS + 1, :] = jnp.zeros((1, SG), F32)
    dt_ref[...] = m.astype(BF)
    live_ref[...] = (lax.broadcasted_iota(jnp.int32, (1, VM), 1) < count_ref[0]).astype(F32)
    for ref, shape, axis in ((w_ref, (XC, SG), 0), (back_ref, (SG, XC), 1)):
        k = (lax.broadcasted_iota(jnp.int32, shape, axis) - off) & (XC - 1)
        j = lax.broadcasted_iota(jnp.int32, shape, 1 - axis)
        c, s = turn((8 * j * k) & (FR - 1))
        c, s, t = (x.astype(BF) for x in (c * (1 / 64), s * (1 / 64), s * (-1 / 64)))
        rows, cols = shape
        ref[0:rows, 0:cols] = c
        ref[rows:, cols:] = c
        ref[0:rows, cols:] = s if axis == 0 else t
        ref[rows:, 0:cols] = t if axis == 0 else s


def kt(offs, order, rk, ck, count, cell, obs, wt):
    return pl.pallas_call(
        kt_body,
        out_shape=(
            jax.ShapeDtypeStruct((SG, VM), BF),
            jax.ShapeDtypeStruct((2, NF, 128), F32),
            jax.ShapeDtypeStruct((1, VM), F32),
            jax.ShapeDtypeStruct((2 * XC, 2 * SG), BF),
            jax.ShapeDtypeStruct((2 * SG, 2 * XC), BF),
            jax.ShapeDtypeStruct((8, SG), F32),
            jax.ShapeDtypeStruct((8, 128), jnp.int32),
            jax.ShapeDtypeStruct((8, EDGE), BF),
            jax.ShapeDtypeStruct((8, EDGE), BF),
        ),
        in_specs=[SMEM] * 5 + [VMEM] * 4,
        out_specs=(VMEM,) * 9,
        compiler_params=PARAMS,
        cost_estimate=pl.CostEstimate(flops=4000000, bytes_accessed=1000000, transcendentals=0),
        name="slot_tables",
    )(offs, order, rk, ck, count, cell, facet_phase(), obs, wt)


def facet_sum(arr, w_ref, pho_ref, u_ref, out_ref):
    u = jnp.dot(arr.reshape(NF * 16, 256), w_ref[...], preferred_element_type=F32)
    u_ref[...] = u.reshape(NF, 16, 2 * SG)
    for h in range(2):
        re = jnp.zeros((16, 128), F32)
        im = jnp.zeros((16, 128), F32)
        for f in range(NF):
            ur = u_ref[f, :, 128 * h : 128 * (h + 1)]
            ui = u_ref[f, :, SG + 128 * h : SG + 128 * (h + 1)]
            pc = pho_ref[0, f : f + 1, :]
            ps = pho_ref[1, f : f + 1, :]
            re = re + (ur * pc - ui * ps)
            im = im + (ur * ps + ui * pc)
        out_ref[:, 128 * h : 128 * (h + 1)] = re
        out_ref[:, SG + 128 * h : SG + 128 * (h + 1)] = im


def project(back_ref, pho_ref, table_ref, y_ref):
    for h in range(2):
        lanes = slice(128 * h, 128 * (h + 1))
        xr, xi = back_ref[0, :, lanes], back_ref[1, :, lanes]
        for f in range(NF):
            pc = pho_ref[0, f : f + 1, :]
            ps = pho_ref[1, f : f + 1, :]
            y_ref[f, :, lanes] = (xr * pc + xi * ps).astype(BF)
            y_ref[f, :, SG + 128 * h : SG + 128 * (h + 1)] = (xi * pc - xr * ps).astype(BF)
    z = jnp.dot(y_ref[...].reshape(NF * 16, 2 * SG), table_ref[...], preferred_element_type=F32)
    return z.astype(BF).reshape(NF, 16, 2 * XC)


def ka_body(arr_ref, w_ref, pho_ref, edge_ref, sibling_ref, neighbour_ref, u_ref):
    arr = jnp.concatenate([arr_ref[:, 0:8, :], arr_ref[:, 24:32, :]], axis=1)
    facet_sum(arr, w_ref, pho_ref, u_ref, edge_ref)
    even = lax.rem(lax.axis_index("uv"), 2) == 0
    first, last = edge_ref[0:8, :], edge_ref[8:16, :]
    sibling_ref[...] = jnp.where(even, last, first).astype(BF)
    neighbour_ref[...] = jnp.where(even, first, last).astype(BF)


EDGE = 3 * VM


def ka(arrived, table, phases):
    return pl.pallas_call(
        ka_body,
        out_shape=(
            jax.ShapeDtypeStruct((16, 2 * SG), F32),
            jax.ShapeDtypeStruct((8, 2 * SG), BF),
            jax.ShapeDtypeStruct((8, 2 * SG), BF),
        ),
        in_specs=[VMEM] * 3,
        out_specs=(VMEM, VMEM, VMEM),
        scratch_shapes=[pltpu.VMEM((NF, 16, 2 * SG), F32)],
        compiler_params=PARAMS,
        name="sum_edges",
    )(arrived, table, phases)


def sides(s, n):
    uv = lax.axis_index("uv")
    even = lax.rem(uv, 2) == 0
    s, n = s.astype(F32), n.astype(F32)
    before = jnp.where(uv > 0, jnp.where(even, n, s), 0.0)
    after = jnp.where(uv < 7, jnp.where(even, s, n), 0.0)
    return before, after


def km_body(
    arr_ref, w_ref, pho_ref, edge_ref, taps_ref, dt_ref, live_ref, obs_ref, wt_ref, back_tab_ref,
    sibling_vis_ref, neighbour_vis_ref,
    mid_ref, vis_ref, res_ref, out_ref, u_ref, s_ref, c_ref, g_ref, back_ref, y_ref, v_ref,
):
    facet_sum(arr_ref[:, 8:24, :], w_ref, pho_ref, u_ref, mid_ref)
    s_ref[0:8, :] = jnp.zeros((8, 2 * SG), F32)
    s_ref[8:16, :] = edge_ref[0:8, :]
    s_ref[16:32, :] = mid_ref[...]
    s_ref[32:40, :] = edge_ref[8:16, :]
    s_ref[40:48, :] = jnp.zeros((8, 2 * SG), F32)
    for p in range(2):
        c = jnp.zeros((CB, SG), F32)
        for t in range(TAPS):
            c = c + taps_ref[t : t + 1, :] * s_ref[5 + t : 37 + t, SG * p : SG * (p + 1)]
        c_ref[p * CB : (p + 1) * CB, :] = c
    model = jnp.dot(c_ref[...].astype(BF), dt_ref[...], preferred_element_type=F32)
    wt = wt_ref[...] * live_ref[...]
    parts = []
    for p in range(2):
        r = wt * (obs_ref[p].astype(F32) - model[p * CB : (p + 1) * CB])
        res_ref[p] = r[8:24]
        parts.append(r)
    rr = jnp.concatenate(parts, axis=0).astype(BF)
    g_ref[...] = lax.dot_general(
        rr, dt_ref[...], (((1,), (1,)), ((), ())), preferred_element_type=F32
    )
    for p in range(2):
        b = jnp.zeros((16, SG), F32)
        for t in range(TAPS):
            first = p * CB + 11 - t
            b = b + taps_ref[t : t + 1, :] * g_ref[first : first + 16, :]
        back_ref[p] = b
    out_ref[...] = project(back_ref, pho_ref, back_tab_ref, y_ref)
    for p in range(3):
        cols = slice(p * VM, (p + 1) * VM)
        before, after = sides(sibling_vis_ref[:, cols], neighbour_vis_ref[:, cols])
        own = obs_ref[p].astype(F32) if p < 2 else wt
        if p == 2:
            before, after = before * live_ref[...], after * live_ref[...]
        v_ref[0:8, :] = before
        v_ref[8:40, :] = own
        v_ref[40:48, :] = after
        vis_ref[p, 0:16, :] = v_ref[4:20, :]
        vis_ref[p, 16:32, :] = v_ref[28:44, :]


def km(arrived, table, phases, edge, taps, grid, live, obs, wt, back, *vis):
    return pl.pallas_call(
        km_body,
        out_shape=(
            jax.ShapeDtypeStruct((16, 2 * SG), F32),
            jax.ShapeDtypeStruct((3, 32, VM), F32),
            jax.ShapeDtypeStruct((2, 16, VM), F32),
            jax.ShapeDtypeStruct((NF, 16, 2 * XC), BF),
        ),
        in_specs=[VMEM] * 12,
        out_specs=(VMEM,) * 4,
        scratch_shapes=[
            pltpu.VMEM((NF, 16, 2 * SG), F32),
            pltpu.VMEM((48, 2 * SG), F32),
            pltpu.VMEM((2 * CB, SG), F32),
            pltpu.VMEM((2 * CB, SG), F32),
            pltpu.VMEM((2, 16, SG), F32),
            pltpu.VMEM((NF, 16, 2 * SG), BF),
            pltpu.VMEM((48, VM), F32),
        ],
        compiler_params=PARAMS,
        cost_estimate=pl.CostEstimate(flops=300000000, bytes_accessed=2000000, transcendentals=0),
        name="inner_columns",
    )(arrived, table, phases, edge, taps, grid, live, obs, wt, back, *vis)


def kb_body(
    taps_ref, edge_ref, mid_ref, vis_ref, sibling_ref, neighbour_ref, back_tab_ref, dt_ref,
    pho_ref, out_mid_ref,
    res_ref, out_ref, s_ref, c_ref, g_ref, back_ref, y_ref,
):
    before, after = sides(sibling_ref[...], neighbour_ref[...])
    s_ref[0, 0:8, :] = before
    s_ref[0, 8:16, :] = edge_ref[0:8, :]
    s_ref[0, 16:24, :] = mid_ref[0:8, :]
    s_ref[1, 0:8, :] = mid_ref[8:16, :]
    s_ref[1, 8:16, :] = edge_ref[8:16, :]
    s_ref[1, 16:24, :] = after
    for p in range(2):
        for side in range(2):
            c = jnp.zeros((16, SG), F32)
            for t in range(TAPS):
                c = c + taps_ref[t : t + 1, :] * s_ref[side, 1 + t : 17 + t, SG * p : SG * (p + 1)]
            c_ref[32 * p + 16 * side : 32 * p + 16 * (side + 1), :] = c
    model = jnp.dot(c_ref[...].astype(BF), dt_ref[...], preferred_element_type=F32)
    parts = []
    for p in range(2):
        r = vis_ref[2] * (vis_ref[p] - model[32 * p : 32 * (p + 1)])
        res_ref[0, p] = r[4:12]
        res_ref[1, p] = r[20:28]
        parts.append(r)
    rr = jnp.concatenate(parts, axis=0).astype(BF)
    g_ref[...] = lax.dot_general(
        rr, dt_ref[...], (((1,), (1,)), ((), ())), preferred_element_type=F32
    )
    for p in range(2):
        for side in range(2):
            b = jnp.zeros((8, SG), F32)
            for t in range(TAPS):
                first = 32 * p + 16 * side + 7 - t
                b = b + taps_ref[t : t + 1, :] * g_ref[first : first + 8, :]
            back_ref[p, 8 * side : 8 * (side + 1), :] = b
    out_ref[:, 8:24, :] = out_mid_ref[...]
    z = project(back_ref, pho_ref, back_tab_ref, y_ref)
    out_ref[:, 0:8, :] = z[:, 0:8, :]
    out_ref[:, 24:32, :] = z[:, 8:16, :]


def kb(taps, edge, mid, vis, sibling, neighbour, back, grid, phases, out_mid):
    return pl.pallas_call(
        kb_body,
        out_shape=(
            jax.ShapeDtypeStruct((2, 2, 8, VM), F32),
            jax.ShapeDtypeStruct((NF, CB, 2 * XC), BF),
        ),
        in_specs=[VMEM] * 10,
        out_specs=(VMEM, VMEM),
        scratch_shapes=[
            pltpu.VMEM((2, 24, 2 * SG), F32),
            pltpu.VMEM((64, SG), F32),
            pltpu.VMEM((64, SG), F32),
            pltpu.VMEM((2, 16, SG), F32),
            pltpu.VMEM((NF, 16, 2 * SG), BF),
        ],
        compiler_params=PARAMS,
        name="edge_columns",
    )(taps, edge, mid, vis, sibling, neighbour, back, grid, phases, out_mid)


def k3_body(
    offset_ref, bp_ref, win_ref, tab_ref, res_edge_ref, res_mid_ref,
    res_hbm, out_hbm, nat_ref, tw_ref, lhs_ref, v_ref, out_ref, res_sem, sem,
):
    done = [pltpu.make_async_copy(res_mid_ref, res_hbm.at[:, pl.ds(8, 16), :], res_sem.at[2])]
    for side in range(2):
        part = res_hbm.at[:, pl.ds(24 * side, 8), :]
        done.append(pltpu.make_async_copy(res_edge_ref.at[side], part, res_sem.at[side]))
    for copy in done:
        copy.start()
    offsets = offset_ref[...]
    tw_ref[0], tw_ref[1] = twiddles(lax.axis_index("facet"))
    nat_ref[...] = jnp.zeros_like(nat_ref)
    lane = lax.broadcasted_iota(jnp.int32, (CB, 128), 1)
    for i in range(NF):
        off = offsets[0, i]
        b, s = off >> 7, off & 127
        keep = lane >= s
        for p in range(2):
            cols = slice(128 * p, 128 * (p + 1))
            x = bp_ref[i, :, cols].astype(F32)
            nat_ref[b, :, cols] += jnp.where(keep, x, 0.0)
            nat_ref[b + 1, :, cols] += jnp.where(keep, 0.0, x)
    nat_ref[0] += nat_ref[16]

    for g in range(2):
        rows = slice(16 * g, 16 * (g + 1))
        for p in range(2):
            cols = slice(128 * p, 128 * (p + 1))
            x = swap_index([nat_ref[b, rows, cols].astype(BF) for b in range(16)])
            for m in range(16):
                lhs_ref[m, rows, cols] = x[m]
    v = jnp.dot(lhs_ref[...].reshape(16 * CB, 256), tab_ref[...], preferred_element_type=F32)
    v_ref[...] = v.reshape(16, CB, 256)
    for g in range(4):
        rows = slice(8 * g, 8 * (g + 1))
        t = []
        for m in range(16):
            vr, vi = v_ref[m, rows, 0:128], v_ref[m, rows, 128:256]
            c, s = tw_ref[0, m : m + 1, :], tw_ref[1, m : m + 1, :]
            t.append((vr * c - vi * s, vr * s + vi * c))
        h = [(t[m][0] + t[-m % 16][0], t[m][1] - t[-m % 16][1]) for m in range(9)]
        x = real_inverse(h)
        for b in range(16):
            lanes = slice(128 * b, 128 * (b + 1))
            out_ref[rows, lanes] = x[b] * (0.5 * win_ref[:, lanes])
        part = pl.ds(8 * g, 8)
        copy = pltpu.make_async_copy(out_ref.at[part, :], out_hbm.at[part, :], sem.at[g])
        copy.start()
        done.append(copy)
    for copy in done:
        copy.wait()


def k3(offsets, bp, res_edge, res_mid):
    return pl.pallas_call(
        k3_body,
        out_shape=(
            jax.ShapeDtypeStruct((2, CB, VM), F32),
            jax.ShapeDtypeStruct((CB, FR), F32),
        ),
        in_specs=[VMEM] * 6,
        out_specs=(ANY, ANY),
        scratch_shapes=[
            pltpu.VMEM((17, CB, 256), F32),
            pltpu.VMEM((2, 16, 128), F32),
            pltpu.VMEM((16, CB, 256), BF),
            pltpu.VMEM((16, CB, 256), F32),
            pltpu.VMEM((CB, FR), F32),
            pltpu.SemaphoreType.DMA((3,)),
            pltpu.SemaphoreType.DMA((4,)),
        ],
        compiler_params=PARAMS,
        name="slots_to_facet",
    )(offsets, bp, window(), jnp.asarray(block_table().T, BF), res_edge, res_mid)


def swapped(sibling, neighbour):
    n = lax.axis_size("uv")
    near = [(i, i ^ 1) for i in range(n)]
    far = [(i, (i - 1 if i % 2 == 0 else i + 1) % n) for i in range(n)]
    return lax.ppermute(sibling, "uv", near), lax.ppermute(neighbour, "uv", far)


def local(
    sky_image, subgrid_offsets, owner_order, visibility_count, visibility_cell, observed,
    visibility_weight, row_kernel, column_kernel,
):
    obs = observed[0]
    wt = visibility_weight[0]

    out = k1(subgrid_offsets, owner_order, sky_image)
    arrived = lax.all_to_all(out, "facet", split_axis=0, concat_axis=0, tiled=True)
    table, phases, live, there, back, taps, offsets, *edges = kt(
        subgrid_offsets, owner_order, row_kernel, column_kernel, visibility_count,
        visibility_cell, obs, wt,
    )
    edges = swapped(*edges)
    edge, sibling, neighbour = ka(arrived, there, phases)
    sibling, neighbour = swapped(sibling, neighbour)
    mid, vis, res_mid, out_mid = km(
        arrived, there, phases, edge, taps, table, live, obs, wt, back, *edges
    )
    res_edge, outgoing = kb(
        taps, edge, mid, vis, sibling, neighbour, back, table, phases, out_mid
    )
    returned = lax.all_to_all(outgoing, "facet", split_axis=0, concat_axis=0, tiled=True)
    res, dirty = k3(offsets, returned, res_edge, res_mid)
    return (res[None], dirty)


def solution(mesh):
    in_specs = (
        P("uv", "facet"),
        P(),
        P(),
        P("facet"),
        P("facet", None),
        P("facet", None, "uv", None),
        P("facet", "uv", None),
        P(),
        P(),
    )
    out_specs = (P("facet", None, "uv", None), P("uv", "facet"))
    return jax.shard_map(local, mesh=mesh, in_specs=in_specs, out_specs=out_specs, check_vma=False)
```

```python
import math

import jax
import jax.numpy as jnp
import numpy as np
from jax import lax
from jax.experimental import pallas as pl
from jax.experimental.pallas import tpu as pltpu
from jax.sharding import PartitionSpec as P

FR = 2048
XC = 128
SG = 256
NF = 32
CB = 32
CE = 40
TAPS = 7
VM = 512
BF = jnp.bfloat16
F32 = jnp.float32


def block_table():
    lane = np.arange(128)[None, :]
    g = 8 * (lane % 16) + lane // 16
    row = np.arange(128)[:, None] + 64
    a = 2.0 * np.pi * ((g * row) % 128) / 128
    c, s = np.cos(a), np.sin(a)
    return np.block([[c, -s], [s, c]]).astype(np.float32)


def facet_phase():
    f = np.arange(NF)[:, None]
    j = np.arange(128)[None, :]
    a = 2.0 * np.pi * ((j * (2 * f + 1)) % 64) / 64
    return np.stack([np.cos(a), np.sin(a)]).astype(np.float32)


def window():
    r = np.arange(FR)
    return (np.sin((r + 0.5) * np.pi / FR) / math.sqrt(FR)).astype(np.float32)[None, :]


def turn(n):
    q = (n + 256) >> 9
    x = (n - (q << 9)).astype(F32) * (math.pi / 1024.0)
    y = x * x
    c = 1.0 + y * (-0.5 + y * (1.0 / 24 + y * (-1.0 / 720 + y * (1.0 / 40320))))
    s = x * (1.0 + y * (-1.0 / 6 + y * (1.0 / 120 + y * (-1.0 / 5040 + y * (1.0 / 362880)))))
    odd = (q & 1) == 1
    cos = jnp.where(odd, s, c)
    sin = jnp.where(odd, c, s)
    cos = jnp.where(((q + 1) & 2) == 2, -cos, cos)
    sin = jnp.where((q & 2) == 2, -sin, sin)
    return cos, sin


def twiddles(facet):
    m = lax.broadcasted_iota(jnp.int32, (16, 128), 0)
    lane = lax.broadcasted_iota(jnp.int32, (16, 128), 1)
    return turn((m * (lane + 64 + 128 * facet)) & (FR - 1))


def make_window(win_ref):
    for b in range(16):
        r = lax.broadcasted_iota(jnp.int32, (8, 128), 1) + (128 * b)
        x = (r.astype(F32) - 1023.5) * (math.pi / FR)
        y = x * x
        c = 1.0 / 24 + y * (-1.0 / 720 + y * (1.0 / 40320 + y * (-1.0 / 3628800 + y / 479001600)))
        win_ref[:, 128 * b : 128 * (b + 1)] = (1.0 + y * (-0.5 + y * c)) * (1.0 / math.sqrt(FR))


def make_block_table(tab_ref, transposed=False):
    lane = lax.broadcasted_iota(jnp.int32, (128, 128), 0 if transposed else 1)
    row = lax.broadcasted_iota(jnp.int32, (128, 128), 1 if transposed else 0) + 64
    g = 8 * (lane & 15) + (lane >> 4)
    c, s = turn((16 * g * row) & (FR - 1))
    c, s, t = c.astype(BF), s.astype(BF), (-s).astype(BF)
    if transposed:
        s, t = t, s
    tab_ref[0:128, 0:128] = c
    tab_ref[0:128, 128:256] = t
    tab_ref[128:256, 0:128] = s
    tab_ref[128:256, 128:256] = c


def cmul(a, w):
    wr, wi = w
    if abs(wi) < 1e-12:
        return a if abs(wr - 1) < 1e-12 else (a[0] * wr, a[1] * wr)
    if abs(wr) < 1e-12:
        return (-a[1], a[0]) if wi > 0 else (a[1], -a[0])
    return (a[0] * wr - a[1] * wi, a[0] * wi + a[1] * wr)


def real_transform(x):
    n = len(x)
    if n == 2:
        zero = jnp.zeros_like(x[0])
        return [(x[0] + x[1], zero), (x[0] - x[1], zero)]
    even, odd = real_transform(x[::2]), real_transform(x[1::2])
    out = [None] * (n // 2 + 1)
    for k in range(n // 4 + 1):
        a = 2.0 * math.pi * k / n
        o = cmul(odd[k], (math.cos(a), -math.sin(a)))
        e = even[k]
        out[k] = (e[0] + o[0], e[1] + o[1])
        if k != n // 2 - k:
            out[n // 2 - k] = (e[0] - o[0], o[1] - e[1])
    return out


def real_inverse(h):
    n = 2 * (len(h) - 1)
    if n == 2:
        return [h[0][0] + h[1][0], h[0][0] - h[1][0]]
    even, odd = [], []
    for k in range(n // 4 + 1):
        a, b = h[k], h[n // 2 - k]
        t = 2.0 * math.pi * k / n
        even.append((a[0] + b[0], a[1] - b[1]))
        odd.append(cmul((a[0] - b[0], a[1] + b[1]), (math.cos(t), math.sin(t))))
    even, odd = real_inverse(even), real_inverse(odd)
    return [v for pair in zip(even, odd) for v in pair]


def lanes_of(shape):
    return lax.broadcasted_iota(jnp.int32, shape, 1).astype(F32).astype(BF)


def swap_index(x):
    lane = lax.broadcasted_iota(jnp.int32, x[0].shape, 1)
    for bit in (1, 2, 4, 8):
        high = (lane & bit).astype(F32).astype(BF) > 0
        y = list(x)
        for i in range(16):
            if i & bit:
                continue
            y[i] = jnp.where(high, pltpu.roll(x[i + bit], bit, 1), x[i])
            y[i + bit] = jnp.where(high, x[i + bit], pltpu.roll(x[i], 128 - bit, 1))
        x = y
    return x


def halo_rows(after, before, axis):
    row = lax.broadcasted_iota(jnp.int32, after.shape, axis)
    return jnp.where(row < 3, after, jnp.where(row >= 5, before, jnp.zeros_like(after)))


def k1_body(
    offs_hbm, order_hbm, sky_hbm,
    out_hbm, offs_ref, order_ref, tw_ref, lhs_ref, u_ref, nat_ref, sky_ref, win_ref, tab_ref,
    out_ref, sky_sem, small_sem, out_sem,
):
    quarters = [
        [
            pltpu.make_async_copy(
                sky_hbm.at[pl.ds(16 * g, 16), pl.ds(512 * q, 512)],
                sky_ref.at[pl.ds(16 * g, 16), pl.ds(512 * q, 512)],
                sky_sem.at[4 * g + q],
            )
            for q in range(4)
        ]
        for g in range(2)
    ]
    small = [
        pltpu.make_async_copy(offs_hbm, offs_ref, small_sem.at[0]),
        pltpu.make_async_copy(order_hbm, order_ref, small_sem.at[1]),
    ]
    for copy in quarters[0] + quarters[1] + small:
        copy.start()
    tw_ref[0], tw_ref[1] = twiddles(lax.axis_index("facet"))
    make_window(win_ref)
    make_block_table(tab_ref)
    for g in range(2):
        for copy in quarters[g]:
            copy.wait()
        rows = slice(16 * g, 16 * (g + 1))
        x = []
        for b in range(16):
            lanes = slice(128 * b, 128 * (b + 1))
            x.append(sky_ref[rows, lanes].astype(F32) * win_ref[0:1, lanes])
        a = real_transform(x)
        for m in range(16):
            ar, ai = a[m] if m <= 8 else (a[16 - m][0], -a[16 - m][1])
            c, s = tw_ref[0, m : m + 1, :], tw_ref[1, m : m + 1, :]
            lhs_ref[m, rows, 0:128] = (ar * c + ai * s).astype(BF)
            lhs_ref[m, rows, 128:256] = (ai * c - ar * s).astype(BF)
    u = jnp.dot(lhs_ref[...].reshape(16 * CB, 256), tab_ref[...], preferred_element_type=F32)
    u_ref[...] = u.astype(BF).reshape(16, CB, 256)

    for g in range(2):
        rows = slice(16 * g, 16 * (g + 1))
        for p in range(2):
            cols = slice(128 * p, 128 * (p + 1))
            x = swap_index([u_ref[m, rows, cols] for m in range(16)])
            for b in range(16):
                nat_ref[b, rows, cols] = x[b]
            nat_ref[16, rows, cols] = x[0]

    for copy in small:
        copy.wait()
    lane = lanes_of((CB, 128))
    done = []
    for i in range(NF):
        off = offs_ref[order_ref[i]]
        b, s = off >> 7, off & 127
        keep = lane >= s.astype(F32).astype(BF)
        for p in range(2):
            cols = slice(128 * p, 128 * (p + 1))
            out_ref[i, :, cols] = jnp.where(keep, nat_ref[b, :, cols], nat_ref[b + 1, :, cols])
        if i % 8 == 7:
            part = pl.ds(i - 7, 8)
            copy = pltpu.make_async_copy(out_ref.at[part], out_hbm.at[part], out_sem.at[i // 8])
            copy.start()
            done.append(copy)
    for copy in done:
        copy.wait()


SMEM = pl.BlockSpec(memory_space=pltpu.SMEM)
VMEM = pl.BlockSpec(memory_space=pltpu.VMEM)
ANY = pl.BlockSpec(memory_space=pl.ANY)
PARAMS = pltpu.CompilerParams(vmem_limit_bytes=24 * 1024 * 1024)


def k1(offs, order, sky):
    return pl.pallas_call(
        k1_body,
        out_shape=jax.ShapeDtypeStruct((NF, CB, 2 * XC), BF),
        in_specs=[ANY] * 3,
        out_specs=ANY,
        scratch_shapes=[
            pltpu.SMEM((NF,), jnp.int32),
            pltpu.SMEM((NF,), jnp.int32),
            pltpu.VMEM((2, 16, 128), F32),
            pltpu.VMEM((16, CB, 256), BF),
            pltpu.VMEM((16, CB, 256), BF),
            pltpu.VMEM((17, CB, 256), BF),
            pltpu.VMEM((CB, FR), BF),
            pltpu.VMEM((8, FR), F32),
            pltpu.VMEM((256, 256), BF),
            pltpu.VMEM((NF, CB, 256), BF),
            pltpu.SemaphoreType.DMA((8,)),
            pltpu.SemaphoreType.DMA((2,)),
            pltpu.SemaphoreType.DMA((4,)),
        ],
        name="facet_to_slots",
    )(offs, order, sky)


def kt_body(
    offs_ref, order_ref, rk_ref, ck_ref, count_ref, cell_ref, ph_ref, obs_ref, wt_ref,
    dt_ref, pho_ref, live_ref, w_ref, back_ref, taps_ref, offset_ref,
    sibling_ref, neighbour_ref,
):
    off = offs_ref[order_ref[lax.axis_index("facet")]]
    back = (128 - 2 * off) & 127
    pho_ref[0] = pltpu.roll(ph_ref[0], back, 1)
    pho_ref[1] = pltpu.roll(ph_ref[1], back, 1)
    even = lax.rem(lax.axis_index("uv"), 2) == 0
    for p in range(3):
        edges = obs_ref[p].astype(F32) if p < 2 else wt_ref[...]
        first, last = edges[0:8], edges[24:32]
        sibling_ref[:, p * VM : (p + 1) * VM] = jnp.where(even, last, first).astype(BF)
        neighbour_ref[:, p * VM : (p + 1) * VM] = jnp.where(even, first, last).astype(BF)
    lane = lax.broadcasted_iota(jnp.int32, (8, 128), 1)
    offsets = jnp.zeros((8, 128), jnp.int32)
    for i in range(NF):
        offsets = jnp.where(lane == i, offs_ref[order_ref[i]], offsets)
    offset_ref[...] = offsets
    d = lax.broadcasted_iota(jnp.int32, (SG, VM), 0) - cell_ref[...] + 3
    m = jnp.zeros((SG, VM), F32)
    for t in range(TAPS):
        m = jnp.where(d == t, rk_ref[t], m)
        taps_ref[t : t + 1, :] = jnp.full((1, SG), ck_ref[t], F32)
    taps_ref[TAPS : TAPS + 1, :] = jnp.zeros((1, SG), F32)
    dt_ref[...] = m.astype(BF)
    live_ref[...] = (lax.broadcasted_iota(jnp.int32, (1, VM), 1) < count_ref[0]).astype(F32)
    for ref, shape, axis in ((w_ref, (XC, SG), 0), (back_ref, (SG, XC), 1)):
        k = (lax.broadcasted_iota(jnp.int32, shape, axis) - off) & (XC - 1)
        j = lax.broadcasted_iota(jnp.int32, shape, 1 - axis)
        c, s = turn((8 * j * k) & (FR - 1))
        c, s, t = (x.astype(BF) for x in (c * (1 / 64), s * (1 / 64), s * (-1 / 64)))
        rows, cols = shape
        ref[0:rows, 0:cols] = c
        ref[rows:, cols:] = c
        ref[0:rows, cols:] = s if axis == 0 else t
        ref[rows:, 0:cols] = t if axis == 0 else s


def kt(offs, order, rk, ck, count, cell, obs, wt):
    return pl.pallas_call(
        kt_body,
        out_shape=(
            jax.ShapeDtypeStruct((SG, VM), BF),
            jax.ShapeDtypeStruct((2, NF, 128), F32),
            jax.ShapeDtypeStruct((1, VM), F32),
            jax.ShapeDtypeStruct((2 * XC, 2 * SG), BF),
            jax.ShapeDtypeStruct((2 * SG, 2 * XC), BF),
            jax.ShapeDtypeStruct((8, SG), F32),
            jax.ShapeDtypeStruct((8, 128), jnp.int32),
            jax.ShapeDtypeStruct((8, EDGE), BF),
            jax.ShapeDtypeStruct((8, EDGE), BF),
        ),
        in_specs=[SMEM] * 5 + [VMEM] * 4,
        out_specs=(VMEM,) * 9,
        compiler_params=PARAMS,
        cost_estimate=pl.CostEstimate(flops=4000000, bytes_accessed=1000000, transcendentals=0),
        name="slot_tables",
    )(offs, order, rk, ck, count, cell, facet_phase(), obs, wt)


def facet_sum(arr, w_ref, pho_ref, u_ref, out_ref):
    u = jnp.dot(arr.reshape(NF * 16, 256), w_ref[...], preferred_element_type=F32)
    u_ref[...] = u.reshape(NF, 16, 2 * SG)
    for h in range(2):
        re = jnp.zeros((16, 128), F32)
        im = jnp.zeros((16, 128), F32)
        for f in range(NF):
            ur = u_ref[f, :, 128 * h : 128 * (h + 1)]
            ui = u_ref[f, :, SG + 128 * h : SG + 128 * (h + 1)]
            pc = pho_ref[0, f : f + 1, :]
            ps = pho_ref[1, f : f + 1, :]
            re = re + (ur * pc - ui * ps)
            im = im + (ur * ps + ui * pc)
        out_ref[:, 128 * h : 128 * (h + 1)] = re
        out_ref[:, SG + 128 * h : SG + 128 * (h + 1)] = im


def project(back_ref, pho_ref, table_ref, y_ref):
    for h in range(2):
        lanes = slice(128 * h, 128 * (h + 1))
        xr, xi = back_ref[0, :, lanes], back_ref[1, :, lanes]
        for f in range(NF):
            pc = pho_ref[0, f : f + 1, :]
            ps = pho_ref[1, f : f + 1, :]
            y_ref[f, :, lanes] = (xr * pc + xi * ps).astype(BF)
            y_ref[f, :, SG + 128 * h : SG + 128 * (h + 1)] = (xi * pc - xr * ps).astype(BF)
    z = jnp.dot(y_ref[...].reshape(NF * 16, 2 * SG), table_ref[...], preferred_element_type=F32)
    return z.astype(BF).reshape(NF, 16, 2 * XC)


def ka_body(arr_ref, w_ref, pho_ref, edge_ref, sibling_ref, neighbour_ref, u_ref):
    arr = jnp.concatenate([arr_ref[:, 0:8, :], arr_ref[:, 24:32, :]], axis=1)
    facet_sum(arr, w_ref, pho_ref, u_ref, edge_ref)
    even = lax.rem(lax.axis_index("uv"), 2) == 0
    first, last = edge_ref[0:8, :], edge_ref[8:16, :]
    sibling_ref[...] = jnp.where(even, last, first).astype(BF)
    neighbour_ref[...] = jnp.where(even, first, last).astype(BF)


EDGE = 3 * VM


def ka(arrived, table, phases):
    return pl.pallas_call(
        ka_body,
        out_shape=(
            jax.ShapeDtypeStruct((16, 2 * SG), F32),
            jax.ShapeDtypeStruct((8, 2 * SG), BF),
            jax.ShapeDtypeStruct((8, 2 * SG), BF),
        ),
        in_specs=[VMEM] * 3,
        out_specs=(VMEM, VMEM, VMEM),
        scratch_shapes=[pltpu.VMEM((NF, 16, 2 * SG), F32)],
        compiler_params=PARAMS,
        name="sum_edges",
    )(arrived, table, phases)


def sides(s, n):
    uv = lax.axis_index("uv")
    even = lax.rem(uv, 2) == 0
    s, n = s.astype(F32), n.astype(F32)
    before = jnp.where(uv > 0, jnp.where(even, n, s), 0.0)
    after = jnp.where(uv < 7, jnp.where(even, s, n), 0.0)
    return before, after


def km_body(
    arr_ref, w_ref, pho_ref, edge_ref, taps_ref, dt_ref, live_ref, obs_ref, wt_ref, back_tab_ref,
    sibling_vis_ref, neighbour_vis_ref,
    mid_ref, vis_ref, res_ref, out_ref, u_ref, s_ref, c_ref, g_ref, back_ref, y_ref, v_ref,
):
    facet_sum(arr_ref[:, 8:24, :], w_ref, pho_ref, u_ref, mid_ref)
    s_ref[0:8, :] = jnp.zeros((8, 2 * SG), F32)
    s_ref[8:16, :] = edge_ref[0:8, :]
    s_ref[16:32, :] = mid_ref[...]
    s_ref[32:40, :] = edge_ref[8:16, :]
    s_ref[40:48, :] = jnp.zeros((8, 2 * SG), F32)
    for p in range(2):
        c = jnp.zeros((CB, SG), F32)
        for t in range(TAPS):
            c = c + taps_ref[t : t + 1, :] * s_ref[5 + t : 37 + t, SG * p : SG * (p + 1)]
        c_ref[p * CB : (p + 1) * CB, :] = c
    model = jnp.dot(c_ref[...].astype(BF), dt_ref[...], preferred_element_type=F32)
    wt = wt_ref[...] * live_ref[...]
    parts = []
    for p in range(2):
        r = wt * (obs_ref[p].astype(F32) - model[p * CB : (p + 1) * CB])
        res_ref[p] = r[8:24]
        parts.append(r)
    rr = jnp.concatenate(parts, axis=0).astype(BF)
    g_ref[...] = lax.dot_general(
        rr, dt_ref[...], (((1,), (1,)), ((), ())), preferred_element_type=F32
    )
    for p in range(2):
        b = jnp.zeros((16, SG), F32)
        for t in range(TAPS):
            first = p * CB + 11 - t
            b = b + taps_ref[t : t + 1, :] * g_ref[first : first + 16, :]
        back_ref[p] = b
    out_ref[...] = project(back_ref, pho_ref, back_tab_ref, y_ref)
    for p in range(3):
        cols = slice(p * VM, (p + 1) * VM)
        before, after = sides(sibling_vis_ref[:, cols], neighbour_vis_ref[:, cols])
        own = obs_ref[p].astype(F32) if p < 2 else wt
        if p == 2:
            before, after = before * live_ref[...], after * live_ref[...]
        v_ref[0:8, :] = before
        v_ref[8:40, :] = own
        v_ref[40:48, :] = after
        vis_ref[p, 0:16, :] = v_ref[4:20, :]
        vis_ref[p, 16:32, :] = v_ref[28:44, :]


def km(arrived, table, phases, edge, taps, grid, live, obs, wt, back, *vis):
    return pl.pallas_call(
        km_body,
        out_shape=(
            jax.ShapeDtypeStruct((16, 2 * SG), F32),
            jax.ShapeDtypeStruct((3, 32, VM), F32),
            jax.ShapeDtypeStruct((2, 16, VM), F32),
            jax.ShapeDtypeStruct((NF, 16, 2 * XC), BF),
        ),
        in_specs=[VMEM] * 12,
        out_specs=(VMEM,) * 4,
        scratch_shapes=[
            pltpu.VMEM((NF, 16, 2 * SG), F32),
            pltpu.VMEM((48, 2 * SG), F32),
            pltpu.VMEM((2 * CB, SG), F32),
            pltpu.VMEM((2 * CB, SG), F32),
            pltpu.VMEM((2, 16, SG), F32),
            pltpu.VMEM((NF, 16, 2 * SG), BF),
            pltpu.VMEM((48, VM), F32),
        ],
        compiler_params=PARAMS,
        cost_estimate=pl.CostEstimate(flops=300000000, bytes_accessed=2000000, transcendentals=0),
        name="inner_columns",
    )(arrived, table, phases, edge, taps, grid, live, obs, wt, back, *vis)


def kb_body(
    taps_ref, edge_ref, mid_ref, vis_ref, sibling_ref, neighbour_ref, back_tab_ref, dt_ref,
    pho_ref, out_mid_ref,
    res_ref, out_ref, s_ref, c_ref, g_ref, back_ref, y_ref,
):
    before, after = sides(sibling_ref[...], neighbour_ref[...])
    s_ref[0, 0:8, :] = before
    s_ref[0, 8:16, :] = edge_ref[0:8, :]
    s_ref[0, 16:24, :] = mid_ref[0:8, :]
    s_ref[1, 0:8, :] = mid_ref[8:16, :]
    s_ref[1, 8:16, :] = edge_ref[8:16, :]
    s_ref[1, 16:24, :] = after
    for p in range(2):
        for side in range(2):
            c = jnp.zeros((16, SG), F32)
            for t in range(TAPS):
                c = c + taps_ref[t : t + 1, :] * s_ref[side, 1 + t : 17 + t, SG * p : SG * (p + 1)]
            c_ref[32 * p + 16 * side : 32 * p + 16 * (side + 1), :] = c
    model = jnp.dot(c_ref[...].astype(BF), dt_ref[...], preferred_element_type=F32)
    parts = []
    for p in range(2):
        r = vis_ref[2] * (vis_ref[p] - model[32 * p : 32 * (p + 1)])
        res_ref[0, p] = r[4:12]
        res_ref[1, p] = r[20:28]
        parts.append(r)
    rr = jnp.concatenate(parts, axis=0).astype(BF)
    g_ref[...] = lax.dot_general(
        rr, dt_ref[...], (((1,), (1,)), ((), ())), preferred_element_type=F32
    )
    for p in range(2):
        for side in range(2):
            b = jnp.zeros((8, SG), F32)
            for t in range(TAPS):
                first = 32 * p + 16 * side + 7 - t
                b = b + taps_ref[t : t + 1, :] * g_ref[first : first + 8, :]
            back_ref[p, 8 * side : 8 * (side + 1), :] = b
    out_ref[:, 8:24, :] = out_mid_ref[...]
    z = project(back_ref, pho_ref, back_tab_ref, y_ref)
    out_ref[:, 0:8, :] = z[:, 0:8, :]
    out_ref[:, 24:32, :] = z[:, 8:16, :]


def kb(taps, edge, mid, vis, sibling, neighbour, back, grid, phases, out_mid):
    return pl.pallas_call(
        kb_body,
        out_shape=(
            jax.ShapeDtypeStruct((2, 2, 8, VM), F32),
            jax.ShapeDtypeStruct((NF, CB, 2 * XC), BF),
        ),
        in_specs=[VMEM] * 10,
        out_specs=(VMEM, VMEM),
        scratch_shapes=[
            pltpu.VMEM((2, 24, 2 * SG), F32),
            pltpu.VMEM((64, SG), F32),
            pltpu.VMEM((64, SG), F32),
            pltpu.VMEM((2, 16, SG), F32),
            pltpu.VMEM((NF, 16, 2 * SG), BF),
        ],
        compiler_params=PARAMS,
        name="edge_columns",
    )(taps, edge, mid, vis, sibling, neighbour, back, grid, phases, out_mid)


def k3_body(
    offset_ref, bp_ref, win_ref, tab_ref, res_edge_ref, res_mid_ref,
    res_hbm, out_hbm, nat_ref, tw_ref, lhs_ref, v_ref, out_ref, res_sem, sem,
):
    done = [pltpu.make_async_copy(res_mid_ref, res_hbm.at[:, pl.ds(8, 16), :], res_sem.at[2])]
    for side in range(2):
        part = res_hbm.at[:, pl.ds(24 * side, 8), :]
        done.append(pltpu.make_async_copy(res_edge_ref.at[side], part, res_sem.at[side]))
    for copy in done:
        copy.start()
    offsets = offset_ref[...]
    tw_ref[0], tw_ref[1] = twiddles(lax.axis_index("facet"))
    nat_ref[...] = jnp.zeros_like(nat_ref)
    lane = lax.broadcasted_iota(jnp.int32, (CB, 128), 1)
    for i in range(NF):
        off = offsets[0, i]
        b, s = off >> 7, off & 127
        keep = lane >= s
        for p in range(2):
            cols = slice(128 * p, 128 * (p + 1))
            x = bp_ref[i, :, cols].astype(F32)
            n = i % 2
            nat_ref[n, b, :, cols] += jnp.where(keep, x, 0.0)
            nat_ref[n, b + 1, :, cols] += jnp.where(keep, 0.0, x)
    nat_ref[0, 0] += nat_ref[0, 16] + nat_ref[1, 16]

    for g in range(2):
        rows = slice(16 * g, 16 * (g + 1))
        for p in range(2):
            cols = slice(128 * p, 128 * (p + 1))
            x = swap_index(
                [(nat_ref[0, b, rows, cols] + nat_ref[1, b, rows, cols]).astype(BF) for b in range(16)]
            )
            for m in range(16):
                lhs_ref[m, rows, cols] = x[m]
    v = jnp.dot(lhs_ref[...].reshape(16 * CB, 256), tab_ref[...], preferred_element_type=F32)
    v_ref[...] = v.reshape(16, CB, 256)
    for g in range(4):
        rows = slice(8 * g, 8 * (g + 1))
        t = []
        for m in range(16):
            vr, vi = v_ref[m, rows, 0:128], v_ref[m, rows, 128:256]
            c, s = tw_ref[0, m : m + 1, :], tw_ref[1, m : m + 1, :]
            t.append((vr * c - vi * s, vr * s + vi * c))
        h = [(t[m][0] + t[-m % 16][0], t[m][1] - t[-m % 16][1]) for m in range(9)]
        x = real_inverse(h)
        for b in range(16):
            lanes = slice(128 * b, 128 * (b + 1))
            out_ref[rows, lanes] = x[b] * (0.5 * win_ref[:, lanes])
        part = pl.ds(8 * g, 8)
        copy = pltpu.make_async_copy(out_ref.at[part, :], out_hbm.at[part, :], sem.at[g])
        copy.start()
        done.append(copy)
    for copy in done:
        copy.wait()


def k3(offsets, bp, res_edge, res_mid):
    return pl.pallas_call(
        k3_body,
        out_shape=(
            jax.ShapeDtypeStruct((2, CB, VM), F32),
            jax.ShapeDtypeStruct((CB, FR), F32),
        ),
        in_specs=[VMEM] * 6,
        out_specs=(ANY, ANY),
        scratch_shapes=[
            pltpu.VMEM((2, 17, CB, 256), F32),
            pltpu.VMEM((2, 16, 128), F32),
            pltpu.VMEM((16, CB, 256), BF),
            pltpu.VMEM((16, CB, 256), F32),
            pltpu.VMEM((CB, FR), F32),
            pltpu.SemaphoreType.DMA((3,)),
            pltpu.SemaphoreType.DMA((4,)),
        ],
        compiler_params=PARAMS,
        name="slots_to_facet",
    )(offsets, bp, window(), jnp.asarray(block_table().T, BF), res_edge, res_mid)


def swapped(sibling, neighbour):
    n = lax.axis_size("uv")
    near = [(i, i ^ 1) for i in range(n)]
    far = [(i, (i - 1 if i % 2 == 0 else i + 1) % n) for i in range(n)]
    return lax.ppermute(sibling, "uv", near), lax.ppermute(neighbour, "uv", far)


def local(
    sky_image, subgrid_offsets, owner_order, visibility_count, visibility_cell, observed,
    visibility_weight, row_kernel, column_kernel,
):
    obs = observed[0]
    wt = visibility_weight[0]

    out = k1(subgrid_offsets, owner_order, sky_image)
    arrived = lax.all_to_all(out, "facet", split_axis=0, concat_axis=0, tiled=True)
    table, phases, live, there, back, taps, offsets, *edges = kt(
        subgrid_offsets, owner_order, row_kernel, column_kernel, visibility_count,
        visibility_cell, obs, wt,
    )
    edges = swapped(*edges)
    edge, sibling, neighbour = ka(arrived, there, phases)
    sibling, neighbour = swapped(sibling, neighbour)
    mid, vis, res_mid, out_mid = km(
        arrived, there, phases, edge, taps, table, live, obs, wt, back, *edges
    )
    res_edge, outgoing = kb(
        taps, edge, mid, vis, sibling, neighbour, back, table, phases, out_mid
    )
    returned = lax.all_to_all(outgoing, "facet", split_axis=0, concat_axis=0, tiled=True)
    res, dirty = k3(offsets, returned, res_edge, res_mid)
    return (res[None], dirty)


def solution(mesh):
    in_specs = (
        P("uv", "facet"),
        P(),
        P(),
        P("facet"),
        P("facet", None),
        P("facet", None, "uv", None),
        P("facet", "uv", None),
        P(),
        P(),
    )
    out_specs = (P("facet", None, "uv", None), P("uv", "facet"))
    return jax.shard_map(local, mesh=mesh, in_specs=in_specs, out_specs=out_specs, check_vma=False)
```
